32 devices in a mesh: seq: 4 (over z), head: 4 (over y, x), dp: 2 (over core).
Axes of the slice: x: 2, y: 2, z: 4, core: 2. Of those that a mesh axis runs over, the one named last changes fastest.
Arguments:
- inputs: bfloat16 [4096, 4096], P(('dp', 'seq'), 'head'), parts along dimension 0, may hold values from -2 to 2
- step_raw: float32 [4096, 64], P(('dp', 'seq'), 'head'), parts along dimension 0, may hold values from -5 to 600
- decay_rate: float32 [64], P('head'), may hold values from 0.002 to 0.1
- skip_gain: float32 [64], P('head'), may hold values from 0.3 to 3
- b_proj: bfloat16 [4096, 8, 256], P(('dp', 'seq')), parts along dimension 0, may hold values from -2 to 2
- c_proj: bfloat16 [4096, 8, 256], P(('dp', 'seq')), parts along dimension 0, may hold values from -2 to 2
- lengths: int32 [4], P('dp'), parts along dimension 0, may hold values from 1 to 512, as said below
- cotangent: bfloat16 [4096, 4096], P(('dp', 'seq'), 'head'), parts along dimension 0, may hold values from -1.5 to 1.5
Outputs:
- outputs: bfloat16 [4096, 4096], P(('dp', 'seq'), 'head'), parts along dimension 0
- grad_inputs: bfloat16 [4096, 4096], P(('dp', 'seq'), 'head'), parts along dimension 0
- grad_step: float32 [4096, 64], P(('dp', 'seq'), 'head'), parts along dimension 0
- grad_b: float32 [4096, 8, 256], P(('dp', 'seq', 'head')), parts along dimension 0
- grad_c: float32 [4096, 8, 256], P(('dp', 'seq', 'head')), parts along dimension 0
The draws below stay inside these ranges and needn't reach their ends.
There are 2 independent parts, one for each index of `dp`. The reference program is written for one: setup_inputs(seed, part) draws one part's arguments, and reference() takes and returns one part's arrays. A program takes and returns all parts, laid end to end along the dimension named above; an argument that names none is the same for every part. Nothing has to cross between parts.
Inputs may be any that keep to these rules, and one draw needn't show every extreme that they name: `lengths`: some response has exactly 512 tokens.
All inputs are finite; a program needn't handle non-finite values.
Results may differ from the reference program's by a relative error of at most 0.009.
Values sent between devices are 32-bit elements; how exact they have to be, the bound alone decides.
A program may use at most 128 MiB of HBM per device.

```python
import math
import jax
import jax.numpy as jnp
from jax import lax

HEADDIM = 64
DSTATE = 256
GROUPS = 8
NHEADS = 64
BLOCK = 256
SLOT_LEN = 512
SEQS_DEV = 1
PREFIX_DEVS = 2
TOKENS = 2048
RESPONSES = 2
N_SEQ = 4
N_HEAD = 4


def marked_entries(key):
    marked_key, level_key = jax.random.split(jax.random.fold_in(key, 11), 2)
    shape_extents = (TOKENS, NHEADS)
    marked = jax.random.uniform(marked_key, shape_extents, jnp.float32) < 0.0025
    level = jax.random.uniform(level_key, shape_extents, jnp.float32, 200.0, 600.0)
    return (marked, level)


def draw_step_raw(key, part):
    value_key = jax.random.fold_in(key, 13)
    shape_extents = (TOKENS, NHEADS)
    value_rows = jnp.clip(jax.random.normal(value_key, shape_extents, jnp.float32) * 0.8 - 1.0, -5.0, 3.0)
    marked, level = marked_entries(key)
    return jnp.where(marked, level, value_rows).astype(jnp.float32)


def draw_inputs(key, part):
    noise_key = jax.random.fold_in(key, 17)
    shape_extents = (TOKENS, NHEADS * HEADDIM)
    base_rows = jnp.clip(jax.random.normal(noise_key, shape_extents, jnp.float32) * 0.5, -2.0, 2.0)
    marked, level = marked_entries(key)
    factor = jnp.where(marked, 1.0 / level, 1.0)
    factor_wide = jnp.repeat(factor, HEADDIM, axis=1)
    return (base_rows * factor_wide).astype(jnp.bfloat16)


def draw_lengths(key, part):
    key_vals, key_spot = jax.random.split(jax.random.fold_in(key, 23), 2)
    values = jax.random.randint(key_vals, (RESPONSES,), 1, SLOT_LEN + 1, dtype=jnp.int32)
    long_spot = jax.random.randint(key_spot, (), 0, RESPONSES, dtype=jnp.int32)
    return values.at[long_spot].set(SLOT_LEN).astype(jnp.int32)


def block_scale(key, shape, cuts, least, high):
    def one(position, parts):
        steps = jax.random.uniform(jax.random.fold_in(jax.random.fold_in(key, 6), position), (parts,), jnp.float32, least / len(cuts), high / len(cuts))
        return jnp.repeat(jnp.exp(steps), shape[position] // parts).reshape((-1,) + (1,) * (len(shape) - position - 1))

    level = one(*cuts[0])
    for cut in cuts[1:]:
        level = level * one(*cut)
    return level


def normal_values(rng, extent, scale, reach, cuts=(), held_as=jnp.bfloat16):
    entries = scale * jax.random.normal(rng, extent, jnp.float32)
    if cuts:
        entries = entries * block_scale(rng, extent, cuts, -0.22, 0.18)
    return jnp.clip(entries, -reach, reach).astype(held_as)


def setup_inputs(seed: int = 0, part: int = 0) -> dict:
    keys = jax.random.split(jax.random.key(seed), 9)
    part_keys = jax.random.split(jax.random.fold_in(keys[8], part), 9)
    return {
        "inputs": draw_inputs(jax.random.fold_in(jax.random.fold_in(keys[8], part), 71), part),
        "step_raw": draw_step_raw(jax.random.fold_in(jax.random.fold_in(keys[8], part), 71), part),
        "decay_rate": jnp.clip(jnp.exp(math.log(0.1) - 3.912023 * jax.random.uniform(keys[2], (NHEADS,), jnp.float32) ** block_scale(keys[2], (NHEADS,), ((0, 4),), -0.2, 0.2)), 0.002, 0.1),
        "skip_gain": jnp.clip(jnp.exp(math.log(3.0) - 2.3025851 * jax.random.uniform(keys[3], (NHEADS,), jnp.float32) ** block_scale(keys[3], (NHEADS,), ((0, 4),), -0.2, 0.2)), 0.3, 3.0),
        "b_proj": normal_values(part_keys[4], (TOKENS, GROUPS, DSTATE), 0.3, 2.0, ((0, 4),)),
        "c_proj": normal_values(part_keys[5], (TOKENS, GROUPS, DSTATE), 0.3, 2.0, ((0, 4),)),
        "lengths": draw_lengths(jax.random.fold_in(jax.random.fold_in(keys[8], part), 71), part),
        "cotangent": normal_values(part_keys[7], (TOKENS, NHEADS * HEADDIM), 0.2, 1.5, ((0, 4), (1, 4))),
    }


PRECISE = lax.Precision.HIGHEST

def step_sizes(step_rows, decay_rate, mask_rows, seq_count, block_len, groups):
    step_size = jax.nn.softplus(step_rows) * mask_rows[:, None]
    head_count = decay_rate.shape[0]
    five_dims = (seq_count, -1, block_len, head_count // groups, groups)
    return (step_size.reshape(five_dims), (-(step_size * decay_rate[None, :])).reshape(five_dims))

def main_terms(in_rows, step_rows, b_rows, c_rows, decay_rate, skip_gain, mask_rows, seq_count, block_len):
    groups, state_dim = (b_rows.shape[1], b_rows.shape[2])
    head_count = decay_rate.shape[0]
    head_width = in_rows.shape[1] // head_count
    per_group = head_count // groups
    step_size, log_step = step_sizes(step_rows, decay_rate, mask_rows, seq_count, block_len, groups)
    within = jnp.cumsum(log_step, axis=2)
    totals = within[:, :, -1]
    blocks = within.shape[1]
    x_dims = (seq_count, blocks, block_len, per_group, groups, head_width)
    g_dims = (seq_count, blocks, block_len, groups, state_dim)
    x_round = in_rows.astype(jnp.bfloat16).astype(jnp.float32).reshape(x_dims)
    b_round = b_rows.astype(jnp.bfloat16).astype(jnp.float32).reshape(g_dims)
    c_round = c_rows.astype(jnp.bfloat16).astype(jnp.float32).reshape(g_dims)
    scores = jnp.einsum('sktgn,skugn->skgtu', c_round, b_round, precision=PRECISE)
    within_t = jnp.moveaxis(within, 2, -1)
    spread = within_t[..., :, None] - within_t[..., None, :]
    causal = jnp.arange(block_len)[:, None] >= jnp.arange(block_len)[None, :]
    decays = jnp.where(causal, jnp.exp(jnp.where(causal, spread, 0.0)), 0.0)
    weights = (scores[:, :, None] * decays * jnp.moveaxis(step_size, 2, -1)[..., None, :]).astype(jnp.bfloat16)
    inside = jnp.einsum('skmgtu,skumgp->sktmgp', weights.astype(jnp.float32), x_round, precision=PRECISE)
    scaled = (in_rows.reshape(x_dims) * (step_size * jnp.exp(totals[:, :, None] - within))[..., None]).astype(jnp.bfloat16)
    block_states = jnp.einsum('skugn,skumgp->skmgnp', b_round, scaled.astype(jnp.float32), precision=PRECISE)
    running = jnp.zeros((seq_count, per_group, groups, state_dim, head_width), jnp.float32)
    entering = []
    for block_index in range(blocks):
        entering.append(running)
        running = jnp.exp(totals[:, block_index])[..., None, None] * running + block_states[:, block_index]
    entered = jnp.stack(entering, axis=1)
    across = jnp.einsum('sktgn,skmgnp->sktmgp', c_rows.reshape(g_dims), entered, precision=PRECISE) * jnp.exp(within)[..., None]
    skip_term = skip_gain.reshape(per_group, groups)[:, :, None] * in_rows.reshape(x_dims)
    result = (inside + across + skip_term) * mask_rows.reshape(seq_count, blocks, block_len, 1, 1, 1)
    return (result.reshape(in_rows.shape), lax.optimization_barrier(jnp.sum(totals, axis=1)), running)

def corr_terms(step_rows, c_rows, start_rows, decay_rate, mask_rows, seq_count, block_len):
    groups, state_dim = (c_rows.shape[1], c_rows.shape[2])
    head_count = decay_rate.shape[0]
    step_size, log_step = step_sizes(step_rows, decay_rate, mask_rows, seq_count, block_len, groups)
    blocks = log_step.shape[1]
    whole = jnp.cumsum(log_step.reshape(seq_count, blocks * block_len, head_count // groups, groups), axis=1).reshape(log_step.shape)
    c_dims = (seq_count, blocks, block_len, groups, state_dim)
    result = jnp.einsum('sktgn,smgnp->sktmgp', c_rows.reshape(c_dims), start_rows, precision=PRECISE) * jnp.exp(whole)[..., None]
    result = result * mask_rows.reshape(seq_count, blocks, block_len, 1, 1, 1)
    return result.reshape(c_rows.shape[0], -1)

def reference(inputs, step_raw, decay_rate, skip_gain, b_proj, c_proj, lengths, cotangent):
    row_count = SEQS_DEV * SLOT_LEN
    slot_ids = jnp.arange(SLOT_LEN, dtype=jnp.int32)
    resp_mask = (slot_ids[None, :] < lengths[:, None]).astype(jnp.float32).reshape(-1)
    full_mask = jnp.concatenate([jnp.ones((PREFIX_DEVS * row_count,), jnp.float32), resp_mask]).reshape(N_SEQ, row_count)
    b_full = b_proj.astype(jnp.float32)
    c_full = c_proj.astype(jnp.float32)

    def per_device(array):
        return array.reshape((N_SEQ, row_count) + array.shape[1:])

    def shard_forward(in_rows, step_rows, b_rows, c_rows, rate_rows, gain_rows):

        def local_part(in_dev, step_dev, b_dev, c_dev, mask_dev):
            return main_terms(in_dev, step_dev, b_dev, c_dev, rate_rows, gain_rows, mask_dev, SEQS_DEV, BLOCK)
        local_out, log_total, local_state = jax.vmap(local_part)(per_device(in_rows), per_device(step_rows), per_device(b_rows), per_device(c_rows), full_mask)
        running = jnp.zeros(local_state.shape[1:], jnp.float32)
        starts = []
        for piece in range(PREFIX_DEVS):
            starts.append(running)
            running = jnp.exp(log_total[piece])[..., None, None] * running + local_state[piece]
        responded = jnp.broadcast_to(running[None], (N_SEQ - PREFIX_DEVS,) + running.shape)
        start_all = jnp.concatenate([jnp.stack(starts), responded])

        def corr_part(step_dev, c_dev, start_dev, mask_dev):
            return corr_terms(step_dev, c_dev, start_dev, rate_rows, mask_dev, SEQS_DEV, BLOCK)
        correction = jax.vmap(corr_part)(per_device(step_rows), per_device(c_rows), start_all, full_mask)
        return (local_out + correction).reshape(TOKENS, -1)

    def per_shard(totals_carry, pieces):
        in_piece, step_piece, cot_piece, rate_piece, gain_piece = pieces

        def forward(in_rows, step_rows, b_rows, c_rows):
            return shard_forward(in_rows, step_rows, b_rows, c_rows, rate_piece, gain_piece)
        y_full, backward = jax.vjp(forward, in_piece.astype(jnp.float32), step_piece, b_full, c_full)
        grad_x, grad_s, grad_bp, grad_cp = backward(cot_piece.astype(jnp.float32))
        return ((totals_carry[0] + grad_bp, totals_carry[1] + grad_cp), (y_full.astype(jnp.bfloat16), grad_x.astype(jnp.bfloat16), grad_s))

    def split_heads(array):
        return array.reshape(TOKENS, N_HEAD, -1).transpose(1, 0, 2)

    def join_heads(array):
        return array.transpose(1, 0, 2).reshape(TOKENS, -1)
    zero_grad = jnp.zeros(b_proj.shape, jnp.float32)
    (grad_b, grad_c), (outs_y, outs_x, outs_s) = lax.scan(per_shard, (zero_grad, zero_grad), (split_heads(inputs), split_heads(step_raw), split_heads(cotangent), decay_rate.reshape(N_HEAD, -1), skip_gain.reshape(N_HEAD, -1)))
    return (join_heads(outs_y), join_heads(outs_x), join_heads(outs_s), grad_b, grad_c)
```

```python
import functools

import jax
import jax.numpy as jnp
from jax import lax
from jax.experimental import pallas as pl
from jax.experimental.pallas import tpu as pltpu
from jax.sharding import PartitionSpec as P

BLOCK = 256
PREFIX_DEVS = 2
LANES = 128
LAG = 2
F32 = jnp.float32
BF16 = jnp.bfloat16
EXACT = lax.Precision.HIGHEST


def mm(a, b, ca, cb):
    return lax.dot_general(a, b, (((ca,), (cb,)), ((), ())), preferred_element_type=F32)


def layer_kernel(
    peers, ranks, heads, groups,
    x_ref, dy_ref, b_ref, c_ref, step_ref, gain_ref, decay_ref, lengths_ref,
    y_ref, dx_ref, gs_ref, db_out, dc_out,
    wi_b, dt_b, wi_t, dt_t, state, first_state, grad_own, later_grad,
    state_in, state_out, grad_in, grad_out, y_acc, dx_acc, q_acc, mask_b, gain_b, decay_b,
    parts, arrived, summed, fs_sem, fr_sem, bs_sem, br_sem, ps_sem, pr_sem, ss_sem, sr_sem,
):
    pos = lax.axis_index("seq")
    rank = lax.axis_index("head")
    prefix = jnp.where(pos < PREFIX_DEVS, 1.0, 0.0).astype(F32)
    rows = x_ref.shape[0]
    blocks = rows // BLOCK
    pairs = groups // 2
    half = groups * 64
    low = lax.broadcasted_iota(jnp.int32, (1, LANES), 1) < 64

    share = rows // ranks
    barrier = pltpu.get_barrier_semaphore()
    for away in range(1, ranks):
        pl.semaphore_signal(
            barrier, inc=1, device_id={"head": lax.rem(rank + away, ranks)},
            device_id_type=pl.DeviceIdType.MESH,
        )

    @pl.when(pos > 0)
    def _():
        pl.semaphore_signal(barrier, inc=1, device_id={"seq": pos - 1}, device_id_type=pl.DeviceIdType.MESH)

    @pl.when(pos < peers - 1)
    def _():
        pl.semaphore_signal(barrier, inc=1, device_id={"seq": pos + 1}, device_id_type=pl.DeviceIdType.MESH)

    tri = lax.broadcasted_iota(jnp.int32, (BLOCK, BLOCK), 0) >= lax.broadcasted_iota(
        jnp.int32, (BLOCK, BLOCK), 1
    )

    def span(k):
        return slice(k * BLOCK, (k + 1) * BLOCK)

    limit = jnp.where(pos < PREFIX_DEVS, rows, lengths_ref[jnp.maximum(pos - PREFIX_DEVS, 0)])
    ids = lax.broadcasted_iota(jnp.int32, (1, BLOCK), 1)
    for h in range(heads):
        gain_b[h : h + 1, :] = jnp.full((1, LANES), gain_ref[h], F32)
        decay_b[h : h + 1, :] = jnp.full((1, LANES), decay_ref[h], F32)
    rate = jnp.concatenate([decay_b[...]] * (BLOCK // LANES), axis=1)

    def kept(k):
        return jnp.where(ids + k * BLOCK < limit, 1.0, 0.0).astype(F32)

    for k in range(blocks):
        raw = step_ref[:, span(k)]
        keep = kept(k)
        step = (jnp.maximum(raw, 0.0) + jnp.log1p(jnp.exp(-jnp.abs(raw)))) * keep
        sums = lax.dot_general(
            -(step * rate), tri.astype(F32), (((1,), (1,)), ((), ())),
            preferred_element_type=F32, precision=EXACT,
        )
        wi_t[:, span(k)] = sums
        dt_t[:, span(k)] = step
        tall = jnp.concatenate(
            [step, sums, jnp.broadcast_to(keep, (LANES - 2 * heads, BLOCK))], axis=0
        ).T
        for h in range(heads):
            wi_b[h, span(k), :] = jnp.broadcast_to(tall[:, heads + h : heads + h + 1], (BLOCK, LANES))
            dt_b[h, span(k), :] = jnp.broadcast_to(tall[:, h : h + 1], (BLOCK, LANES))
        mask_b[span(k), :] = jnp.broadcast_to(tall[:, 2 * heads : 2 * heads + 1], (BLOCK, LANES))

    def turn(v):
        return pltpu.roll(v, 64, 1)

    def slabs(ref, p):
        lo = ref[:, pl.ds(pl.multiple_of(p * LANES, LANES), LANES)].astype(F32)
        hi = ref[:, pl.ds(pl.multiple_of(half + p * LANES, LANES), LANES)].astype(F32)
        return lo, hi

    def join(lo, hi):
        return jnp.where(low, lo, turn(hi)), jnp.where(low, turn(lo), hi)

    def by_head(ref, g, k):
        return jnp.where(low, ref[g, span(k), :], ref[groups + g, span(k), :])

    def total(g, k):
        at = pl.ds((k + 1) * BLOCK - 1, 1)
        return jnp.where(low, wi_b[g, at, :], wi_b[groups + g, at, :])

    def hop_f(p):
        part = pl.ds(2 * p, 2)
        return pltpu.make_async_remote_copy(
            src_ref=state_out.at[part], dst_ref=state_in.at[part],
            send_sem=fs_sem.at[p], recv_sem=fr_sem.at[p],
            device_id={"seq": pos + 1}, device_id_type=pl.DeviceIdType.MESH,
        )

    def hop_b(p):
        part = pl.ds(2 * p, 2)
        return pltpu.make_async_remote_copy(
            src_ref=grad_out.at[part], dst_ref=grad_in.at[part],
            send_sem=bs_sem.at[p], recv_sem=br_sem.at[p],
            device_id={"seq": pos - 1}, device_id_type=pl.DeviceIdType.MESH,
        )

    def give(g, away):
        to = lax.rem(rank + away, ranks)
        return pltpu.make_async_remote_copy(
            src_ref=parts.at[g, :, pl.ds(pl.multiple_of(to * share, share), share), :],
            dst_ref=arrived.at[away - 1, g],
            send_sem=ps_sem.at[away - 1, g], recv_sem=pr_sem.at[away - 1, g],
            device_id={"head": to}, device_id_type=pl.DeviceIdType.MESH,
        )

    def piece(g, kind, owner):
        return parts.at[g, kind, pl.ds(pl.multiple_of(owner * share, share), share), :]

    def flip(bit):
        low_bit = lax.rem(rank, 2)
        if bit == 1:
            return rank + 1 - 2 * low_bit
        if bit == 2:
            return lax.rem(rank + 2, 4)
        return lax.rem(rank + 2, 4) + 1 - 2 * low_bit

    def first_hop(g, kind, which):
        to = flip(kind + 1)
        return pltpu.make_async_remote_copy(
            src_ref=piece(g, kind, to if which == 0 else flip(3)),
            dst_ref=arrived.at[which, g, kind],
            send_sem=ps_sem.at[2 * kind + which, g], recv_sem=pr_sem.at[2 * kind + which, g],
            device_id={"head": to}, device_id_type=pl.DeviceIdType.MESH,
        )

    def second_hop(g, kind):
        to = flip(2 - kind)
        return pltpu.make_async_remote_copy(
            src_ref=piece(g, kind, to), dst_ref=summed.at[g, kind],
            send_sem=ss_sem.at[kind, g], recv_sem=sr_sem.at[kind, g],
            device_id={"head": to}, device_id_type=pl.DeviceIdType.MESH,
        )

    square = ranks == 4

    def send_group(g):
        if square:
            for which in (1, 0):
                for kind in range(2):
                    first_hop(g, kind, which).start()
        else:
            for away in range(1, ranks):
                give(g, away).start()

    def forward_group(g):
        if square:
            for kind in range(2):
                first_hop(g, kind, 1).wait_recv()
                at = pl.ds(pl.multiple_of(flip(2 - kind) * share, share), share)
                parts[g, kind, at, :] += arrived[1, g, kind]
                second_hop(g, kind).start()

    def collect_group(g):
        own = pl.ds(pl.multiple_of(rank * share, share), share)
        for kind, out in enumerate((db_out, dc_out)):
            val = parts[g, kind, own, :]
            if square:
                first_hop(g, kind, 0).wait_recv()
                second_hop(g, kind).wait_recv()
                val = val + arrived[0, g, kind] + summed[g, kind]
            else:
                if kind == 0:
                    for away in range(1, ranks):
                        give(g, away).wait_recv()
                for away in range(1, ranks):
                    val = val + arrived[away - 1, g, kind]
            out[:, g, :] = val

    def settle_group(g):
        if square:
            for kind in range(2):
                for which in range(2):
                    first_hop(g, kind, which).wait_send()
                second_hop(g, kind).wait_send()
        else:
            for away in range(1, ranks):
                give(g, away).wait_send()

    def whole(g):
        return jnp.exp(prefix * (total(g, 0) + total(g, 1)))

    def pass_f(p):
        for j in range(2):
            g = 2 * p + j
            state_out[g] = whole(g) * state_in[g] + prefix * state[g]
        hop_f(p).start()

    def pass_b(p):
        for j in range(2):
            g = 2 * p + j
            grad_out[g] = whole(g) * grad_in[g] + grad_own[g]
        hop_b(p).start()

    @pl.when(pos == 0)
    def _():
        state_in[...] = jnp.zeros_like(state_in)

    @pl.when(pos == peers - 1)
    def _():
        grad_in[...] = jnp.zeros_like(grad_in)

    @pl.when(jnp.logical_or(pos == 0, pos == peers - 1))
    def _():
        pl.semaphore_wait(barrier, ranks)

    @pl.when(jnp.logical_and(pos > 0, pos < peers - 1))
    def _():
        pl.semaphore_wait(barrier, ranks + 1)

    def local_states(p, carry):
        xs = join(*slabs(x_ref, p))
        dys = join(*slabs(dy_ref, p))
        for j in range(2):
            g = 2 * p + j
            adds, backs = [], []
            for k in range(blocks):
                wi = by_head(wi_b, g, k)
                dt = by_head(dt_b, g, k)
                scaled = (xs[j][span(k)] * (dt * jnp.exp(total(g, k) - wi))).astype(BF16)
                adds.append(mm(b_ref[g, span(k), :], scaled, 0, 0))
                lifted = (dys[j][span(k)] * mask_b[span(k), :] * jnp.exp(wi)).astype(BF16)
                backs.append(mm(c_ref[g, span(k), :], lifted, 0, 0))
            first_state[g] = adds[0]
            state[g] = jnp.exp(total(g, 1)) * adds[0] + adds[1]
            later_grad[g] = backs[1]
            grad_own[g] = backs[0] + jnp.exp(total(g, 0)) * backs[1]

        @pl.when(pos == 0)
        def _():
            pass_f(p)

        @pl.when(pos == peers - 1)
        def _():
            pass_b(p)

        return carry

    lax.fori_loop(0, pairs, local_states, 0)

    def inside(p):
        xs = join(*slabs(x_ref, p))
        dys = join(*slabs(dy_ref, p))
        for j in range(2):
            g = 2 * p + j
            for k in range(blocks):
                b_blk = b_ref[g, span(k), :]
                c_blk = c_ref[g, span(k), :]
                scores = mm(c_blk, b_blk, 1, 1)
                x16 = xs[j][span(k)].astype(BF16)
                dyf = dys[j][span(k)] * mask_b[span(k), :]
                dy16 = dyf.astype(BF16)
                ys, dxs = [], []
                d_scores = None
                for m in range(2):
                    h = m * groups + g
                    col = wi_b[h, span(k), :]
                    col = jnp.concatenate([col, col], axis=1)
                    row = wi_t[pl.ds(h, 1), span(k)]
                    decay = jnp.where(tri, jnp.exp(jnp.minimum(col - row, 0.0)), 0.0)
                    decay = decay * dt_t[pl.ds(h, 1), span(k)]
                    weights = (scores * decay).astype(BF16)
                    mine = low if m == 0 else jnp.logical_not(low)
                    dy_m = jnp.where(mine, dyf, 0.0).astype(BF16)
                    d_weights = mm(dy_m, x16, 1, 1) * decay
                    d_scores = d_weights if d_scores is None else d_scores + d_weights
                    ys.append(mm(weights, x16, 1, 0))
                    dxs.append(mm(weights, dy16, 0, 0))
                y_acc[g, span(k), :] = jnp.where(low, ys[0], ys[1])
                dx_acc[g, span(k), :] = jnp.where(low, dxs[0], dxs[1])
                ds16 = d_scores.astype(BF16)
                parts[g, 1, span(k), :] = mm(ds16, b_blk, 1, 0)
                parts[g, 0, span(k), :] = mm(ds16, c_blk, 0, 0)

    q_acc[...] = jnp.zeros_like(q_acc)
    last = lax.broadcasted_iota(jnp.int32, (BLOCK, 1), 0) == BLOCK - 1
    pick_row = lax.broadcasted_iota(jnp.int32, (4 * LANES, LANES), 0)
    pick_col = lax.broadcasted_iota(jnp.int32, (4 * LANES, LANES), 1)
    pick_head = (
        jnp.where(pick_row % LANES >= 64, groups, 0) + jnp.where(pick_row >= 2 * LANES, heads, 0)
    )

    def across(p):
        @pl.when(pos == peers - 1)
        def _():
            hop_f(p).wait_recv()

        @pl.when(pos == 0)
        def _():
            hop_b(p).wait_recv()

        xs = join(*slabs(x_ref, p))
        dys = join(*slabs(dy_ref, p))
        y_parts, dx_parts = [], []
        for j in range(2):
            g = 2 * p + j
            pick = (pick_col == pick_head + g).astype(BF16)
            gain = jnp.where(low, gain_b[pl.ds(g, 1), :], gain_b[pl.ds(groups + g, 1), :])
            start = state_in[g]
            carry_grad = prefix * grad_in[g]
            entered = (start, jnp.exp(total(g, 0)) * start + first_state[g])
            leaving = (later_grad[g] + jnp.exp(total(g, 1)) * carry_grad, carry_grad)
            y_rows, dx_rows = [], []
            for k in range(blocks):
                wi = by_head(wi_b, g, k)
                dt = by_head(dt_b, g, k)
                end = total(g, k)
                up = jnp.exp(wi)
                down = dt * jnp.exp(end - wi)
                e16 = entered[k].astype(BF16)
                g16 = leaving[k].astype(BF16)
                x = xs[j][span(k)]
                mask = mask_b[span(k), :]
                dy = dys[j][span(k)] * mask
                b_blk = b_ref[g, span(k), :]
                c_blk = c_ref[g, span(k), :]
                y = y_acc[g, span(k), :] + up * mm(c_blk, e16, 1, 0)
                dx_s = down * mm(b_blk, g16, 1, 0)
                dx = dx_acc[g, span(k), :] + dx_s
                parts[g, 1, span(k), :] += mm((dy * up).astype(BF16), e16, 1, 1)
                parts[g, 0, span(k), :] += mm((x * down).astype(BF16), g16, 1, 1)
                q2 = x * dx
                extra = jnp.sum(x * dx_s, axis=0, keepdims=True) + jnp.exp(end) * jnp.sum(
                    leaving[k] * entered[k], axis=0, keepdims=True
                )
                q1 = dy * y - q2 + jnp.where(last, extra, 0.0)
                q1h = q1.astype(BF16)
                q2h = q2.astype(BF16)
                q1l = (q1 - q1h.astype(F32)).astype(BF16)
                q2l = (q2 - q2h.astype(F32)).astype(BF16)
                q_acc[span(k), :] += mm(jnp.concatenate([q1h, q1l, q2h, q2l], axis=1), pick, 1, 0)
                y_rows.append((y + gain * x) * mask)
                dx_rows.append(dx + gain * dy)
            send_group(g)
            y_parts.append(jnp.concatenate(y_rows, axis=0))
            dx_parts.append(jnp.concatenate(dx_rows, axis=0))
        for ref, pair in ((y_ref, y_parts), (dx_ref, dx_parts)):
            lo, hi = join(*pair)
            ref[:, pl.ds(pl.multiple_of(p * LANES, LANES), LANES)] = lo.astype(BF16)
            ref[:, pl.ds(pl.multiple_of(half + p * LANES, LANES), LANES)] = hi.astype(BF16)

    lag = max(1, peers - 3)
    middle = jnp.logical_and(pos > 0, pos < peers - 1)

    def stage(s, carry):
        pf = s - (pos - 1)
        pb = s - (peers - 2 - pos)

        @pl.when(jnp.logical_and(middle, jnp.logical_and(pf >= 0, pf < pairs)))
        def _():
            hop_f(pf).wait_recv()
            pass_f(pf)

        @pl.when(jnp.logical_and(middle, jnp.logical_and(pb >= 0, pb < pairs)))
        def _():
            hop_b(pb).wait_recv()
            pass_b(pb)

        @pl.when(s < pairs)
        def _():
            inside(s)

        @pl.when(jnp.logical_and(s >= lag, s < pairs + lag))
        def _():
            across(s - lag)

        @pl.when(jnp.logical_and(s > lag, s < pairs + lag))
        def _():
            for j in range(2):
                forward_group(2 * (s - lag - 1) + j)

        return carry

    lax.fori_loop(0, pairs + lag, stage, 0)
    for g in range(groups - 2, groups):
        forward_group(g)

    for k in range(blocks):
        q = q_acc[span(k), :].T
        step = dt_t[:, span(k)]
        d_log = lax.dot_general(
            q[:heads], tri.astype(F32), (((1,), (0,)), ((), ())),
            preferred_element_type=F32, precision=EXACT,
        )
        slope = jax.nn.sigmoid(step_ref[:, span(k)]) * kept(k)
        safe = jnp.where(step > 0.0, step, 1.0)
        gs_ref[:, span(k)] = slope * (q[heads : 2 * heads] / safe - rate * d_log)

    for g in range(groups):
        collect_group(g)
    for g in range(groups):
        settle_group(g)

    def finish(p, carry):
        @pl.when(pos < peers - 1)
        def _():
            hop_f(p).wait_send()

        @pl.when(pos > 0)
        def _():
            hop_b(p).wait_send()

        return carry

    lax.fori_loop(0, pairs, finish, 0)


def paired_kernel(
    peers, heads, groups,
    x_ref, dy_ref, b_ref, c_ref, step_ref, gain_ref, decay_ref, lengths_ref,
    y_ref, dx_ref, gs_ref, db_out, dc_out,
    wi_b, dt_b, wd_t, wd_f, wi_f, dt_f, xj, dyj, fx, fdy,
    state, first_state, grad_own, later_grad, state_in, state_out, grad_in, grad_out,
    y_acc, dx_acc, q_acc, mask_b, gain_b, decay_b, parts, arrived, summed,
    xs_sem, xr_sem, ws_sem, wr_sem, fs_sem, fr_sem, bs_sem, br_sem, ps_sem, pr_sem, ss_sem, sr_sem,
):
    ranks = 4
    pos = lax.axis_index("seq")
    rank = lax.axis_index("head")
    bit_x = lax.rem(rank, 2)
    bit_y = rank // 2
    prefix = jnp.where(pos < PREFIX_DEVS, 1.0, 0.0).astype(F32)
    rows = x_ref.shape[0]
    blocks = rows // BLOCK
    pairs = groups // 2
    half = groups * 64
    share = rows // ranks
    zero_unit = groups + pairs
    low = lax.broadcasted_iota(jnp.int32, (1, LANES), 1) < 64
    mesh_id = pl.DeviceIdType.MESH

    def bit(par):
        return (1 - par) * bit_x + par * bit_y

    def beside(par):
        return rank + (1 - par) * (1 - 2 * bit_x) + 2 * par * (1 - 2 * bit_y)

    def mine(p):
        return 2 * p + bit(p % 2)

    def given(p):
        return 2 * p + 1 - bit(p % 2)

    barrier = pltpu.get_barrier_semaphore()
    for par in range(2):
        pl.semaphore_signal(barrier, inc=1, device_id={"head": beside(par)}, device_id_type=mesh_id)

    @pl.when(pos > 0)
    def _():
        pl.semaphore_signal(barrier, inc=1, device_id={"seq": pos - 1}, device_id_type=mesh_id)

    @pl.when(pos < peers - 1)
    def _():
        pl.semaphore_signal(barrier, inc=1, device_id={"seq": pos + 1}, device_id_type=mesh_id)

    def span(k):
        return slice(k * BLOCK, (k + 1) * BLOCK)

    tri = lax.broadcasted_iota(jnp.int32, (BLOCK, BLOCK), 0) >= lax.broadcasted_iota(
        jnp.int32, (BLOCK, BLOCK), 1
    )
    limit = jnp.where(pos < PREFIX_DEVS, rows, lengths_ref[jnp.maximum(pos - PREFIX_DEVS, 0)])
    ids = lax.broadcasted_iota(jnp.int32, (1, BLOCK), 1)
    tall_ids = lax.broadcasted_iota(jnp.int32, (BLOCK, LANES), 0)

    def kept(k):
        return jnp.where(ids + k * BLOCK < limit, 1.0, 0.0).astype(F32)

    def turn(v):
        return pltpu.roll(v, 64, 1)

    def join(lo, hi):
        return jnp.where(low, lo, turn(hi)), jnp.where(low, turn(lo), hi)

    def copy_of(src, dst, send, recv, where):
        return pltpu.make_async_remote_copy(
            src_ref=src, dst_ref=dst, send_sem=send, recv_sem=recv, device_id=where, device_id_type=mesh_id
        )

    def raw(p, which):
        src, dst = ((xj, fx), (dyj, fdy))[which]
        return copy_of(
            src.at[given(p)], dst.at[p], xs_sem.at[which, p], xr_sem.at[which, p], {"head": beside(p % 2)}
        )

    def tell(par):
        return copy_of(wd_t, wd_f.at[par], ws_sem.at[par], wr_sem.at[par], {"head": beside(par)})

    def hop_f(u):
        return copy_of(state_out.at[u], state_in.at[u], fs_sem.at[u], fr_sem.at[u], {"seq": pos + 1})

    def hop_b(u):
        return copy_of(grad_out.at[u], grad_in.at[u], bs_sem.at[u], br_sem.at[u], {"seq": pos - 1})

    def piece(p, kind, owner):
        return parts.at[p, kind, pl.ds(pl.multiple_of(owner * share, share), share), :]

    def first_hop(p, kind, which):
        par = p % 2
        to = beside(1 - par)
        opposite = 3 - rank
        return copy_of(
            piece(p, kind, to if which == 0 else opposite), arrived.at[which, p, kind],
            ps_sem.at[which, p, kind], pr_sem.at[which, p, kind], {"head": to},
        )

    def second_hop(p, kind):
        to = beside(p % 2)
        return copy_of(
            piece(p, kind, to), summed.at[p, kind], ss_sem.at[p, kind], sr_sem.at[p, kind], {"head": to}
        )

    for k in range(blocks):
        mask_b[span(k), :] = jnp.where(tall_ids + k * BLOCK < limit, 1.0, 0.0).astype(F32)

    def spread(p):
        at_lo = pl.ds(pl.multiple_of(p * LANES, LANES), LANES)
        at_hi = pl.ds(pl.multiple_of(half + p * LANES, LANES), LANES)
        xj[2 * p], xj[2 * p + 1] = join(x_ref[:, at_lo].astype(F32), x_ref[:, at_hi].astype(F32))
        mask = mask_b[...]
        dyj[2 * p], dyj[2 * p + 1] = join(dy_ref[:, at_lo].astype(F32) * mask, dy_ref[:, at_hi].astype(F32) * mask)

    for p in range(2):
        spread(p)

    @pl.when(jnp.logical_or(pos == 0, pos == peers - 1))
    def _():
        pl.semaphore_wait(barrier, 3)

    @pl.when(jnp.logical_and(pos > 0, pos < peers - 1))
    def _():
        pl.semaphore_wait(barrier, 4)

    for which in range(2):
        for p in range(2):
            raw(p, which).start()

    for h in range(heads):
        gain_b[h : h + 1, :] = jnp.full((1, LANES), gain_ref[h], F32)
        decay_b[h : h + 1, :] = jnp.full((1, LANES), decay_ref[h], F32)
    rate = jnp.concatenate([decay_b[...]] * (BLOCK // LANES), axis=1)
    for k in range(blocks):
        step_in = step_ref[:, span(k)]
        step = (jnp.maximum(step_in, 0.0) + jnp.log1p(jnp.exp(-jnp.abs(step_in)))) * kept(k)
        sums = lax.dot_general(
            -(step * rate), tri.astype(F32), (((1,), (1,)), ((), ())),
            preferred_element_type=F32, precision=EXACT,
        )
        wd_t[0, :, span(k)] = sums
        wd_t[1, :, span(k)] = step
    for par in range(2):
        tell(par).start()
    for p in range(2, pairs):
        spread(p)
        for which in range(2):
            raw(p, which).start()
    state_in[zero_unit] = jnp.zeros_like(state_in[zero_unit])
    grad_in[zero_unit] = jnp.zeros_like(grad_in[zero_unit])
    for k in range(blocks):
        tall = jnp.concatenate(
            [wd_t[1, :, span(k)], wd_t[0, :, span(k)], jnp.zeros((LANES - 2 * heads, BLOCK), F32)], axis=0
        ).T
        for h in range(heads):
            wi_b[h, span(k), :] = jnp.broadcast_to(tall[:, heads + h : heads + h + 1], (BLOCK, LANES))
            dt_b[h, span(k), :] = jnp.broadcast_to(tall[:, h : h + 1], (BLOCK, LANES))

    class Own:
        def __init__(self, g):
            self.unit, self.group = g, g

        def x(self, k):
            return xj[self.group, span(k), :]

        def dy(self, k):
            return dyj[self.group, span(k), :]

        def within(self, k):
            return jnp.where(low, wi_b[self.group, span(k), :], wi_b[groups + self.group, span(k), :])

        def step(self, k):
            return jnp.where(low, dt_b[self.group, span(k), :], dt_b[groups + self.group, span(k), :])

        def total(self, k):
            at = pl.ds((k + 1) * BLOCK - 1, 1)
            return jnp.where(low, wi_b[self.group, at, :], wi_b[groups + self.group, at, :])

    class Handed:
        def __init__(self, p):
            self.unit, self.group, self.pair = groups + p, mine(p), p

        def x(self, k):
            return fx[self.pair, span(k), :]

        def dy(self, k):
            return fdy[self.pair, span(k), :]

        def within(self, k):
            return wi_f[self.pair, span(k), :]

        def step(self, k):
            return dt_f[self.pair, span(k), :]

        def total(self, k):
            return wi_f[self.pair, pl.ds((k + 1) * BLOCK - 1, 1), :]

    def whole(part):
        return jnp.exp(prefix * (part.total(0) + part.total(1)))

    def start_of(u):
        return state_in[jnp.where(pos > 0, u, zero_unit)]

    def carry_of(u):
        return grad_in[jnp.where(pos < PREFIX_DEVS, u, zero_unit)]

    def entered_by(part):
        start = start_of(part.unit)
        return start, jnp.exp(part.total(0)) * start + first_state[part.unit]

    def leaving_by(part):
        carry = carry_of(part.unit)
        return later_grad[part.unit] + jnp.exp(part.total(1)) * carry, carry

    def pass_f(part):
        u = part.unit
        state_out[u] = whole(part) * start_of(u) + prefix * state[u]
        hop_f(u).start()

    def pass_b(part):
        u = part.unit
        held = grad_in[jnp.where(pos < peers - 1, u, zero_unit)]
        grad_out[u] = whole(part) * held + grad_own[u]
        hop_b(u).start()

    def emit(part):
        @pl.when(pos == 0)
        def _():
            pass_f(part)

        @pl.when(pos == peers - 1)
        def _():
            pass_b(part)

    def relay_f(part):
        @pl.when(pos > 0)
        def _():
            hop_f(part.unit).wait_recv()

        @pl.when(jnp.logical_and(pos > 0, pos < peers - 1))
        def _():
            pass_f(part)

    def relay_b(part):
        @pl.when(pos < peers - 1)
        def _():
            hop_b(part.unit).wait_recv()

        @pl.when(jnp.logical_and(pos > 0, pos < peers - 1))
        def _():
            pass_b(part)

    def relay(i, how):
        @pl.when(jnp.logical_and(i >= 0, i < pairs))
        def _():
            how(Own(mine(i)))

        r = i - pairs
        p = 2 * (r // 4) + r % 2

        @pl.when(jnp.logical_and(jnp.logical_and(r >= 0, r < 2 * pairs), r % 4 < 2))
        def _():
            how(Handed(p))

        @pl.when(jnp.logical_and(jnp.logical_and(r >= 0, r < 2 * pairs), r % 4 >= 2))
        def _():
            how(Own(given(p)))

    def serve(slot):
        relay(slot + LAG - LAG * pos, relay_f)
        relay(slot + LAG - LAG * (peers - 1 - pos), relay_b)

    def local_states(part):
        u, g = part.unit, part.group
        adds, backs = [], []
        for k in range(blocks):
            wi = part.within(k)
            scaled = (part.x(k) * (part.step(k) * jnp.exp(part.total(k) - wi))).astype(BF16)
            adds.append(mm(b_ref[g, span(k), :], scaled, 0, 0))
            lifted = (part.dy(k) * jnp.exp(wi)).astype(BF16)
            backs.append(mm(c_ref[g, span(k), :], lifted, 0, 0))
        first_state[u] = adds[0]
        state[u] = jnp.exp(part.total(1)) * adds[0] + adds[1]
        later_grad[u] = backs[1]
        grad_own[u] = backs[0] + jnp.exp(part.total(0)) * backs[1]

    def decay_by(col, row, dt_row):
        col = jnp.concatenate([col, col], axis=1)
        return jnp.where(tri, jnp.exp(jnp.minimum(col - row, 0.0)), 0.0) * dt_row

    def only(m, v):
        return jnp.where(low if m == 0 else jnp.logical_not(low), v, 0.0).astype(BF16)

    def inside(p, g, with_scores):
        for k in range(blocks):
            scores = mm(c_ref[g, span(k), :], b_ref[g, span(k), :], 1, 1)
            x16 = xj[g, span(k), :].astype(BF16)
            dyf = dyj[g, span(k), :]
            dy16 = dyf.astype(BF16)
            ys, dxs, d_scores = [], [], None
            for m in range(2):
                h = m * groups + g
                decay = decay_by(
                    wi_b[h, span(k), :], wd_t[0, pl.ds(h, 1), span(k)], wd_t[1, pl.ds(h, 1), span(k)]
                )
                weights = (scores * decay).astype(BF16)
                if with_scores:
                    d_weights = mm(only(m, dyf), x16, 1, 1) * decay
                    d_scores = d_weights if d_scores is None else d_scores + d_weights
                ys.append(mm(weights, x16, 1, 0))
                dxs.append(mm(weights, dy16, 0, 0))
            y_acc[g, span(k), :] = jnp.where(low, ys[0], ys[1])
            dx_acc[g, span(k), :] = jnp.where(low, dxs[0], dxs[1])
            if with_scores:
                parts[p, 0, span(k), :] = d_scores

    def handed_scores(p):
        g = mine(p)
        for k in range(blocks):
            x16 = fx[p, span(k), :].astype(BF16)
            dyf = fdy[p, span(k), :]
            d_scores = parts[p, 0, span(k), :]
            for m in range(2):
                at = pl.ds(m * groups + g, 1)
                row = wd_f[p % 2, 0, at, span(k)]
                decay = decay_by(jnp.broadcast_to(row, (LANES, BLOCK)).T, row, wd_f[p % 2, 1, at, span(k)])
                d_scores = d_scores + mm(only(m, dyf), x16, 1, 1) * decay
            ds16 = d_scores.astype(BF16)
            parts[p, 1, span(k), :] = mm(ds16, b_ref[g, span(k), :], 1, 0)
            parts[p, 0, span(k), :] = mm(ds16, c_ref[g, span(k), :], 0, 0)

    def grow_c(p):
        both = (Own(mine(p)), Handed(p))
        entered = [entered_by(part) for part in both]
        for k in range(blocks):
            e16 = jnp.concatenate([e[k].astype(BF16) for e in entered], axis=1)
            lifted = jnp.concatenate(
                [(part.dy(k) * jnp.exp(part.within(k))).astype(BF16) for part in both], axis=1
            )
            parts[p, 1, span(k), :] += mm(lifted, e16, 1, 1)

    def grow_b(p):
        both = (Own(mine(p)), Handed(p))
        leaving = [leaving_by(part) for part in both]
        for k in range(blocks):
            g16 = jnp.concatenate([v[k].astype(BF16) for v in leaving], axis=1)
            scaled = jnp.concatenate(
                [
                    (part.x(k) * (part.step(k) * jnp.exp(part.total(k) - part.within(k)))).astype(BF16)
                    for part in both
                ],
                axis=1,
            )
            parts[p, 0, span(k), :] += mm(scaled, g16, 1, 1)

    early_kind = jnp.where(pos < PREFIX_DEVS, 1, 0)
    late_kind = 1 - early_kind

    def send(p, kind):
        for which in (1, 0):
            first_hop(p, kind, which).start()

    def early(p):
        @pl.when(pos < PREFIX_DEVS)
        def _():
            grow_c(p)

        @pl.when(pos >= PREFIX_DEVS)
        def _():
            grow_b(p)

        send(p, early_kind)

    def late(p):
        @pl.when(pos < PREFIX_DEVS)
        def _():
            grow_b(p)

        @pl.when(pos >= PREFIX_DEVS)
        def _():
            grow_c(p)

        send(p, late_kind)

    def forward(p, kind):
        first_hop(p, kind, 1).wait_recv()
        at = pl.ds(pl.multiple_of(beside(p % 2) * share, share), share)
        parts[p, kind, at, :] += arrived[1, p, kind]
        second_hop(p, kind).start()

    def receive(p):
        for which in range(2):
            raw(p, which).wait_recv()
        g = mine(p)
        for k in range(blocks):
            for kind, ref in ((0, wi_f), (1, dt_f)):
                cols = [
                    jnp.broadcast_to(wd_f[p % 2, kind, pl.ds(m * groups + g, 1), span(k)], (64, BLOCK))
                    for m in range(2)
                ]
                ref[p, span(k), :] = jnp.concatenate(cols, axis=0).T
        part = Handed(p)
        local_states(part)
        emit(part)
        handed_scores(p)

    last = lax.broadcasted_iota(jnp.int32, (BLOCK, 1), 0) == BLOCK - 1
    pick_row = lax.broadcasted_iota(jnp.int32, (4 * LANES, LANES), 0)
    pick_col = lax.broadcasted_iota(jnp.int32, (4 * LANES, LANES), 1)
    pick_head = (
        jnp.where(pick_row % LANES >= 64, groups, 0) + jnp.where(pick_row >= 2 * LANES, heads, 0)
    )

    def across(p):
        y_parts, dx_parts = [], []
        for j in range(2):
            g = 2 * p + j
            part = Own(g)
            pick = (pick_col == pick_head + g).astype(BF16)
            gain = jnp.where(low, gain_b[pl.ds(g, 1), :], gain_b[pl.ds(groups + g, 1), :])
            entered = entered_by(part)
            leaving = leaving_by(part)
            y_rows, dx_rows = [], []
            for k in range(blocks):
                wi = part.within(k)
                end = part.total(k)
                up = jnp.exp(wi)
                down = part.step(k) * jnp.exp(end - wi)
                x = part.x(k)
                dy = part.dy(k)
                y = y_acc[g, span(k), :] + up * mm(c_ref[g, span(k), :], entered[k].astype(BF16), 1, 0)
                dx_s = down * mm(b_ref[g, span(k), :], leaving[k].astype(BF16), 1, 0)
                dx = dx_acc[g, span(k), :] + dx_s
                q2 = x * dx
                extra = jnp.sum(x * dx_s, axis=0, keepdims=True) + jnp.exp(end) * jnp.sum(
                    leaving[k] * entered[k], axis=0, keepdims=True
                )
                q1 = dy * y - q2 + jnp.where(last, extra, 0.0)
                q1h = q1.astype(BF16)
                q2h = q2.astype(BF16)
                q1l = (q1 - q1h.astype(F32)).astype(BF16)
                q2l = (q2 - q2h.astype(F32)).astype(BF16)
                q_acc[span(k), :] += mm(jnp.concatenate([q1h, q1l, q2h, q2l], axis=1), pick, 1, 0)
                y_rows.append((y + gain * x) * mask_b[span(k), :])
                dx_rows.append(dx + gain * dy)
            y_parts.append(jnp.concatenate(y_rows, axis=0))
            dx_parts.append(jnp.concatenate(dx_rows, axis=0))
        for ref, pair in ((y_ref, y_parts), (dx_ref, dx_parts)):
            lo, hi = join(*pair)
            ref[:, pl.ds(pl.multiple_of(p * LANES, LANES), LANES)] = lo.astype(BF16)
            ref[:, pl.ds(pl.multiple_of(half + p * LANES, LANES), LANES)] = hi.astype(BF16)

    def loop(start, stop, body):
        def step(i, carry):
            body(i)
            return carry

        lax.fori_loop(start, stop, step, 0)

    def begin(p):
        for j in range(2):
            local_states(Own(2 * p + j))
        emit(Own(mine(p)))

    def within_blocks(p):
        inside(p, mine(p), True)
        inside(p, given(p), False)
        serve(p)

    q_acc[...] = jnp.zeros_like(q_acc)
    loop(0, pairs, begin)
    loop(0, pairs, within_blocks)
    for par in range(2):
        tell(par).wait_recv()

    def in_turn(t):
        @pl.when(t > 0)
        def _():
            loop(6, 8, serve)

        loop(2 * t, 2 * t + 2, receive)
        loop(2 * t, 2 * t + 2, lambda p: emit(Own(given(p))))

        def ahead(p):
            serve(4 + 2 * t + p)
            early(p)

        loop(2 * t, 2 * t + 2, ahead)

    loop(0, pairs // 2, in_turn)
    loop(0, 2, late)
    loop(0, 2, lambda p: forward(p, early_kind))
    loop(10, 12, serve)
    loop(0, 2, across)
    loop(2, 4, lambda p: forward(p, early_kind))
    loop(12, 14, serve)
    loop(2, 4, late)
    loop(0, 2, lambda p: forward(p, late_kind))
    loop(14, 16, serve)
    loop(2, 4, across)
    loop(2, 4, lambda p: forward(p, late_kind))

    for k in range(blocks):
        q = q_acc[span(k), :].T
        step = wd_t[1, :, span(k)]
        d_log = lax.dot_general(
            q[:heads], tri.astype(F32), (((1,), (0,)), ((), ())),
            preferred_element_type=F32, precision=EXACT,
        )
        slope = jax.nn.sigmoid(step_ref[:, span(k)]) * kept(k)
        safe = jnp.where(step > 0.0, step, 1.0)
        gs_ref[:, span(k)] = slope * (q[heads : 2 * heads] / safe - rate * d_log)

    own = pl.ds(pl.multiple_of(rank * share, share), share)
    for late_turn in range(2):
        for p in range(pairs):
            kind = late_kind if late_turn else early_kind
            first_hop(p, kind, 0).wait_recv()
            second_hop(p, kind).wait_recv()
    for p in range(pairs):
        for kind, out in enumerate((db_out, dc_out)):
            kept_sum = parts[p, kind, own, :] + arrived[0, p, kind]
            other = summed[p, kind]
            first = bit(p % 2) == 0
            out[:, 2 * p, :] = jnp.where(first, kept_sum, other)
            out[:, 2 * p + 1, :] = jnp.where(first, other, kept_sum)

    for par in range(2):
        tell(par).wait_send()

    def settle(p):
        for kind in range(2):
            raw(p, kind).wait_send()
            for which in range(2):
                first_hop(p, kind, which).wait_send()
            second_hop(p, kind).wait_send()

    loop(0, pairs, settle)

    def finish(u):
        @pl.when(pos < peers - 1)
        def _():
            hop_f(u).wait_send()

        @pl.when(pos > 0)
        def _():
            hop_b(u).wait_send()

    loop(0, groups + pairs, finish)


def on_device(inputs, step_raw, decay_rate, skip_gain, b_proj, c_proj, lengths, cotangent):
    rows, width = inputs.shape
    heads = decay_rate.shape[0]
    groups, states = b_proj.shape[1:]
    peers = lax.axis_size("seq")
    ranks = lax.axis_size("head")
    hops = 2 if ranks == 4 else ranks - 1
    b_lead = jnp.swapaxes(b_proj, 0, 1)
    c_lead = jnp.swapaxes(c_proj, 0, 1)
    vmem = pl.BlockSpec(memory_space=pltpu.VMEM)
    smem = pl.BlockSpec(memory_space=pltpu.SMEM)
    carry = pltpu.VMEM((groups, states, LANES), F32)
    dma = pltpu.SemaphoreType.DMA((groups // 2,))

    if ranks == 4 and peers == 4:
        pairs = groups // 2
        units = pltpu.VMEM((groups + pairs, states, LANES), F32)
        arriving = pltpu.VMEM((groups + pairs + 1, states, LANES), F32)
        per_pair = pltpu.VMEM((pairs, rows, LANES), F32)
        per_group = pltpu.VMEM((groups, rows, LANES), F32)
        hop = pltpu.SemaphoreType.DMA((groups + pairs,))
        kernel = functools.partial(paired_kernel, peers, heads, groups)
        scratch = [
            pltpu.VMEM((heads, rows, LANES), F32),
            pltpu.VMEM((heads, rows, LANES), F32),
            pltpu.VMEM((2, heads, rows), F32),
            pltpu.VMEM((2, 2, heads, rows), F32),
            per_pair, per_pair, per_group, per_group, per_pair, per_pair,
            units, units, units, units, arriving, units, arriving, units,
            per_group, per_group,
            pltpu.VMEM((rows, LANES), F32),
            pltpu.VMEM((rows, LANES), F32),
            pltpu.VMEM((heads, LANES), F32),
            pltpu.VMEM((heads, LANES), F32),
            pltpu.VMEM((pairs, 2, rows, states), F32),
            pltpu.VMEM((2, pairs, 2, rows // ranks, states), F32),
            pltpu.VMEM((pairs, 2, rows // ranks, states), F32),
            pltpu.SemaphoreType.DMA((2, pairs)),
            pltpu.SemaphoreType.DMA((2, pairs)),
            pltpu.SemaphoreType.DMA((2,)),
            pltpu.SemaphoreType.DMA((2,)),
            hop, hop, hop, hop,
            pltpu.SemaphoreType.DMA((2, pairs, 2)),
            pltpu.SemaphoreType.DMA((2, pairs, 2)),
            pltpu.SemaphoreType.DMA((pairs, 2)),
            pltpu.SemaphoreType.DMA((pairs, 2)),
        ]
    else:
        kernel = functools.partial(layer_kernel, peers, ranks, heads, groups)
        scratch = [
            pltpu.VMEM((heads, rows, LANES), F32),
            pltpu.VMEM((heads, rows, LANES), F32),
            pltpu.VMEM((heads, rows), F32),
            pltpu.VMEM((heads, rows), F32),
            carry, carry, carry, carry, carry, carry, carry, carry,
            pltpu.VMEM((groups, rows, LANES), F32),
            pltpu.VMEM((groups, rows, LANES), F32),
            pltpu.VMEM((rows, LANES), F32),
            pltpu.VMEM((rows, LANES), F32),
            pltpu.VMEM((heads, LANES), F32),
            pltpu.VMEM((heads, LANES), F32),
            pltpu.VMEM((groups, 2, rows, states), F32),
            pltpu.VMEM((hops, groups, 2, rows // ranks, states), F32),
            pltpu.VMEM((groups, 2, rows // ranks, states), F32),
            dma, dma, dma, dma,
            pltpu.SemaphoreType.DMA((max(ranks - 1, 4), groups)),
            pltpu.SemaphoreType.DMA((max(ranks - 1, 4), groups)),
            pltpu.SemaphoreType.DMA((2, groups)),
            pltpu.SemaphoreType.DMA((2, groups)),
        ]

    y, dx, gs, db, dc = pl.pallas_call(
        kernel,
        out_shape=(
            jax.ShapeDtypeStruct((rows, width), BF16),
            jax.ShapeDtypeStruct((rows, width), BF16),
            jax.ShapeDtypeStruct((heads, rows), F32),
            jax.ShapeDtypeStruct((rows // ranks, groups, states), F32),
            jax.ShapeDtypeStruct((rows // ranks, groups, states), F32),
        ),
        in_specs=[vmem] * 5 + [smem] * 3,
        out_specs=(vmem,) * 5,
        scratch_shapes=scratch,
        compiler_params=pltpu.CompilerParams(
            collective_id=0, has_side_effects=True, vmem_limit_bytes=56 * 1024 * 1024
        ),
    )(
        inputs, cotangent, b_lead, c_lead, step_raw.T, skip_gain, decay_rate, lengths
    )
    return (y, dx, gs.T, db, dc)


def solution(mesh):
    rows = P(("dp", "seq"), "head")
    proj = P(("dp", "seq"), None, None)
    grads = P(("dp", "seq", "head"), None, None)
    return jax.shard_map(
        on_device,
        mesh=mesh,
        in_specs=(rows, rows, P("head"), P("head"), proj, proj, P("dp"), rows),
        out_specs=(rows, rows, rows, grads, grads),
        check_vma=False,
    )
```

```python
import functools

import jax
import jax.numpy as jnp
from jax import lax
from jax.experimental import pallas as pl
from jax.experimental.pallas import tpu as pltpu
from jax.sharding import PartitionSpec as P

BLOCK = 256
PREFIX_DEVS = 2
LANES = 128
LAG = 2
F32 = jnp.float32
BF16 = jnp.bfloat16
EXACT = lax.Precision.HIGHEST


def mm(a, b, ca, cb):
    return lax.dot_general(a, b, (((ca,), (cb,)), ((), ())), preferred_element_type=F32)


def layer_kernel(
    peers, ranks, heads, groups,
    x_ref, dy_ref, b_ref, c_ref, step_ref, gain_ref, decay_ref, lengths_ref,
    y_ref, dx_ref, gs_ref, db_out, dc_out,
    wi_b, dt_b, wi_t, dt_t, state, first_state, grad_own, later_grad,
    state_in, state_out, grad_in, grad_out, y_acc, dx_acc, q_acc, mask_b, gain_b, decay_b,
    parts, arrived, summed, fs_sem, fr_sem, bs_sem, br_sem, ps_sem, pr_sem, ss_sem, sr_sem,
):
    pos = lax.axis_index("seq")
    rank = lax.axis_index("head")
    prefix = jnp.where(pos < PREFIX_DEVS, 1.0, 0.0).astype(F32)
    rows = x_ref.shape[0]
    blocks = rows // BLOCK
    pairs = groups // 2
    half = groups * 64
    low = lax.broadcasted_iota(jnp.int32, (1, LANES), 1) < 64

    share = rows // ranks
    barrier = pltpu.get_barrier_semaphore()
    for away in range(1, ranks):
        pl.semaphore_signal(
            barrier, inc=1, device_id={"head": lax.rem(rank + away, ranks)},
            device_id_type=pl.DeviceIdType.MESH,
        )

    @pl.when(pos > 0)
    def _():
        pl.semaphore_signal(barrier, inc=1, device_id={"seq": pos - 1}, device_id_type=pl.DeviceIdType.MESH)

    @pl.when(pos < peers - 1)
    def _():
        pl.semaphore_signal(barrier, inc=1, device_id={"seq": pos + 1}, device_id_type=pl.DeviceIdType.MESH)

    tri = lax.broadcasted_iota(jnp.int32, (BLOCK, BLOCK), 0) >= lax.broadcasted_iota(
        jnp.int32, (BLOCK, BLOCK), 1
    )

    def span(k):
        return slice(k * BLOCK, (k + 1) * BLOCK)

    limit = jnp.where(pos < PREFIX_DEVS, rows, lengths_ref[jnp.maximum(pos - PREFIX_DEVS, 0)])
    ids = lax.broadcasted_iota(jnp.int32, (1, BLOCK), 1)
    for h in range(heads):
        gain_b[h : h + 1, :] = jnp.full((1, LANES), gain_ref[h], F32)
        decay_b[h : h + 1, :] = jnp.full((1, LANES), decay_ref[h], F32)
    rate = jnp.concatenate([decay_b[...]] * (BLOCK // LANES), axis=1)

    def kept(k):
        return jnp.where(ids + k * BLOCK < limit, 1.0, 0.0).astype(F32)

    for k in range(blocks):
        raw = step_ref[:, span(k)]
        keep = kept(k)
        step = (jnp.maximum(raw, 0.0) + jnp.log1p(jnp.exp(-jnp.abs(raw)))) * keep
        sums = lax.dot_general(
            -(step * rate), tri.astype(F32), (((1,), (1,)), ((), ())),
            preferred_element_type=F32, precision=EXACT,
        )
        wi_t[:, span(k)] = sums
        dt_t[:, span(k)] = step
        tall = jnp.concatenate(
            [step, sums, jnp.broadcast_to(keep, (LANES - 2 * heads, BLOCK))], axis=0
        ).T
        for h in range(heads):
            wi_b[h, span(k), :] = jnp.broadcast_to(tall[:, heads + h : heads + h + 1], (BLOCK, LANES))
            dt_b[h, span(k), :] = jnp.broadcast_to(tall[:, h : h + 1], (BLOCK, LANES))
        mask_b[span(k), :] = jnp.broadcast_to(tall[:, 2 * heads : 2 * heads + 1], (BLOCK, LANES))

    def turn(v):
        return pltpu.roll(v, 64, 1)

    def slabs(ref, p):
        lo = ref[:, pl.ds(pl.multiple_of(p * LANES, LANES), LANES)].astype(F32)
        hi = ref[:, pl.ds(pl.multiple_of(half + p * LANES, LANES), LANES)].astype(F32)
        return lo, hi

    def join(lo, hi):
        return jnp.where(low, lo, turn(hi)), jnp.where(low, turn(lo), hi)

    def by_head(ref, g, k):
        return jnp.where(low, ref[g, span(k), :], ref[groups + g, span(k), :])

    def total(g, k):
        at = pl.ds((k + 1) * BLOCK - 1, 1)
        return jnp.where(low, wi_b[g, at, :], wi_b[groups + g, at, :])

    def hop_f(p):
        part = pl.ds(2 * p, 2)
        return pltpu.make_async_remote_copy(
            src_ref=state_out.at[part], dst_ref=state_in.at[part],
            send_sem=fs_sem.at[p], recv_sem=fr_sem.at[p],
            device_id={"seq": pos + 1}, device_id_type=pl.DeviceIdType.MESH,
        )

    def hop_b(p):
        part = pl.ds(2 * p, 2)
        return pltpu.make_async_remote_copy(
            src_ref=grad_out.at[part], dst_ref=grad_in.at[part],
            send_sem=bs_sem.at[p], recv_sem=br_sem.at[p],
            device_id={"seq": pos - 1}, device_id_type=pl.DeviceIdType.MESH,
        )

    def give(g, away):
        to = lax.rem(rank + away, ranks)
        return pltpu.make_async_remote_copy(
            src_ref=parts.at[g, :, pl.ds(pl.multiple_of(to * share, share), share), :],
            dst_ref=arrived.at[away - 1, g],
            send_sem=ps_sem.at[away - 1, g], recv_sem=pr_sem.at[away - 1, g],
            device_id={"head": to}, device_id_type=pl.DeviceIdType.MESH,
        )

    def piece(g, kind, owner):
        return parts.at[g, kind, pl.ds(pl.multiple_of(owner * share, share), share), :]

    def flip(bit):
        low_bit = lax.rem(rank, 2)
        if bit == 1:
            return rank + 1 - 2 * low_bit
        if bit == 2:
            return lax.rem(rank + 2, 4)
        return lax.rem(rank + 2, 4) + 1 - 2 * low_bit

    def first_hop(g, kind, which):
        to = flip(kind + 1)
        return pltpu.make_async_remote_copy(
            src_ref=piece(g, kind, to if which == 0 else flip(3)),
            dst_ref=arrived.at[which, g, kind],
            send_sem=ps_sem.at[2 * kind + which, g], recv_sem=pr_sem.at[2 * kind + which, g],
            device_id={"head": to}, device_id_type=pl.DeviceIdType.MESH,
        )

    def second_hop(g, kind):
        to = flip(2 - kind)
        return pltpu.make_async_remote_copy(
            src_ref=piece(g, kind, to), dst_ref=summed.at[g, kind],
            send_sem=ss_sem.at[kind, g], recv_sem=sr_sem.at[kind, g],
            device_id={"head": to}, device_id_type=pl.DeviceIdType.MESH,
        )

    square = ranks == 4

    def send_group(g):
        if square:
            for which in (1, 0):
                for kind in range(2):
                    first_hop(g, kind, which).start()
        else:
            for away in range(1, ranks):
                give(g, away).start()

    def forward_group(g):
        if square:
            for kind in range(2):
                first_hop(g, kind, 1).wait_recv()
                at = pl.ds(pl.multiple_of(flip(2 - kind) * share, share), share)
                parts[g, kind, at, :] += arrived[1, g, kind]
                second_hop(g, kind).start()

    def collect_group(g):
        own = pl.ds(pl.multiple_of(rank * share, share), share)
        for kind, out in enumerate((db_out, dc_out)):
            val = parts[g, kind, own, :]
            if square:
                first_hop(g, kind, 0).wait_recv()
                second_hop(g, kind).wait_recv()
                val = val + arrived[0, g, kind] + summed[g, kind]
            else:
                if kind == 0:
                    for away in range(1, ranks):
                        give(g, away).wait_recv()
                for away in range(1, ranks):
                    val = val + arrived[away - 1, g, kind]
            out[:, g, :] = val

    def settle_group(g):
        if square:
            for kind in range(2):
                for which in range(2):
                    first_hop(g, kind, which).wait_send()
                second_hop(g, kind).wait_send()
        else:
            for away in range(1, ranks):
                give(g, away).wait_send()

    def whole(g):
        return jnp.exp(prefix * (total(g, 0) + total(g, 1)))

    def pass_f(p):
        for j in range(2):
            g = 2 * p + j
            state_out[g] = whole(g) * state_in[g] + prefix * state[g]
        hop_f(p).start()

    def pass_b(p):
        for j in range(2):
            g = 2 * p + j
            grad_out[g] = whole(g) * grad_in[g] + grad_own[g]
        hop_b(p).start()

    @pl.when(pos == 0)
    def _():
        state_in[...] = jnp.zeros_like(state_in)

    @pl.when(pos == peers - 1)
    def _():
        grad_in[...] = jnp.zeros_like(grad_in)

    @pl.when(jnp.logical_or(pos == 0, pos == peers - 1))
    def _():
        pl.semaphore_wait(barrier, ranks)

    @pl.when(jnp.logical_and(pos > 0, pos < peers - 1))
    def _():
        pl.semaphore_wait(barrier, ranks + 1)

    def local_states(p, carry):
        xs = join(*slabs(x_ref, p))
        dys = join(*slabs(dy_ref, p))
        for j in range(2):
            g = 2 * p + j
            adds, backs = [], []
            for k in range(blocks):
                wi = by_head(wi_b, g, k)
                dt = by_head(dt_b, g, k)
                scaled = (xs[j][span(k)] * (dt * jnp.exp(total(g, k) - wi))).astype(BF16)
                adds.append(mm(b_ref[g, span(k), :], scaled, 0, 0))
                lifted = (dys[j][span(k)] * mask_b[span(k), :] * jnp.exp(wi)).astype(BF16)
                backs.append(mm(c_ref[g, span(k), :], lifted, 0, 0))
            first_state[g] = adds[0]
            state[g] = jnp.exp(total(g, 1)) * adds[0] + adds[1]
            later_grad[g] = backs[1]
            grad_own[g] = backs[0] + jnp.exp(total(g, 0)) * backs[1]

        @pl.when(pos == 0)
        def _():
            pass_f(p)

        @pl.when(pos == peers - 1)
        def _():
            pass_b(p)

        return carry

    lax.fori_loop(0, pairs, local_states, 0)

    def inside(p):
        xs = join(*slabs(x_ref, p))
        dys = join(*slabs(dy_ref, p))
        for j in range(2):
            g = 2 * p + j
            for k in range(blocks):
                b_blk = b_ref[g, span(k), :]
                c_blk = c_ref[g, span(k), :]
                scores = mm(c_blk, b_blk, 1, 1)
                x16 = xs[j][span(k)].astype(BF16)
                dyf = dys[j][span(k)] * mask_b[span(k), :]
                dy16 = dyf.astype(BF16)
                ys, dxs = [], []
                d_scores = None
                for m in range(2):
                    h = m * groups + g
                    col = wi_b[h, span(k), :]
                    col = jnp.concatenate([col, col], axis=1)
                    row = wi_t[pl.ds(h, 1), span(k)]
                    decay = jnp.where(tri, jnp.exp(jnp.minimum(col - row, 0.0)), 0.0)
                    decay = decay * dt_t[pl.ds(h, 1), span(k)]
                    weights = (scores * decay).astype(BF16)
                    mine = low if m == 0 else jnp.logical_not(low)
                    dy_m = jnp.where(mine, dyf, 0.0).astype(BF16)
                    d_weights = mm(dy_m, x16, 1, 1) * decay
                    d_scores = d_weights if d_scores is None else d_scores + d_weights
                    ys.append(mm(weights, x16, 1, 0))
                    dxs.append(mm(weights, dy16, 0, 0))
                y_acc[g, span(k), :] = jnp.where(low, ys[0], ys[1])
                dx_acc[g, span(k), :] = jnp.where(low, dxs[0], dxs[1])
                ds16 = d_scores.astype(BF16)
                parts[g, 1, span(k), :] = mm(ds16, b_blk, 1, 0)
                parts[g, 0, span(k), :] = mm(ds16, c_blk, 0, 0)

    q_acc[...] = jnp.zeros_like(q_acc)
    last = lax.broadcasted_iota(jnp.int32, (BLOCK, 1), 0) == BLOCK - 1
    pick_row = lax.broadcasted_iota(jnp.int32, (4 * LANES, LANES), 0)
    pick_col = lax.broadcasted_iota(jnp.int32, (4 * LANES, LANES), 1)
    pick_head = (
        jnp.where(pick_row % LANES >= 64, groups, 0) + jnp.where(pick_row >= 2 * LANES, heads, 0)
    )

    def across(p):
        @pl.when(pos == peers - 1)
        def _():
            hop_f(p).wait_recv()

        @pl.when(pos == 0)
        def _():
            hop_b(p).wait_recv()

        xs = join(*slabs(x_ref, p))
        dys = join(*slabs(dy_ref, p))
        y_parts, dx_parts = [], []
        for j in range(2):
            g = 2 * p + j
            pick = (pick_col == pick_head + g).astype(BF16)
            gain = jnp.where(low, gain_b[pl.ds(g, 1), :], gain_b[pl.ds(groups + g, 1), :])
            start = state_in[g]
            carry_grad = prefix * grad_in[g]
            entered = (start, jnp.exp(total(g, 0)) * start + first_state[g])
            leaving = (later_grad[g] + jnp.exp(total(g, 1)) * carry_grad, carry_grad)
            y_rows, dx_rows = [], []
            for k in range(blocks):
                wi = by_head(wi_b, g, k)
                dt = by_head(dt_b, g, k)
                end = total(g, k)
                up = jnp.exp(wi)
                down = dt * jnp.exp(end - wi)
                e16 = entered[k].astype(BF16)
                g16 = leaving[k].astype(BF16)
                x = xs[j][span(k)]
                mask = mask_b[span(k), :]
                dy = dys[j][span(k)] * mask
                b_blk = b_ref[g, span(k), :]
                c_blk = c_ref[g, span(k), :]
                y = y_acc[g, span(k), :] + up * mm(c_blk, e16, 1, 0)
                dx_s = down * mm(b_blk, g16, 1, 0)
                dx = dx_acc[g, span(k), :] + dx_s
                parts[g, 1, span(k), :] += mm((dy * up).astype(BF16), e16, 1, 1)
                parts[g, 0, span(k), :] += mm((x * down).astype(BF16), g16, 1, 1)
                q2 = x * dx
                extra = jnp.sum(x * dx_s, axis=0, keepdims=True) + jnp.exp(end) * jnp.sum(
                    leaving[k] * entered[k], axis=0, keepdims=True
                )
                q1 = dy * y - q2 + jnp.where(last, extra, 0.0)
                q1h = q1.astype(BF16)
                q2h = q2.astype(BF16)
                q1l = (q1 - q1h.astype(F32)).astype(BF16)
                q2l = (q2 - q2h.astype(F32)).astype(BF16)
                q_acc[span(k), :] += mm(jnp.concatenate([q1h, q1l, q2h, q2l], axis=1), pick, 1, 0)
                y_rows.append((y + gain * x) * mask)
                dx_rows.append(dx + gain * dy)
            send_group(g)
            y_parts.append(jnp.concatenate(y_rows, axis=0))
            dx_parts.append(jnp.concatenate(dx_rows, axis=0))
        for ref, pair in ((y_ref, y_parts), (dx_ref, dx_parts)):
            lo, hi = join(*pair)
            ref[:, pl.ds(pl.multiple_of(p * LANES, LANES), LANES)] = lo.astype(BF16)
            ref[:, pl.ds(pl.multiple_of(half + p * LANES, LANES), LANES)] = hi.astype(BF16)

    lag = max(1, peers - 3)
    middle = jnp.logical_and(pos > 0, pos < peers - 1)

    def stage(s, carry):
        pf = s - (pos - 1)
        pb = s - (peers - 2 - pos)

        @pl.when(jnp.logical_and(middle, jnp.logical_and(pf >= 0, pf < pairs)))
        def _():
            hop_f(pf).wait_recv()
            pass_f(pf)

        @pl.when(jnp.logical_and(middle, jnp.logical_and(pb >= 0, pb < pairs)))
        def _():
            hop_b(pb).wait_recv()
            pass_b(pb)

        @pl.when(s < pairs)
        def _():
            inside(s)

        @pl.when(jnp.logical_and(s >= lag, s < pairs + lag))
        def _():
            across(s - lag)

        @pl.when(jnp.logical_and(s > lag, s < pairs + lag))
        def _():
            for j in range(2):
                forward_group(2 * (s - lag - 1) + j)

        return carry

    lax.fori_loop(0, pairs + lag, stage, 0)
    for g in range(groups - 2, groups):
        forward_group(g)

    for k in range(blocks):
        q = q_acc[span(k), :].T
        step = dt_t[:, span(k)]
        d_log = lax.dot_general(
            q[:heads], tri.astype(F32), (((1,), (0,)), ((), ())),
            preferred_element_type=F32, precision=EXACT,
        )
        slope = jax.nn.sigmoid(step_ref[:, span(k)]) * kept(k)
        safe = jnp.where(step > 0.0, step, 1.0)
        gs_ref[:, span(k)] = slope * (q[heads : 2 * heads] / safe - rate * d_log)

    for g in range(groups):
        collect_group(g)
    for g in range(groups):
        settle_group(g)

    def finish(p, carry):
        @pl.when(pos < peers - 1)
        def _():
            hop_f(p).wait_send()

        @pl.when(pos > 0)
        def _():
            hop_b(p).wait_send()

        return carry

    lax.fori_loop(0, pairs, finish, 0)


def paired_kernel(
    peers, heads, groups,
    x_hbm, dy_hbm, b_hbm, c_hbm, step_ref, gain_ref, decay_ref, lengths_ref,
    y_hbm, dx_hbm, gs_ref, db_out, dc_out,
    x_ref, dy_ref, b_in, c_in, b_ref, c_ref, wide, wi_c, dt_c, wd_t, wd_f, xj, dyj,
    state, first_state, grad_own, later_grad, state_in, state_out, grad_in, grad_out,
    y_acc, dx_acc, q_acc, mask_b, gain_b, decay_b, parts, arrived, summed,
    in_sem, bc_sem, out_sem, xs_sem, xr_sem, ws_sem, wr_sem, fs_sem, fr_sem, bs_sem, br_sem, ps_sem, pr_sem, ss_sem, sr_sem,
):
    ranks = 4
    pos = lax.axis_index("seq")
    rank = lax.axis_index("head")
    bit_x = lax.rem(rank, 2)
    bit_y = rank // 2
    prefix = jnp.where(pos < PREFIX_DEVS, 1.0, 0.0).astype(F32)
    rows = x_ref.shape[0]
    blocks = rows // BLOCK
    pairs = groups // 2
    share = rows // ranks
    zero_unit = groups + pairs
    low = lax.broadcasted_iota(jnp.int32, (1, LANES), 1) < 64
    mesh_id = pl.DeviceIdType.MESH

    def bit(par):
        return (1 - par) * bit_x + par * bit_y

    def beside(par):
        return rank + (1 - par) * (1 - 2 * bit_x) + 2 * par * (1 - 2 * bit_y)

    def mine(p):
        return 2 * p + bit(p % 2)

    def given(p):
        return 2 * p + 1 - bit(p % 2)

    def slab(i):
        return pl.ds(pl.multiple_of(i * LANES, LANES), LANES)

    def fetch(i, which):
        src, dst = ((x_hbm, x_ref), (dy_hbm, dy_ref))[which]
        return pltpu.make_async_copy(src.at[:, slab(i)], dst.at[:, slab(i)], in_sem.at[which, i])

    def fetch_proj(which):
        src, dst = ((b_hbm, b_in), (c_hbm, c_in))[which]
        return pltpu.make_async_copy(src, dst, bc_sem.at[which])

    def leave(i, which):
        src, dst = ((x_ref, y_hbm), (dy_ref, dx_hbm))[which]
        return pltpu.make_async_copy(src.at[:, slab(i)], dst.at[:, slab(i)], out_sem.at[which, i])

    for p in range(pairs):
        for which in range(2):
            for i in (p, pairs + p):
                fetch(i, which).start()
    for which in range(2):
        fetch_proj(which).start()

    barrier = pltpu.get_barrier_semaphore()
    for par in range(2):
        pl.semaphore_signal(barrier, inc=1, device_id={"head": beside(par)}, device_id_type=mesh_id)

    @pl.when(pos > 0)
    def _():
        pl.semaphore_signal(barrier, inc=1, device_id={"seq": pos - 1}, device_id_type=mesh_id)

    @pl.when(pos < peers - 1)
    def _():
        pl.semaphore_signal(barrier, inc=1, device_id={"seq": pos + 1}, device_id_type=mesh_id)

    def span(k):
        return slice(k * BLOCK, (k + 1) * BLOCK)

    tri = lax.broadcasted_iota(jnp.int32, (BLOCK, BLOCK), 0) >= lax.broadcasted_iota(
        jnp.int32, (BLOCK, BLOCK), 1
    )
    limit = jnp.where(pos < PREFIX_DEVS, rows, lengths_ref[jnp.maximum(pos - PREFIX_DEVS, 0)])
    ids = lax.broadcasted_iota(jnp.int32, (1, BLOCK), 1)
    tall_ids = lax.broadcasted_iota(jnp.int32, (BLOCK, LANES), 0)

    def kept(k):
        return jnp.where(ids + k * BLOCK < limit, 1.0, 0.0).astype(F32)

    def turn(v):
        return pltpu.roll(v, 64, 1)

    def join(lo, hi):
        return jnp.where(low, lo, turn(hi)), jnp.where(low, turn(lo), hi)

    def copy_of(src, dst, send, recv, where):
        return pltpu.make_async_remote_copy(
            src_ref=src, dst_ref=dst, send_sem=send, recv_sem=recv, device_id=where, device_id_type=mesh_id
        )

    def raw(p, which):
        ref = (xj, dyj)[which]
        return copy_of(
            ref.at[given(p)], ref.at[groups + p], xs_sem.at[which, p], xr_sem.at[which, p], {"head": beside(p % 2)}
        )

    def tell(par):
        return copy_of(wd_t, wd_f.at[par], ws_sem.at[par], wr_sem.at[par], {"head": beside(par)})

    def hop_f(u):
        return copy_of(state_out.at[u], state_in.at[u], fs_sem.at[u], fr_sem.at[u], {"seq": pos + 1})

    def hop_b(u):
        return copy_of(grad_out.at[u], grad_in.at[u], bs_sem.at[u], br_sem.at[u], {"seq": pos - 1})

    def piece(p, kind, owner):
        return parts.at[p, kind, pl.ds(pl.multiple_of(owner * share, share), share), :]

    def first_hop(p, kind, which):
        par = p % 2
        to = beside(1 - par)
        opposite = 3 - rank
        return copy_of(
            piece(p, kind, to if which == 0 else opposite), arrived.at[which, p, kind],
            ps_sem.at[which, p, kind], pr_sem.at[which, p, kind], {"head": to},
        )

    def second_hop(p, kind):
        to = beside(p % 2)
        return copy_of(
            piece(p, kind, to), summed.at[p, kind], ss_sem.at[p, kind], sr_sem.at[p, kind], {"head": to}
        )

    for k in range(blocks):
        mask_b[span(k), :] = jnp.where(tall_ids + k * BLOCK < limit, 1.0, 0.0).astype(F32)

    def spread(p):
        for which in range(2):
            for i in (p, pairs + p):
                fetch(i, which).wait()
        at_lo, at_hi = slab(p), slab(pairs + p)
        xj[2 * p], xj[2 * p + 1] = join(x_ref[:, at_lo].astype(F32), x_ref[:, at_hi].astype(F32))
        mask = mask_b[...]
        dyj[2 * p], dyj[2 * p + 1] = join(dy_ref[:, at_lo].astype(F32) * mask, dy_ref[:, at_hi].astype(F32) * mask)

    for p in range(2):
        spread(p)

    @pl.when(jnp.logical_or(pos == 0, pos == peers - 1))
    def _():
        pl.semaphore_wait(barrier, 3)

    @pl.when(jnp.logical_and(pos > 0, pos < peers - 1))
    def _():
        pl.semaphore_wait(barrier, 4)

    for which in range(2):
        for p in range(2):
            raw(p, which).start()

    for h in range(heads):
        gain_b[h : h + 1, :] = jnp.full((1, LANES), gain_ref[h], F32)
        decay_b[h : h + 1, :] = jnp.full((1, LANES), decay_ref[h], F32)
    rate = jnp.concatenate([decay_b[...]] * (BLOCK // LANES), axis=1)
    for k in range(blocks):
        step_in = step_ref[:, span(k)]
        step = (jnp.maximum(step_in, 0.0) + jnp.log1p(jnp.exp(-jnp.abs(step_in)))) * kept(k)
        sums = lax.dot_general(
            -(step * rate), tri.astype(F32), (((1,), (1,)), ((), ())),
            preferred_element_type=F32, precision=EXACT,
        )
        wd_t[0, :, span(k)] = sums
        wd_t[1, :, span(k)] = step
    for par in range(2):
        tell(par).start()
    for p in range(2, pairs):
        spread(p)
        for which in range(2):
            raw(p, which).start()
    state_in[zero_unit] = jnp.zeros_like(state_in[zero_unit])
    grad_in[zero_unit] = jnp.zeros_like(grad_in[zero_unit])

    def loop(start, stop, body):
        def step(i, carry):
            body(i)
            return carry

        lax.fori_loop(start, stop, step, 0)

    def columns(src, u, g):
        for kind, ref in ((0, wi_c), (1, dt_c)):
            for k in range(blocks):
                cols = [
                    jnp.broadcast_to(src(kind, pl.ds(m * groups + g, 1), span(k)), (64, BLOCK)) for m in range(2)
                ]
                ref[u, span(k), :] = jnp.concatenate(cols, axis=0).T

    chunk = rows // ranks
    for which in range(2):
        fetch_proj(which).wait()

    def group_first(i):
        at = pl.ds(pl.multiple_of(i * chunk, chunk), chunk)
        for src, dst in ((b_in, b_ref), (c_in, c_ref)):
            flat = src[at].astype(F32).reshape(chunk * groups, src.shape[2])
            for n in range(src.shape[2] // LANES):
                cut = slice(n * LANES, (n + 1) * LANES)
                wide[n] = flat[:, cut]
                for g in range(groups):
                    dst[g, at, cut] = wide[n, pl.ds(g, chunk, stride=groups), :].astype(BF16)

    loop(0, ranks, group_first)
    loop(0, groups, lambda g: columns(lambda kind, at, cut: wd_t[kind, at, cut], g, g))

    class Part:
        def __init__(self, unit, group):
            self.unit, self.group = unit, group

        def x(self, k):
            return xj[self.unit, span(k), :]

        def dy(self, k):
            return dyj[self.unit, span(k), :]

        def within(self, k):
            return wi_c[self.unit, span(k), :]

        def step(self, k):
            return dt_c[self.unit, span(k), :]

        def total(self, k):
            return wi_c[self.unit, pl.ds((k + 1) * BLOCK - 1, 1), :]

    def own_part(g):
        return Part(g, g)

    def handed_part(p):
        return Part(groups + p, mine(p))

    def whole(part):
        return jnp.exp(prefix * (part.total(0) + part.total(1)))

    def start_of(u):
        return state_in[jnp.where(pos > 0, u, zero_unit)]

    def carry_of(u):
        return grad_in[jnp.where(pos < PREFIX_DEVS, u, zero_unit)]

    def entered_by(part):
        start = start_of(part.unit)
        return start, jnp.exp(part.total(0)) * start + first_state[part.unit]

    def leaving_by(part):
        carry = carry_of(part.unit)
        return later_grad[part.unit] + jnp.exp(part.total(1)) * carry, carry

    def pass_f(part):
        u = part.unit
        state_out[u] = whole(part) * start_of(u) + prefix * state[u]
        hop_f(u).start()

    def pass_b(part):
        u = part.unit
        held = grad_in[jnp.where(pos < peers - 1, u, zero_unit)]
        grad_out[u] = whole(part) * held + grad_own[u]
        hop_b(u).start()

    def emit(part):
        @pl.when(pos == 0)
        def _():
            pass_f(part)

        @pl.when(pos == peers - 1)
        def _():
            pass_b(part)

    def relay_f(part):
        @pl.when(pos > 0)
        def _():
            hop_f(part.unit).wait_recv()

        @pl.when(jnp.logical_and(pos > 0, pos < peers - 1))
        def _():
            pass_f(part)

    def relay_b(part):
        @pl.when(pos < peers - 1)
        def _():
            hop_b(part.unit).wait_recv()

        @pl.when(jnp.logical_and(pos > 0, pos < peers - 1))
        def _():
            pass_b(part)

    def relay(i, how):
        @pl.when(jnp.logical_and(i >= 0, i < pairs))
        def _():
            how(own_part(mine(i)))

        r = i - pairs
        p = 2 * (r // 4) + r % 2

        @pl.when(jnp.logical_and(jnp.logical_and(r >= 0, r < 2 * pairs), r % 4 < 2))
        def _():
            how(handed_part(p))

        @pl.when(jnp.logical_and(jnp.logical_and(r >= 0, r < 2 * pairs), r % 4 >= 2))
        def _():
            how(own_part(given(p)))

    def serve(slot):
        relay(slot + LAG - LAG * pos, relay_f)
        relay(slot + LAG - LAG * (peers - 1 - pos), relay_b)

    def local_states(part):
        u, g = part.unit, part.group
        adds, backs = [], []
        for k in range(blocks):
            wi = part.within(k)
            scaled = (part.x(k) * (part.step(k) * jnp.exp(part.total(k) - wi))).astype(BF16)
            adds.append(mm(b_ref[g, span(k), :], scaled, 0, 0))
            lifted = (part.dy(k) * jnp.exp(wi)).astype(BF16)
            backs.append(mm(c_ref[g, span(k), :], lifted, 0, 0))
        first_state[u] = adds[0]
        state[u] = jnp.exp(part.total(1)) * adds[0] + adds[1]
        later_grad[u] = backs[1]
        grad_own[u] = backs[0] + jnp.exp(part.total(0)) * backs[1]

    def decay_by(row, dt_row):
        col = jnp.broadcast_to(row, (LANES, BLOCK)).T
        col = jnp.concatenate([col, col], axis=1)
        return jnp.where(tri, jnp.exp(jnp.minimum(col - row, 0.0)), 0.0) * dt_row

    def only(m, v):
        return jnp.where(low if m == 0 else jnp.logical_not(low), v, 0.0).astype(BF16)

    def inside(p, g, with_scores):
        for k in range(blocks):
            scores = mm(c_ref[g, span(k), :], b_ref[g, span(k), :], 1, 1)
            x16 = xj[g, span(k), :].astype(BF16)
            dyf = dyj[g, span(k), :]
            dy16 = dyf.astype(BF16)
            ys, dxs, d_scores = [], [], None
            for m in range(2):
                h = m * groups + g
                decay = decay_by(wd_t[0, pl.ds(h, 1), span(k)], wd_t[1, pl.ds(h, 1), span(k)])
                weights = (scores * decay).astype(BF16)
                if with_scores:
                    d_weights = mm(only(m, dyf), x16, 1, 1) * decay
                    d_scores = d_weights if d_scores is None else d_scores + d_weights
                ys.append(mm(weights, x16, 1, 0))
                dxs.append(mm(weights, dy16, 0, 0))
            y_acc[g, span(k), :] = jnp.where(low, ys[0], ys[1])
            dx_acc[g, span(k), :] = jnp.where(low, dxs[0], dxs[1])
            if with_scores:
                parts[p, 0, span(k), :] = d_scores

    def handed_scores(p):
        g = mine(p)
        for k in range(blocks):
            x16 = xj[groups + p, span(k), :].astype(BF16)
            dyf = dyj[groups + p, span(k), :]
            d_scores = parts[p, 0, span(k), :]
            for m in range(2):
                at = pl.ds(m * groups + g, 1)
                decay = decay_by(wd_f[p % 2, 0, at, span(k)], wd_f[p % 2, 1, at, span(k)])
                d_scores = d_scores + mm(only(m, dyf), x16, 1, 1) * decay
            ds16 = d_scores.astype(BF16)
            parts[p, 1, span(k), :] = mm(ds16, b_ref[g, span(k), :], 1, 0)
            parts[p, 0, span(k), :] = mm(ds16, c_ref[g, span(k), :], 0, 0)

    def grow_c(p):
        both = (own_part(mine(p)), handed_part(p))
        entered = [entered_by(part) for part in both]
        for k in range(blocks):
            e16 = jnp.concatenate([e[k].astype(BF16) for e in entered], axis=1)
            lifted = jnp.concatenate(
                [(part.dy(k) * jnp.exp(part.within(k))).astype(BF16) for part in both], axis=1
            )
            parts[p, 1, span(k), :] += mm(lifted, e16, 1, 1)

    def grow_b(p):
        both = (own_part(mine(p)), handed_part(p))
        leaving = [leaving_by(part) for part in both]
        for k in range(blocks):
            g16 = jnp.concatenate([v[k].astype(BF16) for v in leaving], axis=1)
            scaled = jnp.concatenate(
                [
                    (part.x(k) * (part.step(k) * jnp.exp(part.total(k) - part.within(k)))).astype(BF16)
                    for part in both
                ],
                axis=1,
            )
            parts[p, 0, span(k), :] += mm(scaled, g16, 1, 1)

    early_kind = jnp.where(pos < PREFIX_DEVS, 1, 0)
    late_kind = 1 - early_kind

    def send(p, kind):
        for which in (1, 0):
            first_hop(p, kind, which).start()

    def early(p):
        @pl.when(pos < PREFIX_DEVS)
        def _():
            grow_c(p)

        @pl.when(pos >= PREFIX_DEVS)
        def _():
            grow_b(p)

        send(p, early_kind)

    def late(p):
        @pl.when(pos < PREFIX_DEVS)
        def _():
            grow_b(p)

        @pl.when(pos >= PREFIX_DEVS)
        def _():
            grow_c(p)

        send(p, late_kind)

    def forward(p, kind):
        first_hop(p, kind, 1).wait_recv()
        at = pl.ds(pl.multiple_of(beside(p % 2) * share, share), share)
        parts[p, kind, at, :] += arrived[1, p, kind]
        second_hop(p, kind).start()

    def receive(p):
        for which in range(2):
            raw(p, which).wait_recv()
        columns(lambda kind, at, cut: wd_f[p % 2, kind, at, cut], groups + p, mine(p))
        part = handed_part(p)
        local_states(part)
        emit(part)
        handed_scores(p)

    last = lax.broadcasted_iota(jnp.int32, (BLOCK, 1), 0) == BLOCK - 1
    pick_row = lax.broadcasted_iota(jnp.int32, (4 * LANES, LANES), 0)
    pick_col = lax.broadcasted_iota(jnp.int32, (4 * LANES, LANES), 1)
    pick_head = (
        jnp.where(pick_row % LANES >= 64, groups, 0) + jnp.where(pick_row >= 2 * LANES, heads, 0)
    )

    def across(p):
        y_parts, dx_parts = [], []
        for j in range(2):
            g = 2 * p + j
            part = own_part(g)
            pick = (pick_col == pick_head + g).astype(BF16)
            gain = jnp.where(low, gain_b[pl.ds(g, 1), :], gain_b[pl.ds(groups + g, 1), :])
            entered = entered_by(part)
            leaving = leaving_by(part)
            y_rows, dx_rows = [], []
            for k in range(blocks):
                wi = part.within(k)
                end = part.total(k)
                up = jnp.exp(wi)
                down = part.step(k) * jnp.exp(end - wi)
                x = part.x(k)
                dy = part.dy(k)
                y = y_acc[g, span(k), :] + up * mm(c_ref[g, span(k), :], entered[k].astype(BF16), 1, 0)
                dx_s = down * mm(b_ref[g, span(k), :], leaving[k].astype(BF16), 1, 0)
                dx = dx_acc[g, span(k), :] + dx_s
                q2 = x * dx
                extra = jnp.sum(x * dx_s, axis=0, keepdims=True) + jnp.exp(end) * jnp.sum(
                    leaving[k] * entered[k], axis=0, keepdims=True
                )
                q1 = dy * y - q2 + jnp.where(last, extra, 0.0)
                q1h = q1.astype(BF16)
                q2h = q2.astype(BF16)
                q1l = (q1 - q1h.astype(F32)).astype(BF16)
                q2l = (q2 - q2h.astype(F32)).astype(BF16)
                q_acc[span(k), :] += mm(jnp.concatenate([q1h, q1l, q2h, q2l], axis=1), pick, 1, 0)
                y_rows.append((y + gain * x) * mask_b[span(k), :])
                dx_rows.append(dx + gain * dy)
            y_parts.append(jnp.concatenate(y_rows, axis=0))
            dx_parts.append(jnp.concatenate(dx_rows, axis=0))
        for which, (ref, pair) in enumerate(((x_ref, y_parts), (dy_ref, dx_parts))):
            lo, hi = join(*pair)
            ref[:, slab(p)] = lo.astype(BF16)
            ref[:, slab(pairs + p)] = hi.astype(BF16)
            for i in (p, pairs + p):
                leave(i, which).start()

    def begin(p):
        for j in range(2):
            local_states(own_part(2 * p + j))
        emit(own_part(mine(p)))

    def within_blocks(p):
        inside(p, mine(p), True)
        inside(p, given(p), False)
        serve(p)

    q_acc[...] = jnp.zeros_like(q_acc)
    loop(0, pairs, begin)
    loop(0, pairs, within_blocks)
    for par in range(2):
        tell(par).wait_recv()

    def in_turn(t):
        @pl.when(t > 0)
        def _():
            loop(6, 8, serve)

        loop(2 * t, 2 * t + 2, receive)
        loop(2 * t, 2 * t + 2, lambda p: emit(own_part(given(p))))

        def ahead(p):
            serve(4 + 2 * t + p)
            early(p)

        loop(2 * t, 2 * t + 2, ahead)

    loop(0, pairs // 2, in_turn)
    loop(0, 2, late)
    loop(0, 2, lambda p: forward(p, early_kind))
    loop(10, 12, serve)
    loop(0, 2, across)
    loop(2, 4, lambda p: forward(p, early_kind))
    loop(12, 14, serve)
    loop(2, 4, late)
    loop(0, 2, lambda p: forward(p, late_kind))
    loop(14, 16, serve)
    loop(2, 4, across)
    loop(2, 4, lambda p: forward(p, late_kind))

    for k in range(blocks):
        q = q_acc[span(k), :].T
        step = wd_t[1, :, span(k)]
        d_log = lax.dot_general(
            q[:heads], tri.astype(F32), (((1,), (0,)), ((), ())),
            preferred_element_type=F32, precision=EXACT,
        )
        slope = jax.nn.sigmoid(step_ref[:, span(k)]) * kept(k)
        safe = jnp.where(step > 0.0, step, 1.0)
        gs_ref[:, span(k)] = slope * (q[heads : 2 * heads] / safe - rate * d_log)

    own = pl.ds(pl.multiple_of(rank * share, share), share)
    for late_turn in range(2):
        for p in range(pairs):
            kind = late_kind if late_turn else early_kind
            first_hop(p, kind, 0).wait_recv()
            second_hop(p, kind).wait_recv()
    for p in range(pairs):
        for kind, out in enumerate((db_out, dc_out)):
            kept_sum = parts[p, kind, own, :] + arrived[0, p, kind]
            other = summed[p, kind]
            first = bit(p % 2) == 0
            out[:, 2 * p, :] = jnp.where(first, kept_sum, other)
            out[:, 2 * p + 1, :] = jnp.where(first, other, kept_sum)

    for par in range(2):
        tell(par).wait_send()
    for which in range(2):
        for i in range(2 * pairs):
            leave(i, which).wait()

    def settle(p):
        for kind in range(2):
            raw(p, kind).wait_send()
            for which in range(2):
                first_hop(p, kind, which).wait_send()
            second_hop(p, kind).wait_send()

    loop(0, pairs, settle)

    def finish(u):
        @pl.when(pos < peers - 1)
        def _():
            hop_f(u).wait_send()

        @pl.when(pos > 0)
        def _():
            hop_b(u).wait_send()

    loop(0, groups + pairs, finish)


def writing_kernel(pieces, count, *refs):
    sources, targets, held = refs[:count], refs[count : 2 * count], refs[2 * count : 3 * count]
    in_sem, out_sem = refs[3 * count :]
    arrive, leave = [], []
    for i in range(count):
        for n in range(pieces):
            part = held[i].shape[0] // pieces
            at = pl.ds(n * part, part)
            arrive.append(pltpu.make_async_copy(sources[i].at[at], held[i].at[at], in_sem.at[i, n]))
            leave.append(pltpu.make_async_copy(held[i].at[at], targets[i].at[at], out_sem.at[i, n]))
    for copy in arrive:
        copy.start()
    for copy, onward in zip(arrive, leave):
        copy.wait()
        onward.start()
    for copy in leave:
        copy.wait()


def write_out(values, pieces):
    anywhere = pl.BlockSpec(memory_space=pl.ANY)
    sems = pltpu.SemaphoreType.DMA((len(values), pieces))
    return pl.pallas_call(
        functools.partial(writing_kernel, pieces, len(values)),
        out_shape=tuple(jax.ShapeDtypeStruct(v.shape, v.dtype) for v in values),
        in_specs=[anywhere] * len(values),
        out_specs=(anywhere,) * len(values),
        scratch_shapes=[pltpu.VMEM(v.shape, v.dtype) for v in values] + [sems, sems],
        compiler_params=pltpu.CompilerParams(vmem_limit_bytes=56 * 1024 * 1024),
    )(*values)


def on_device(inputs, step_raw, decay_rate, skip_gain, b_proj, c_proj, lengths, cotangent):
    rows, width = inputs.shape
    heads = decay_rate.shape[0]
    groups, states = b_proj.shape[1:]
    peers = lax.axis_size("seq")
    ranks = lax.axis_size("head")
    hops = 2 if ranks == 4 else ranks - 1
    vmem = pl.BlockSpec(memory_space=pltpu.VMEM)
    smem = pl.BlockSpec(memory_space=pltpu.SMEM)
    carry = pltpu.VMEM((groups, states, LANES), F32)
    dma = pltpu.SemaphoreType.DMA((groups // 2,))

    if ranks == 4 and peers == 4:
        pairs = groups // 2
        units = pltpu.VMEM((groups + pairs, states, LANES), F32)
        arriving = pltpu.VMEM((groups + pairs + 1, states, LANES), F32)
        per_group = pltpu.VMEM((groups, rows, LANES), F32)
        per_unit = pltpu.VMEM((groups + pairs, rows, LANES), F32)
        wide_rows = pltpu.VMEM((rows, width), BF16)
        proj = pltpu.VMEM((rows, groups, states), BF16)
        lead = pltpu.VMEM((groups, rows, states), BF16)
        hop = pltpu.SemaphoreType.DMA((groups + pairs,))
        kernel = functools.partial(paired_kernel, peers, heads, groups)
        operands = (b_proj, c_proj)
        big = pl.BlockSpec(memory_space=pl.ANY)
        scratch = [
            wide_rows, wide_rows, proj, proj, lead, lead,
            pltpu.VMEM((states // LANES, rows // ranks * groups, LANES), F32),
            per_unit, per_unit,
            pltpu.VMEM((2, heads, rows), F32),
            pltpu.VMEM((2, 2, heads, rows), F32),
            per_unit, per_unit,
            units, units, units, units, arriving, units, arriving, units,
            per_group, per_group,
            pltpu.VMEM((rows, LANES), F32),
            pltpu.VMEM((rows, LANES), F32),
            pltpu.VMEM((heads, LANES), F32),
            pltpu.VMEM((heads, LANES), F32),
            pltpu.VMEM((pairs, 2, rows, states), F32),
            pltpu.VMEM((2, pairs, 2, rows // ranks, states), F32),
            pltpu.VMEM((pairs, 2, rows // ranks, states), F32),
            pltpu.SemaphoreType.DMA((2, groups)),
            pltpu.SemaphoreType.DMA((2,)),
            pltpu.SemaphoreType.DMA((2, groups)),
            pltpu.SemaphoreType.DMA((2, pairs)),
            pltpu.SemaphoreType.DMA((2, pairs)),
            pltpu.SemaphoreType.DMA((2,)),
            pltpu.SemaphoreType.DMA((2,)),
            hop, hop, hop, hop,
            pltpu.SemaphoreType.DMA((2, pairs, 2)),
            pltpu.SemaphoreType.DMA((2, pairs, 2)),
            pltpu.SemaphoreType.DMA((pairs, 2)),
            pltpu.SemaphoreType.DMA((pairs, 2)),
        ]
    else:
        kernel = functools.partial(layer_kernel, peers, ranks, heads, groups)
        operands = (jnp.swapaxes(b_proj, 0, 1), jnp.swapaxes(c_proj, 0, 1))
        big = vmem
        scratch = [
            pltpu.VMEM((heads, rows, LANES), F32),
            pltpu.VMEM((heads, rows, LANES), F32),
            pltpu.VMEM((heads, rows), F32),
            pltpu.VMEM((heads, rows), F32),
            carry, carry, carry, carry, carry, carry, carry, carry,
            pltpu.VMEM((groups, rows, LANES), F32),
            pltpu.VMEM((groups, rows, LANES), F32),
            pltpu.VMEM((rows, LANES), F32),
            pltpu.VMEM((rows, LANES), F32),
            pltpu.VMEM((heads, LANES), F32),
            pltpu.VMEM((heads, LANES), F32),
            pltpu.VMEM((groups, 2, rows, states), F32),
            pltpu.VMEM((hops, groups, 2, rows // ranks, states), F32),
            pltpu.VMEM((groups, 2, rows // ranks, states), F32),
            dma, dma, dma, dma,
            pltpu.SemaphoreType.DMA((max(ranks - 1, 4), groups)),
            pltpu.SemaphoreType.DMA((max(ranks - 1, 4), groups)),
            pltpu.SemaphoreType.DMA((2, groups)),
            pltpu.SemaphoreType.DMA((2, groups)),
        ]

    y, dx, gs, db, dc = pl.pallas_call(
        kernel,
        out_shape=(
            jax.ShapeDtypeStruct((rows, width), BF16),
            jax.ShapeDtypeStruct((rows, width), BF16),
            jax.ShapeDtypeStruct((heads, rows), F32),
            jax.ShapeDtypeStruct((rows // ranks, groups, states), F32),
            jax.ShapeDtypeStruct((rows // ranks, groups, states), F32),
        ),
        in_specs=[big] * 4 + [vmem] + [smem] * 3,
        out_specs=(big, big, vmem, vmem, vmem),
        scratch_shapes=scratch,
        compiler_params=pltpu.CompilerParams(
            collective_id=0, has_side_effects=True, vmem_limit_bytes=56 * 1024 * 1024
        ),
    )(
        inputs, cotangent, *operands, step_raw.T, skip_gain, decay_rate, lengths
    )
    if ranks == 4 and peers == 4:
        y, dx, gs, db, dc = write_out((y, dx, gs, db, dc), 2)
    return (y, dx, gs.T, db, dc)


def solution(mesh):
    rows = P(("dp", "seq"), "head")
    proj = P(("dp", "seq"), None, None)
    grads = P(("dp", "seq", "head"), None, None)
    return jax.shard_map(
        on_device,
        mesh=mesh,
        in_specs=(rows, rows, P("head"), P("head"), proj, proj, P("dp"), rows),
        out_specs=(rows, rows, rows, grads, grads),
        check_vma=False,
    )
```

```python
import functools

import jax
import jax.numpy as jnp
from jax import lax
from jax.experimental import pallas as pl
from jax.experimental.pallas import tpu as pltpu
from jax.sharding import PartitionSpec as P

BLOCK = 256
PREFIX_DEVS = 2
LANES = 128
PAIRS = 4
F32 = jnp.float32
BF16 = jnp.bfloat16
EXACT = lax.Precision.HIGHEST


def mm(a, b, ca, cb):
    return lax.dot_general(a, b, (((ca,), (cb,)), ((), ())), preferred_element_type=F32)


def layer_kernel(
    peers, ranks, heads, groups,
    x_ref, dy_ref, b_ref, c_ref, step_ref, gain_ref, decay_ref, lengths_ref,
    y_ref, dx_ref, gs_ref, db_out, dc_out,
    wi_b, dt_b, wi_t, dt_t, state, first_state, grad_own, later_grad,
    state_in, state_out, grad_in, grad_out, y_acc, dx_acc, q_acc, mask_b, gain_b, decay_b,
    parts, arrived, summed, fs_sem, fr_sem, bs_sem, br_sem, ps_sem, pr_sem, ss_sem, sr_sem,
):
    pos = lax.axis_index("seq")
    rank = lax.axis_index("head")
    prefix = jnp.where(pos < PREFIX_DEVS, 1.0, 0.0).astype(F32)
    rows = x_ref.shape[0]
    blocks = rows // BLOCK
    pairs = groups // 2
    half = groups * 64
    low = lax.broadcasted_iota(jnp.int32, (1, LANES), 1) < 64

    share = rows // ranks
    barrier = pltpu.get_barrier_semaphore()
    for away in range(1, ranks):
        pl.semaphore_signal(
            barrier, inc=1, device_id={"head": lax.rem(rank + away, ranks)},
            device_id_type=pl.DeviceIdType.MESH,
        )

    @pl.when(pos > 0)
    def _():
        pl.semaphore_signal(barrier, inc=1, device_id={"seq": pos - 1}, device_id_type=pl.DeviceIdType.MESH)

    @pl.when(pos < peers - 1)
    def _():
        pl.semaphore_signal(barrier, inc=1, device_id={"seq": pos + 1}, device_id_type=pl.DeviceIdType.MESH)

    tri = lax.broadcasted_iota(jnp.int32, (BLOCK, BLOCK), 0) >= lax.broadcasted_iota(
        jnp.int32, (BLOCK, BLOCK), 1
    )

    def span(k):
        return slice(k * BLOCK, (k + 1) * BLOCK)

    limit = jnp.where(pos < PREFIX_DEVS, rows, lengths_ref[jnp.maximum(pos - PREFIX_DEVS, 0)])
    ids = lax.broadcasted_iota(jnp.int32, (1, BLOCK), 1)
    for h in range(heads):
        gain_b[h : h + 1, :] = jnp.full((1, LANES), gain_ref[h], F32)
        decay_b[h : h + 1, :] = jnp.full((1, LANES), decay_ref[h], F32)
    rate = jnp.concatenate([decay_b[...]] * (BLOCK // LANES), axis=1)

    def kept(k):
        return jnp.where(ids + k * BLOCK < limit, 1.0, 0.0).astype(F32)

    for k in range(blocks):
        raw = step_ref[:, span(k)]
        keep = kept(k)
        step = (jnp.maximum(raw, 0.0) + jnp.log1p(jnp.exp(-jnp.abs(raw)))) * keep
        sums = lax.dot_general(
            -(step * rate), tri.astype(F32), (((1,), (1,)), ((), ())),
            preferred_element_type=F32, precision=EXACT,
        )
        wi_t[:, span(k)] = sums
        dt_t[:, span(k)] = step
        tall = jnp.concatenate(
            [step, sums, jnp.broadcast_to(keep, (LANES - 2 * heads, BLOCK))], axis=0
        ).T
        for h in range(heads):
            wi_b[h, span(k), :] = jnp.broadcast_to(tall[:, heads + h : heads + h + 1], (BLOCK, LANES))
            dt_b[h, span(k), :] = jnp.broadcast_to(tall[:, h : h + 1], (BLOCK, LANES))
        mask_b[span(k), :] = jnp.broadcast_to(tall[:, 2 * heads : 2 * heads + 1], (BLOCK, LANES))

    def turn(v):
        return pltpu.roll(v, 64, 1)

    def slabs(ref, p):
        lo = ref[:, pl.ds(pl.multiple_of(p * LANES, LANES), LANES)].astype(F32)
        hi = ref[:, pl.ds(pl.multiple_of(half + p * LANES, LANES), LANES)].astype(F32)
        return lo, hi

    def join(lo, hi):
        return jnp.where(low, lo, turn(hi)), jnp.where(low, turn(lo), hi)

    def by_head(ref, g, k):
        return jnp.where(low, ref[g, span(k), :], ref[groups + g, span(k), :])

    def total(g, k):
        at = pl.ds((k + 1) * BLOCK - 1, 1)
        return jnp.where(low, wi_b[g, at, :], wi_b[groups + g, at, :])

    def hop_f(p):
        part = pl.ds(2 * p, 2)
        return pltpu.make_async_remote_copy(
            src_ref=state_out.at[part], dst_ref=state_in.at[part],
            send_sem=fs_sem.at[p], recv_sem=fr_sem.at[p],
            device_id={"seq": pos + 1}, device_id_type=pl.DeviceIdType.MESH,
        )

    def hop_b(p):
        part = pl.ds(2 * p, 2)
        return pltpu.make_async_remote_copy(
            src_ref=grad_out.at[part], dst_ref=grad_in.at[part],
            send_sem=bs_sem.at[p], recv_sem=br_sem.at[p],
            device_id={"seq": pos - 1}, device_id_type=pl.DeviceIdType.MESH,
        )

    def give(g, away):
        to = lax.rem(rank + away, ranks)
        return pltpu.make_async_remote_copy(
            src_ref=parts.at[g, :, pl.ds(pl.multiple_of(to * share, share), share), :],
            dst_ref=arrived.at[away - 1, g],
            send_sem=ps_sem.at[away - 1, g], recv_sem=pr_sem.at[away - 1, g],
            device_id={"head": to}, device_id_type=pl.DeviceIdType.MESH,
        )

    def piece(g, kind, owner):
        return parts.at[g, kind, pl.ds(pl.multiple_of(owner * share, share), share), :]

    def flip(bit):
        low_bit = lax.rem(rank, 2)
        if bit == 1:
            return rank + 1 - 2 * low_bit
        if bit == 2:
            return lax.rem(rank + 2, 4)
        return lax.rem(rank + 2, 4) + 1 - 2 * low_bit

    def first_hop(g, kind, which):
        to = flip(kind + 1)
        return pltpu.make_async_remote_copy(
            src_ref=piece(g, kind, to if which == 0 else flip(3)),
            dst_ref=arrived.at[which, g, kind],
            send_sem=ps_sem.at[2 * kind + which, g], recv_sem=pr_sem.at[2 * kind + which, g],
            device_id={"head": to}, device_id_type=pl.DeviceIdType.MESH,
        )

    def second_hop(g, kind):
        to = flip(2 - kind)
        return pltpu.make_async_remote_copy(
            src_ref=piece(g, kind, to), dst_ref=summed.at[g, kind],
            send_sem=ss_sem.at[kind, g], recv_sem=sr_sem.at[kind, g],
            device_id={"head": to}, device_id_type=pl.DeviceIdType.MESH,
        )

    square = ranks == 4

    def send_group(g):
        if square:
            for which in (1, 0):
                for kind in range(2):
                    first_hop(g, kind, which).start()
        else:
            for away in range(1, ranks):
                give(g, away).start()

    def forward_group(g):
        if square:
            for kind in range(2):
                first_hop(g, kind, 1).wait_recv()
                at = pl.ds(pl.multiple_of(flip(2 - kind) * share, share), share)
                parts[g, kind, at, :] += arrived[1, g, kind]
                second_hop(g, kind).start()

    def collect_group(g):
        own = pl.ds(pl.multiple_of(rank * share, share), share)
        for kind, out in enumerate((db_out, dc_out)):
            val = parts[g, kind, own, :]
            if square:
                first_hop(g, kind, 0).wait_recv()
                second_hop(g, kind).wait_recv()
                val = val + arrived[0, g, kind] + summed[g, kind]
            else:
                if kind == 0:
                    for away in range(1, ranks):
                        give(g, away).wait_recv()
                for away in range(1, ranks):
                    val = val + arrived[away - 1, g, kind]
            out[:, g, :] = val

    def settle_group(g):
        if square:
            for kind in range(2):
                for which in range(2):
                    first_hop(g, kind, which).wait_send()
                second_hop(g, kind).wait_send()
        else:
            for away in range(1, ranks):
                give(g, away).wait_send()

    def whole(g):
        return jnp.exp(prefix * (total(g, 0) + total(g, 1)))

    def pass_f(p):
        for j in range(2):
            g = 2 * p + j
            state_out[g] = whole(g) * state_in[g] + prefix * state[g]
        hop_f(p).start()

    def pass_b(p):
        for j in range(2):
            g = 2 * p + j
            grad_out[g] = whole(g) * grad_in[g] + grad_own[g]
        hop_b(p).start()

    @pl.when(pos == 0)
    def _():
        state_in[...] = jnp.zeros_like(state_in)

    @pl.when(pos == peers - 1)
    def _():
        grad_in[...] = jnp.zeros_like(grad_in)

    @pl.when(jnp.logical_or(pos == 0, pos == peers - 1))
    def _():
        pl.semaphore_wait(barrier, ranks)

    @pl.when(jnp.logical_and(pos > 0, pos < peers - 1))
    def _():
        pl.semaphore_wait(barrier, ranks + 1)

    def local_states(p, carry):
        xs = join(*slabs(x_ref, p))
        dys = join(*slabs(dy_ref, p))
        for j in range(2):
            g = 2 * p + j
            adds, backs = [], []
            for k in range(blocks):
                wi = by_head(wi_b, g, k)
                dt = by_head(dt_b, g, k)
                scaled = (xs[j][span(k)] * (dt * jnp.exp(total(g, k) - wi))).astype(BF16)
                adds.append(mm(b_ref[g, span(k), :], scaled, 0, 0))
                lifted = (dys[j][span(k)] * mask_b[span(k), :] * jnp.exp(wi)).astype(BF16)
                backs.append(mm(c_ref[g, span(k), :], lifted, 0, 0))
            first_state[g] = adds[0]
            state[g] = jnp.exp(total(g, 1)) * adds[0] + adds[1]
            later_grad[g] = backs[1]
            grad_own[g] = backs[0] + jnp.exp(total(g, 0)) * backs[1]

        @pl.when(pos == 0)
        def _():
            pass_f(p)

        @pl.when(pos == peers - 1)
        def _():
            pass_b(p)

        return carry

    lax.fori_loop(0, pairs, local_states, 0)

    def inside(p):
        xs = join(*slabs(x_ref, p))
        dys = join(*slabs(dy_ref, p))
        for j in range(2):
            g = 2 * p + j
            for k in range(blocks):
                b_blk = b_ref[g, span(k), :]
                c_blk = c_ref[g, span(k), :]
                scores = mm(c_blk, b_blk, 1, 1)
                x16 = xs[j][span(k)].astype(BF16)
                dyf = dys[j][span(k)] * mask_b[span(k), :]
                dy16 = dyf.astype(BF16)
                ys, dxs = [], []
                d_scores = None
                for m in range(2):
                    h = m * groups + g
                    col = wi_b[h, span(k), :]
                    col = jnp.concatenate([col, col], axis=1)
                    row = wi_t[pl.ds(h, 1), span(k)]
                    decay = jnp.where(tri, jnp.exp(jnp.minimum(col - row, 0.0)), 0.0)
                    decay = decay * dt_t[pl.ds(h, 1), span(k)]
                    weights = (scores * decay).astype(BF16)
                    mine = low if m == 0 else jnp.logical_not(low)
                    dy_m = jnp.where(mine, dyf, 0.0).astype(BF16)
                    d_weights = mm(dy_m, x16, 1, 1) * decay
                    d_scores = d_weights if d_scores is None else d_scores + d_weights
                    ys.append(mm(weights, x16, 1, 0))
                    dxs.append(mm(weights, dy16, 0, 0))
                y_acc[g, span(k), :] = jnp.where(low, ys[0], ys[1])
                dx_acc[g, span(k), :] = jnp.where(low, dxs[0], dxs[1])
                ds16 = d_scores.astype(BF16)
                parts[g, 1, span(k), :] = mm(ds16, b_blk, 1, 0)
                parts[g, 0, span(k), :] = mm(ds16, c_blk, 0, 0)

    q_acc[...] = jnp.zeros_like(q_acc)
    last = lax.broadcasted_iota(jnp.int32, (BLOCK, 1), 0) == BLOCK - 1
    pick_row = lax.broadcasted_iota(jnp.int32, (4 * LANES, LANES), 0)
    pick_col = lax.broadcasted_iota(jnp.int32, (4 * LANES, LANES), 1)
    pick_head = (
        jnp.where(pick_row % LANES >= 64, groups, 0) + jnp.where(pick_row >= 2 * LANES, heads, 0)
    )

    def across(p):
        @pl.when(pos == peers - 1)
        def _():
            hop_f(p).wait_recv()

        @pl.when(pos == 0)
        def _():
            hop_b(p).wait_recv()

        xs = join(*slabs(x_ref, p))
        dys = join(*slabs(dy_ref, p))
        y_parts, dx_parts = [], []
        for j in range(2):
            g = 2 * p + j
            pick = (pick_col == pick_head + g).astype(BF16)
            gain = jnp.where(low, gain_b[pl.ds(g, 1), :], gain_b[pl.ds(groups + g, 1), :])
            start = state_in[g]
            carry_grad = prefix * grad_in[g]
            entered = (start, jnp.exp(total(g, 0)) * start + first_state[g])
            leaving = (later_grad[g] + jnp.exp(total(g, 1)) * carry_grad, carry_grad)
            y_rows, dx_rows = [], []
            for k in range(blocks):
                wi = by_head(wi_b, g, k)
                dt = by_head(dt_b, g, k)
                end = total(g, k)
                up = jnp.exp(wi)
                down = dt * jnp.exp(end - wi)
                e16 = entered[k].astype(BF16)
                g16 = leaving[k].astype(BF16)
                x = xs[j][span(k)]
                mask = mask_b[span(k), :]
                dy = dys[j][span(k)] * mask
                b_blk = b_ref[g, span(k), :]
                c_blk = c_ref[g, span(k), :]
                y = y_acc[g, span(k), :] + up * mm(c_blk, e16, 1, 0)
                dx_s = down * mm(b_blk, g16, 1, 0)
                dx = dx_acc[g, span(k), :] + dx_s
                parts[g, 1, span(k), :] += mm((dy * up).astype(BF16), e16, 1, 1)
                parts[g, 0, span(k), :] += mm((x * down).astype(BF16), g16, 1, 1)
                q2 = x * dx
                extra = jnp.sum(x * dx_s, axis=0, keepdims=True) + jnp.exp(end) * jnp.sum(
                    leaving[k] * entered[k], axis=0, keepdims=True
                )
                q1 = dy * y - q2 + jnp.where(last, extra, 0.0)
                q1h = q1.astype(BF16)
                q2h = q2.astype(BF16)
                q1l = (q1 - q1h.astype(F32)).astype(BF16)
                q2l = (q2 - q2h.astype(F32)).astype(BF16)
                q_acc[span(k), :] += mm(jnp.concatenate([q1h, q1l, q2h, q2l], axis=1), pick, 1, 0)
                y_rows.append((y + gain * x) * mask)
                dx_rows.append(dx + gain * dy)
            send_group(g)
            y_parts.append(jnp.concatenate(y_rows, axis=0))
            dx_parts.append(jnp.concatenate(dx_rows, axis=0))
        for ref, pair in ((y_ref, y_parts), (dx_ref, dx_parts)):
            lo, hi = join(*pair)
            ref[:, pl.ds(pl.multiple_of(p * LANES, LANES), LANES)] = lo.astype(BF16)
            ref[:, pl.ds(pl.multiple_of(half + p * LANES, LANES), LANES)] = hi.astype(BF16)

    lag = max(1, peers - 3)
    middle = jnp.logical_and(pos > 0, pos < peers - 1)

    def stage(s, carry):
        pf = s - (pos - 1)
        pb = s - (peers - 2 - pos)

        @pl.when(jnp.logical_and(middle, jnp.logical_and(pf >= 0, pf < pairs)))
        def _():
            hop_f(pf).wait_recv()
            pass_f(pf)

        @pl.when(jnp.logical_and(middle, jnp.logical_and(pb >= 0, pb < pairs)))
        def _():
            hop_b(pb).wait_recv()
            pass_b(pb)

        @pl.when(s < pairs)
        def _():
            inside(s)

        @pl.when(jnp.logical_and(s >= lag, s < pairs + lag))
        def _():
            across(s - lag)

        @pl.when(jnp.logical_and(s > lag, s < pairs + lag))
        def _():
            for j in range(2):
                forward_group(2 * (s - lag - 1) + j)

        return carry

    lax.fori_loop(0, pairs + lag, stage, 0)
    for g in range(groups - 2, groups):
        forward_group(g)

    for k in range(blocks):
        q = q_acc[span(k), :].T
        step = dt_t[:, span(k)]
        d_log = lax.dot_general(
            q[:heads], tri.astype(F32), (((1,), (0,)), ((), ())),
            preferred_element_type=F32, precision=EXACT,
        )
        slope = jax.nn.sigmoid(step_ref[:, span(k)]) * kept(k)
        safe = jnp.where(step > 0.0, step, 1.0)
        gs_ref[:, span(k)] = slope * (q[heads : 2 * heads] / safe - rate * d_log)

    for g in range(groups):
        collect_group(g)
    for g in range(groups):
        settle_group(g)

    def finish(p, carry):
        @pl.when(pos < peers - 1)
        def _():
            hop_f(p).wait_send()

        @pl.when(pos > 0)
        def _():
            hop_b(p).wait_send()

        return carry

    lax.fori_loop(0, pairs, finish, 0)


def paired_kernel(
    peers, heads, groups,
    x_hbm, dy_hbm, b_hbm, c_hbm, step_ref, gain_ref, decay_ref, lengths_ref,
    y_hbm, dx_hbm, gs_ref, grads,
    x_in, dy_in, b_in, c_in, b_ref, c_ref, wide, wi_c, dt_c, wd_t, wd_f, xj, dyj,
    state, first_state, grad_own, later_grad, state_in, grad_in,
    y_acc, dx_acc, q_acc, mask_b, gain_b, decay_b, parts, arrived, summed,
    in_sem, bc_sem, out_sem, xs_sem, xr_sem, ws_sem, wr_sem, fs_sem, fr_sem, bs_sem, br_sem, ps_sem, pr_sem, ss_sem, sr_sem,
):
    ranks = 4
    pos = lax.axis_index("seq")
    rank = lax.axis_index("head")
    bit_x = lax.rem(rank, 2)
    bit_y = rank // 2
    prefix = jnp.where(pos < PREFIX_DEVS, 1.0, 0.0).astype(F32)
    rows = x_in.shape[0]
    blocks = rows // BLOCK
    pairs = groups // 2
    share = rows // ranks
    zero_unit = groups + pairs
    low = lax.broadcasted_iota(jnp.int32, (1, LANES), 1) < 64
    mesh_id = pl.DeviceIdType.MESH

    def bit(par):
        return (1 - par) * bit_x + par * bit_y

    def beside(par):
        return rank + (1 - par) * (1 - 2 * bit_x) + 2 * par * (1 - 2 * bit_y)

    def mine(p):
        return 2 * p + bit(p % 2)

    def given(p):
        return 2 * p + 1 - bit(p % 2)

    def slab(i):
        return pl.ds(pl.multiple_of(i * LANES, LANES), LANES)

    def fetch(i, which):
        src, dst = ((x_hbm, x_in), (dy_hbm, dy_in))[which]
        return pltpu.make_async_copy(src.at[:, slab(i)], dst.at[:, slab(i)], in_sem.at[which, i])

    def leave(i, which):
        src, dst = ((x_in, y_hbm), (dy_in, dx_hbm))[which]
        return pltpu.make_async_copy(src.at[:, slab(i)], dst.at[:, slab(i)], out_sem.at[which, i])

    chunk = b_in.shape[1]
    chunks = rows // chunk

    def fetch_proj(i, which):
        src, dst = ((b_hbm, b_in), (c_hbm, c_in))[which]
        at = pl.ds(pl.multiple_of(i * chunk, chunk), chunk)
        return pltpu.make_async_copy(src.at[at], dst.at[i % 2], bc_sem.at[which, i])

    for p in range(pairs):
        for which in range(2):
            for i in (p, pairs + p):
                fetch(i, which).start()
    for i in range(2):
        for which in range(2):
            fetch_proj(i, which).start()

    barrier = pltpu.get_barrier_semaphore()
    for par in range(2):
        pl.semaphore_signal(barrier, inc=1, device_id={"head": beside(par)}, device_id_type=mesh_id)

    @pl.when(pos > 0)
    def _():
        pl.semaphore_signal(barrier, inc=1, device_id={"seq": pos - 1}, device_id_type=mesh_id)

    @pl.when(pos < peers - 1)
    def _():
        pl.semaphore_signal(barrier, inc=1, device_id={"seq": pos + 1}, device_id_type=mesh_id)

    def span(k):
        return slice(k * BLOCK, (k + 1) * BLOCK)

    tri = lax.broadcasted_iota(jnp.int32, (BLOCK, BLOCK), 0) >= lax.broadcasted_iota(
        jnp.int32, (BLOCK, BLOCK), 1
    )
    limit = jnp.where(pos < PREFIX_DEVS, rows, lengths_ref[jnp.maximum(pos - PREFIX_DEVS, 0)])
    ids = lax.broadcasted_iota(jnp.int32, (1, BLOCK), 1)
    tall_ids = lax.broadcasted_iota(jnp.int32, (BLOCK, LANES), 0)

    def kept(k):
        return jnp.where(ids + k * BLOCK < limit, 1.0, 0.0).astype(F32)

    def turn(v):
        return pltpu.roll(v, 64, 1)

    def join(lo, hi):
        return jnp.where(low, lo, turn(hi)), jnp.where(low, turn(lo), hi)

    def copy_of(src, dst, send, recv, where):
        return pltpu.make_async_remote_copy(
            src_ref=src, dst_ref=dst, send_sem=send, recv_sem=recv, device_id=where, device_id_type=mesh_id
        )

    def raw(p, which):
        ref = (xj, dyj)[which]
        return copy_of(
            ref.at[given(p)], ref.at[groups + p], xs_sem.at[which, p], xr_sem.at[which, p], {"head": beside(p % 2)}
        )

    def tell(par):
        return copy_of(wd_t, wd_f.at[par], ws_sem.at[par], wr_sem.at[par], {"head": beside(par)})

    def hop_f(u):
        return copy_of(state.at[u], state_in.at[u], fs_sem.at[u], fr_sem.at[u], {"seq": pos + 1})

    def hop_b(u):
        return copy_of(grad_own.at[u], grad_in.at[u], bs_sem.at[u], br_sem.at[u], {"seq": pos - 1})

    def piece(p, kind, owner):
        return parts.at[p, kind, pl.ds(pl.multiple_of(owner * share, share), share), :]

    def first_hop(p, kind, which):
        par = p % 2
        to = beside(1 - par)
        opposite = 3 - rank
        return copy_of(
            piece(p, kind, to if which == 0 else opposite), arrived.at[which, p, kind],
            ps_sem.at[which, p, kind], pr_sem.at[which, p, kind], {"head": to},
        )

    def second_hop(p, kind):
        to = beside(p % 2)
        return copy_of(
            piece(p, kind, to), summed.at[p, kind], ss_sem.at[p, kind], sr_sem.at[p, kind], {"head": to}
        )

    for k in range(blocks):
        mask_b[span(k), :] = jnp.where(tall_ids + k * BLOCK < limit, 1.0, 0.0).astype(F32)

    def spread(p):
        for which in range(2):
            for i in (p, pairs + p):
                fetch(i, which).wait()
        at_lo, at_hi = slab(p), slab(pairs + p)
        xj[2 * p], xj[2 * p + 1] = join(x_in[:, at_lo].astype(F32), x_in[:, at_hi].astype(F32))
        mask = mask_b[...]
        dyj[2 * p], dyj[2 * p + 1] = join(dy_in[:, at_lo].astype(F32) * mask, dy_in[:, at_hi].astype(F32) * mask)

    for p in range(2):
        spread(p)

    @pl.when(jnp.logical_or(pos == 0, pos == peers - 1))
    def _():
        pl.semaphore_wait(barrier, 3)

    @pl.when(jnp.logical_and(pos > 0, pos < peers - 1))
    def _():
        pl.semaphore_wait(barrier, 4)

    for which in range(2):
        for p in range(2):
            raw(p, which).start()

    for h in range(heads):
        gain_b[h : h + 1, :] = jnp.full((1, LANES), gain_ref[h], F32)
        decay_b[h : h + 1, :] = jnp.full((1, LANES), decay_ref[h], F32)
    rate = jnp.concatenate([decay_b[...]] * (BLOCK // LANES), axis=1)
    for k in range(blocks):
        step_in = step_ref[:, span(k)]
        step = (jnp.maximum(step_in, 0.0) + jnp.log1p(jnp.exp(-jnp.abs(step_in)))) * kept(k)
        sums = lax.dot_general(
            -(step * rate), tri.astype(F32), (((1,), (1,)), ((), ())),
            preferred_element_type=F32, precision=EXACT,
        )
        wd_t[0, :, span(k)] = sums
        wd_t[1, :, span(k)] = step
    for par in range(2):
        tell(par).start()
    for p in range(2, pairs):
        spread(p)
        for which in range(2):
            raw(p, which).start()
    state_in[zero_unit] = jnp.zeros_like(state_in[zero_unit])
    grad_in[zero_unit] = jnp.zeros_like(grad_in[zero_unit])

    def loop(start, stop, body):
        def step(i, carry):
            body(i)
            return carry

        lax.fori_loop(start, stop, step, 0)

    def columns(src, u, g):
        for kind, ref in ((0, wi_c), (1, dt_c)):
            for k in range(blocks):
                cols = [
                    jnp.broadcast_to(src(kind, pl.ds(m * groups + g, 1), span(k)), (64, BLOCK)) for m in range(2)
                ]
                ref[u, span(k), :] = jnp.concatenate(cols, axis=0).T

    def group_first(i):
        at = pl.ds(pl.multiple_of(i * chunk, chunk), chunk)
        for which, (src, dst) in enumerate(((b_in, b_ref), (c_in, c_ref))):
            fetch_proj(i, which).wait()
            flat = src[i % 2].astype(F32).reshape(chunk * groups, src.shape[3])
            for n in range(src.shape[3] // LANES):
                cut = slice(n * LANES, (n + 1) * LANES)
                wide[n] = flat[:, cut]
                for g in range(groups):
                    dst[g, at, cut] = wide[n, pl.ds(g, chunk, stride=groups), :].astype(BF16)

        @pl.when(i + 2 < chunks)
        def _():
            for which in range(2):
                fetch_proj(i + 2, which).start()

    loop(0, chunks, group_first)
    loop(0, groups, lambda g: columns(lambda kind, at, cut: wd_t[kind, at, cut], g, g))

    class Part:
        def __init__(self, unit, group):
            self.unit, self.group = unit, group

        def x(self, k):
            return xj[self.unit, span(k), :]

        def dy(self, k):
            return dyj[self.unit, span(k), :]

        def within(self, k):
            return wi_c[self.unit, span(k), :]

        def step(self, k):
            return dt_c[self.unit, span(k), :]

        def total(self, k):
            return wi_c[self.unit, pl.ds((k + 1) * BLOCK - 1, 1), :]

    def own_part(g):
        return Part(g, g)

    def handed_part(p):
        return Part(groups + p, mine(p))

    def whole(part):
        return jnp.exp(prefix * (part.total(0) + part.total(1)))

    def start_of(u):
        return state_in[jnp.where(pos > 0, u, zero_unit)]

    def carry_of(u):
        return grad_in[jnp.where(pos < PREFIX_DEVS, u, zero_unit)]

    def entered_by(part):
        start = start_of(part.unit)
        return start, jnp.exp(part.total(0)) * start + first_state[part.unit]

    def leaving_by(part):
        carry = carry_of(part.unit)
        return later_grad[part.unit] + jnp.exp(part.total(1)) * carry, carry

    def pass_f(part):
        u = part.unit
        state[u] = whole(part) * start_of(u) + prefix * state[u]
        hop_f(u).start()

    def pass_b(part):
        u = part.unit
        held = grad_in[jnp.where(pos < peers - 1, u, zero_unit)]
        grad_own[u] = whole(part) * held + grad_own[u]
        hop_b(u).start()

    def emit(part):
        @pl.when(pos == 0)
        def _():
            pass_f(part)

        @pl.when(pos == peers - 1)
        def _():
            pass_b(part)

    def relay_f(unit):
        hop_f(unit).wait_recv()

        @pl.when(pos < peers - 1)
        def _():
            pass_f(Part(unit, 0))

    def relay_b(unit):
        hop_b(unit).wait_recv()

        @pl.when(pos > 0)
        def _():
            pass_b(Part(unit, 0))

    order = [mine(0), mine(1), mine(2), groups, groups + 1, mine(3), given(0), groups + 2, groups + 3]
    order += [given(1), given(2), given(3)]

    def unit_at(i):
        unit = order[0]
        for k in range(1, len(order)):
            unit = jnp.where(i == k, order[k], unit)
        return unit

    served = [(0, 0, 0)]

    def serve(*upto):
        before = served[-1]
        served.append(upto)

        def count(marks, hops):
            marked = [jnp.where(hops == d + 1, marks[d], 0) for d in range(3)]
            return marked[0] + marked[1] + marked[2]

        for hops, how in ((pos, relay_f), (peers - 1 - pos, relay_b)):
            loop(count(before, hops), count(upto, hops), lambda i: how(unit_at(i)))

    def local_states(part):
        u, g = part.unit, part.group
        adds, backs = [], []
        for k in range(blocks):
            wi = part.within(k)
            scaled = (part.x(k) * (part.step(k) * jnp.exp(part.total(k) - wi))).astype(BF16)
            adds.append(mm(b_ref[g, span(k), :], scaled, 0, 0))
            lifted = (part.dy(k) * jnp.exp(wi)).astype(BF16)
            backs.append(mm(c_ref[g, span(k), :], lifted, 0, 0))
        first_state[u] = adds[0]
        state[u] = jnp.exp(part.total(1)) * adds[0] + adds[1]
        later_grad[u] = backs[1]
        grad_own[u] = backs[0] + jnp.exp(part.total(0)) * backs[1]

    def decay_by(row, dt_row):
        col = jnp.broadcast_to(row, (LANES, BLOCK)).T
        col = jnp.concatenate([col, col], axis=1)
        return jnp.where(tri, jnp.exp(jnp.minimum(col - row, 0.0)), 0.0) * dt_row

    def only(m, v):
        return jnp.where(low if m == 0 else jnp.logical_not(low), v, 0.0).astype(BF16)

    def inside(p, g, with_scores):
        for k in range(blocks):
            scores = mm(c_ref[g, span(k), :], b_ref[g, span(k), :], 1, 1)
            x16 = xj[g, span(k), :].astype(BF16)
            dyf = dyj[g, span(k), :]
            dy16 = dyf.astype(BF16)
            ys, dxs, d_scores = [], [], None
            for m in range(2):
                h = m * groups + g
                decay = decay_by(wd_t[0, pl.ds(h, 1), span(k)], wd_t[1, pl.ds(h, 1), span(k)])
                weights = (scores * decay).astype(BF16)
                if with_scores:
                    d_weights = mm(only(m, dyf), x16, 1, 1) * decay
                    d_scores = d_weights if d_scores is None else d_scores + d_weights
                ys.append(mm(weights, x16, 1, 0))
                dxs.append(mm(weights, dy16, 0, 0))
            y_acc[g, span(k), :] = jnp.where(low, ys[0], ys[1])
            dx_acc[g, span(k), :] = jnp.where(low, dxs[0], dxs[1])
            if with_scores:
                parts[p, 0, span(k), :] = d_scores

    def handed_scores(p):
        g = mine(p)
        for k in range(blocks):
            x16 = xj[groups + p, span(k), :].astype(BF16)
            dyf = dyj[groups + p, span(k), :]
            d_scores = parts[p, 0, span(k), :]
            for m in range(2):
                at = pl.ds(m * groups + g, 1)
                decay = decay_by(wd_f[p % 2, 0, at, span(k)], wd_f[p % 2, 1, at, span(k)])
                d_scores = d_scores + mm(only(m, dyf), x16, 1, 1) * decay
            ds16 = d_scores.astype(BF16)
            parts[p, 1, span(k), :] = mm(ds16, b_ref[g, span(k), :], 1, 0)
            parts[p, 0, span(k), :] = mm(ds16, c_ref[g, span(k), :], 0, 0)

    def grow_c(p):
        both = (own_part(mine(p)), handed_part(p))
        entered = [entered_by(part) for part in both]
        for k in range(blocks):
            e16 = jnp.concatenate([e[k].astype(BF16) for e in entered], axis=1)
            lifted = jnp.concatenate(
                [(part.dy(k) * jnp.exp(part.within(k))).astype(BF16) for part in both], axis=1
            )
            parts[p, 1, span(k), :] += mm(lifted, e16, 1, 1)

    def grow_b(p):
        both = (own_part(mine(p)), handed_part(p))
        leaving = [leaving_by(part) for part in both]
        for k in range(blocks):
            g16 = jnp.concatenate([v[k].astype(BF16) for v in leaving], axis=1)
            scaled = jnp.concatenate(
                [
                    (part.x(k) * (part.step(k) * jnp.exp(part.total(k) - part.within(k)))).astype(BF16)
                    for part in both
                ],
                axis=1,
            )
            parts[p, 0, span(k), :] += mm(scaled, g16, 1, 1)

    early_kind = jnp.where(pos < PREFIX_DEVS, 1, 0)
    late_kind = 1 - early_kind

    def send(p, kind):
        for which in (1, 0):
            first_hop(p, kind, which).start()

    def early(p):
        @pl.when(pos < PREFIX_DEVS)
        def _():
            grow_c(p)

        @pl.when(pos >= PREFIX_DEVS)
        def _():
            grow_b(p)

        send(p, early_kind)

    def late(p):
        @pl.when(pos < PREFIX_DEVS)
        def _():
            grow_b(p)

        @pl.when(pos >= PREFIX_DEVS)
        def _():
            grow_c(p)

        send(p, late_kind)

    def forward(p, kind):
        first_hop(p, kind, 1).wait_recv()
        at = pl.ds(pl.multiple_of(beside(p % 2) * share, share), share)
        parts[p, kind, at, :] += arrived[1, p, kind]
        second_hop(p, kind).start()

    def receive(p):
        for which in range(2):
            raw(p, which).wait_recv()
        columns(lambda kind, at, cut: wd_f[p % 2, kind, at, cut], groups + p, mine(p))
        part = handed_part(p)
        local_states(part)
        emit(part)
        handed_scores(p)

    last = lax.broadcasted_iota(jnp.int32, (BLOCK, 1), 0) == BLOCK - 1
    pick_row = lax.broadcasted_iota(jnp.int32, (4 * LANES, LANES), 0)
    pick_col = lax.broadcasted_iota(jnp.int32, (4 * LANES, LANES), 1)
    pick_head = (
        jnp.where(pick_row % LANES >= 64, groups, 0) + jnp.where(pick_row >= 2 * LANES, heads, 0)
    )

    def across(p):
        y_parts, dx_parts = [], []
        for j in range(2):
            g = 2 * p + j
            part = own_part(g)
            pick = (pick_col == pick_head + g).astype(BF16)
            gain = jnp.where(low, gain_b[pl.ds(g, 1), :], gain_b[pl.ds(groups + g, 1), :])
            entered = entered_by(part)
            leaving = leaving_by(part)
            y_rows, dx_rows = [], []
            for k in range(blocks):
                wi = part.within(k)
                end = part.total(k)
                up = jnp.exp(wi)
                down = part.step(k) * jnp.exp(end - wi)
                x = part.x(k)
                dy = part.dy(k)
                y = y_acc[g, span(k), :] + up * mm(c_ref[g, span(k), :], entered[k].astype(BF16), 1, 0)
                dx_s = down * mm(b_ref[g, span(k), :], leaving[k].astype(BF16), 1, 0)
                dx = dx_acc[g, span(k), :] + dx_s
                q2 = x * dx
                extra = jnp.sum(x * dx_s, axis=0, keepdims=True) + jnp.exp(end) * jnp.sum(
                    leaving[k] * entered[k], axis=0, keepdims=True
                )
                q1 = dy * y - q2 + jnp.where(last, extra, 0.0)
                q1h = q1.astype(BF16)
                q2h = q2.astype(BF16)
                q1l = (q1 - q1h.astype(F32)).astype(BF16)
                q2l = (q2 - q2h.astype(F32)).astype(BF16)
                q_acc[span(k), :] += mm(jnp.concatenate([q1h, q1l, q2h, q2l], axis=1), pick, 1, 0)
                y_rows.append((y + gain * x) * mask_b[span(k), :])
                dx_rows.append(dx + gain * dy)
            y_parts.append(jnp.concatenate(y_rows, axis=0))
            dx_parts.append(jnp.concatenate(dx_rows, axis=0))
        for which, (ref, pair) in enumerate(((x_in, y_parts), (dy_in, dx_parts))):
            lo, hi = join(*pair)
            ref[:, slab(p)] = lo.astype(BF16)
            ref[:, slab(pairs + p)] = hi.astype(BF16)
            for i in (p, pairs + p):
                leave(i, which).start()

    def finish_steps():
        for k in range(blocks):
            q = q_acc[span(k), :].T
            step = wd_t[1, :, span(k)]
            d_log = lax.dot_general(
                q[:heads], tri.astype(F32), (((1,), (0,)), ((), ())),
                preferred_element_type=F32, precision=EXACT,
            )
            slope = jax.nn.sigmoid(step_ref[:, span(k)]) * kept(k)
            safe = jnp.where(step > 0.0, step, 1.0)
            gs_ref[:, span(k)] = slope * (q[heads : 2 * heads] / safe - rate * d_log)

    def begin(p):
        local_states(own_part(mine(p)))

        @pl.when(p < pairs - 1)
        def _():
            emit(own_part(mine(p)))

    def kept_blocks(p):
        inside(p, mine(p), True)

    def given_blocks(p):
        local_states(own_part(given(p)))
        inside(p, given(p), False)

    own = pl.ds(pl.multiple_of(rank * share, share), share)

    def collect(p, kind):
        first_hop(p, kind, 0).wait_recv()
        second_hop(p, kind).wait_recv()
        kept_sum = parts[p, kind, own, :] + arrived[0, p, kind]
        other = summed[p, kind]
        first = bit(p % 2) == 0
        grads[kind, :, 2 * p, :] = jnp.where(first, kept_sum, other)
        grads[kind, :, 2 * p + 1, :] = jnp.where(first, other, kept_sum)

    q_acc[...] = jnp.zeros_like(q_acc)
    loop(0, pairs, begin)
    loop(0, pairs, kept_blocks)
    for par in range(2):
        tell(par).wait_recv()
    serve(1, 0, 0)
    receive(0)
    serve(2, 0, 0)
    receive(1)
    emit(own_part(mine(3)))
    serve(3, 1, 0)
    given_blocks(0)
    emit(own_part(given(0)))
    serve(4, 2, 0)
    early(0)
    given_blocks(1)
    serve(5, 3, 1)
    early(1)
    given_blocks(2)
    serve(6, 4, 2)
    receive(2)
    serve(6, 5, 3)
    receive(3)
    for p in (1, 2):
        emit(own_part(given(p)))
    serve(8, 6, 4)
    early(2)
    forward(0, early_kind)
    serve(9, 6, 4)
    early(3)
    forward(1, early_kind)
    serve(9, 7, 5)
    late(0)
    late(1)
    given_blocks(3)
    emit(own_part(given(3)))
    serve(10, 8, 6)
    forward(2, early_kind)
    forward(3, early_kind)
    serve(11, 9, 8)
    late(2)
    serve(12, 10, 9)
    late(3)
    forward(0, late_kind)
    forward(1, late_kind)
    across(0)
    serve(12, 11, 10)
    across(1)
    serve(12, 12, 11)
    across(2)
    serve(12, 12, 12)
    forward(2, late_kind)
    forward(3, late_kind)
    across(3)
    finish_steps()
    for kind in (early_kind, late_kind):
        for p in range(pairs):
            collect(p, kind)

    for par in range(2):
        tell(par).wait_send()
    for which in range(2):
        for i in range(2 * pairs):
            leave(i, which).wait()
    def settle(p):
        for kind in range(2):
            raw(p, kind).wait_send()
            for which in range(2):
                first_hop(p, kind, which).wait_send()
            second_hop(p, kind).wait_send()

    loop(0, pairs, settle)

    def finish(u):
        @pl.when(pos < peers - 1)
        def _():
            hop_f(u).wait_send()

        @pl.when(pos > 0)
        def _():
            hop_b(u).wait_send()

    loop(0, groups + pairs, finish)


def writing_kernel(pieces, y_hbm, dx_hbm, gs_hbm, grads, *refs):
    sources = (y_hbm, dx_hbm, gs_hbm, grads.at[0], grads.at[1])
    count = len(sources)
    targets, held, (in_sem, out_sem) = refs[:count], refs[count : 2 * count], refs[2 * count :]
    arrive, onward = [], []
    for i in range(count):
        cuts = pieces if i != 2 else 1
        for n in range(cuts):
            part = held[i].shape[0] // cuts
            at = pl.ds(n * part, part)
            arrive.append(pltpu.make_async_copy(sources[i].at[at], held[i].at[at], in_sem.at[i, n]))
            onward.append(pltpu.make_async_copy(held[i].at[at], targets[i].at[at], out_sem.at[i, n]))
    for copy in arrive:
        copy.start()
    for copy, after in zip(arrive, onward):
        copy.wait()
        after.start()
    for copy in onward:
        copy.wait()


def write_out(pieces, y, dx, gs, grads):
    anywhere = pl.BlockSpec(memory_space=pl.ANY)
    shapes = [(v.shape, v.dtype) for v in (y, dx, gs)] + [(grads.shape[1:], grads.dtype)] * 2
    sems = pltpu.SemaphoreType.DMA((len(shapes), pieces))
    return pl.pallas_call(
        functools.partial(writing_kernel, pieces),
        out_shape=tuple(jax.ShapeDtypeStruct(*shape) for shape in shapes),
        in_specs=[anywhere] * 4,
        out_specs=(anywhere,) * len(shapes),
        scratch_shapes=[pltpu.VMEM(*shape) for shape in shapes] + [sems, sems],
        compiler_params=pltpu.CompilerParams(vmem_limit_bytes=56 * 1024 * 1024),
    )(y, dx, gs, grads)


def on_device(inputs, step_raw, decay_rate, skip_gain, b_proj, c_proj, lengths, cotangent):
    rows, width = inputs.shape
    heads = decay_rate.shape[0]
    groups, states = b_proj.shape[1:]
    peers = lax.axis_size("seq")
    ranks = lax.axis_size("head")
    hops = 2 if ranks == 4 else ranks - 1
    vmem = pl.BlockSpec(memory_space=pltpu.VMEM)
    smem = pl.BlockSpec(memory_space=pltpu.SMEM)
    carry = pltpu.VMEM((groups, states, LANES), F32)
    dma = pltpu.SemaphoreType.DMA((groups // 2,))

    if ranks == 4 and peers == 4 and groups == 2 * PAIRS:
        pairs = groups // 2
        units = pltpu.VMEM((groups + pairs, states, LANES), F32)
        arriving = pltpu.VMEM((groups + pairs + 1, states, LANES), F32)
        per_group = pltpu.VMEM((groups, rows, LANES), F32)
        per_unit = pltpu.VMEM((groups + pairs, rows, LANES), F32)
        wide_rows = pltpu.VMEM((rows, width), BF16)
        proj = pltpu.VMEM((2, rows // 4, groups, states), BF16)
        lead = pltpu.VMEM((groups, rows, states), BF16)
        hop = pltpu.SemaphoreType.DMA((groups + pairs,))
        kernel = functools.partial(paired_kernel, peers, heads, groups)
        operands = (b_proj, c_proj)
        big = pl.BlockSpec(memory_space=pl.ANY)
        out_specs = (big, big, vmem, vmem)
        grads = (jax.ShapeDtypeStruct((2, rows // ranks, groups, states), F32),)
        scratch = [
            wide_rows, wide_rows, proj, proj, lead, lead,
            pltpu.VMEM((states // LANES, rows // 4 * groups, LANES), F32),
            per_unit, per_unit,
            pltpu.VMEM((2, heads, rows), F32),
            pltpu.VMEM((2, 2, heads, rows), F32),
            per_unit, per_unit,
            units, units, units, units, arriving, arriving,
            per_group, per_group,
            pltpu.VMEM((rows, LANES), F32),
            pltpu.VMEM((rows, LANES), F32),
            pltpu.VMEM((heads, LANES), F32),
            pltpu.VMEM((heads, LANES), F32),
            pltpu.VMEM((pairs, 2, rows, states), F32),
            pltpu.VMEM((2, pairs, 2, rows // ranks, states), F32),
            pltpu.VMEM((pairs, 2, rows // ranks, states), F32),
            pltpu.SemaphoreType.DMA((2, groups)),
            pltpu.SemaphoreType.DMA((2, 4)),
            pltpu.SemaphoreType.DMA((2, groups)),
            pltpu.SemaphoreType.DMA((2, pairs)),
            pltpu.SemaphoreType.DMA((2, pairs)),
            pltpu.SemaphoreType.DMA((2,)),
            pltpu.SemaphoreType.DMA((2,)),
            hop, hop, hop, hop,
            pltpu.SemaphoreType.DMA((2, pairs, 2)),
            pltpu.SemaphoreType.DMA((2, pairs, 2)),
            pltpu.SemaphoreType.DMA((pairs, 2)),
            pltpu.SemaphoreType.DMA((pairs, 2)),
        ]
    else:
        kernel = functools.partial(layer_kernel, peers, ranks, heads, groups)
        operands = (jnp.swapaxes(b_proj, 0, 1), jnp.swapaxes(c_proj, 0, 1))
        big = vmem
        out_specs = (vmem,) * 5
        grads = (jax.ShapeDtypeStruct((rows // ranks, groups, states), F32),) * 2
        scratch = [
            pltpu.VMEM((heads, rows, LANES), F32),
            pltpu.VMEM((heads, rows, LANES), F32),
            pltpu.VMEM((heads, rows), F32),
            pltpu.VMEM((heads, rows), F32),
            carry, carry, carry, carry, carry, carry, carry, carry,
            pltpu.VMEM((groups, rows, LANES), F32),
            pltpu.VMEM((groups, rows, LANES), F32),
            pltpu.VMEM((rows, LANES), F32),
            pltpu.VMEM((rows, LANES), F32),
            pltpu.VMEM((heads, LANES), F32),
            pltpu.VMEM((heads, LANES), F32),
            pltpu.VMEM((groups, 2, rows, states), F32),
            pltpu.VMEM((hops, groups, 2, rows // ranks, states), F32),
            pltpu.VMEM((groups, 2, rows // ranks, states), F32),
            dma, dma, dma, dma,
            pltpu.SemaphoreType.DMA((max(ranks - 1, 4), groups)),
            pltpu.SemaphoreType.DMA((max(ranks - 1, 4), groups)),
            pltpu.SemaphoreType.DMA((2, groups)),
            pltpu.SemaphoreType.DMA((2, groups)),
        ]

    results = pl.pallas_call(
        kernel,
        out_shape=(
            jax.ShapeDtypeStruct((rows, width), BF16),
            jax.ShapeDtypeStruct((rows, width), BF16),
            jax.ShapeDtypeStruct((heads, rows), F32),
            *grads,
        ),
        in_specs=[big] * 4 + [vmem] + [smem] * 3,
        out_specs=out_specs,
        scratch_shapes=scratch,
        compiler_params=pltpu.CompilerParams(
            collective_id=0, has_side_effects=True, vmem_limit_bytes=56 * 1024 * 1024
        ),
    )(
        inputs, cotangent, *operands, step_raw.T, skip_gain, decay_rate, lengths
    )
    if ranks == 4 and peers == 4 and groups == 2 * PAIRS:
        results = write_out(4, *results)
    y, dx, gs, db, dc = results
    return (y, dx, gs.T, db, dc)


def solution(mesh):
    rows = P(("dp", "seq"), "head")
    proj = P(("dp", "seq"), None, None)
    grads = P(("dp", "seq", "head"), None, None)
    return jax.shard_map(
        on_device,
        mesh=mesh,
        in_specs=(rows, rows, P("head"), P("head"), proj, proj, P("dp"), rows),
        out_specs=(rows, rows, rows, grads, grads),
        check_vma=False,
    )
```

```python
import functools

import jax
import jax.numpy as jnp
from jax import lax
from jax.experimental import pallas as pl
from jax.experimental.pallas import tpu as pltpu
from jax.sharding import PartitionSpec as P

BLOCK = 256
PREFIX_DEVS = 2
LANES = 128
PAIRS = 4
F32 = jnp.float32
BF16 = jnp.bfloat16
EXACT = lax.Precision.HIGHEST


def mm(a, b, ca, cb):
    return lax.dot_general(a, b, (((ca,), (cb,)), ((), ())), preferred_element_type=F32)


def layer_kernel(
    peers, ranks, heads, groups,
    x_ref, dy_ref, b_ref, c_ref, step_ref, gain_ref, decay_ref, lengths_ref,
    y_ref, dx_ref, gs_ref, db_out, dc_out,
    wi_b, dt_b, wi_t, dt_t, state, first_state, grad_own, later_grad,
    state_in, state_out, grad_in, grad_out, y_acc, dx_acc, q_acc, mask_b, gain_b, decay_b,
    parts, arrived, summed, fs_sem, fr_sem, bs_sem, br_sem, ps_sem, pr_sem, ss_sem, sr_sem,
):
    pos = lax.axis_index("seq")
    rank = lax.axis_index("head")
    prefix = jnp.where(pos < PREFIX_DEVS, 1.0, 0.0).astype(F32)
    rows = x_ref.shape[0]
    blocks = rows // BLOCK
    pairs = groups // 2
    half = groups * 64
    low = lax.broadcasted_iota(jnp.int32, (1, LANES), 1) < 64

    share = rows // ranks
    barrier = pltpu.get_barrier_semaphore()
    for away in range(1, ranks):
        pl.semaphore_signal(
            barrier, inc=1, device_id={"head": lax.rem(rank + away, ranks)},
            device_id_type=pl.DeviceIdType.MESH,
        )

    @pl.when(pos > 0)
    def _():
        pl.semaphore_signal(barrier, inc=1, device_id={"seq": pos - 1}, device_id_type=pl.DeviceIdType.MESH)

    @pl.when(pos < peers - 1)
    def _():
        pl.semaphore_signal(barrier, inc=1, device_id={"seq": pos + 1}, device_id_type=pl.DeviceIdType.MESH)

    tri = lax.broadcasted_iota(jnp.int32, (BLOCK, BLOCK), 0) >= lax.broadcasted_iota(
        jnp.int32, (BLOCK, BLOCK), 1
    )

    def span(k):
        return slice(k * BLOCK, (k + 1) * BLOCK)

    limit = jnp.where(pos < PREFIX_DEVS, rows, lengths_ref[jnp.maximum(pos - PREFIX_DEVS, 0)])
    ids = lax.broadcasted_iota(jnp.int32, (1, BLOCK), 1)
    for h in range(heads):
        gain_b[h : h + 1, :] = jnp.full((1, LANES), gain_ref[h], F32)
        decay_b[h : h + 1, :] = jnp.full((1, LANES), decay_ref[h], F32)
    rate = jnp.concatenate([decay_b[...]] * (BLOCK // LANES), axis=1)

    def kept(k):
        return jnp.where(ids + k * BLOCK < limit, 1.0, 0.0).astype(F32)

    for k in range(blocks):
        raw = step_ref[:, span(k)]
        keep = kept(k)
        step = (jnp.maximum(raw, 0.0) + jnp.log1p(jnp.exp(-jnp.abs(raw)))) * keep
        sums = lax.dot_general(
            -(step * rate), tri.astype(F32), (((1,), (1,)), ((), ())),
            preferred_element_type=F32, precision=EXACT,
        )
        wi_t[:, span(k)] = sums
        dt_t[:, span(k)] = step
        tall = jnp.concatenate(
            [step, sums, jnp.broadcast_to(keep, (LANES - 2 * heads, BLOCK))], axis=0
        ).T
        for h in range(heads):
            wi_b[h, span(k), :] = jnp.broadcast_to(tall[:, heads + h : heads + h + 1], (BLOCK, LANES))
            dt_b[h, span(k), :] = jnp.broadcast_to(tall[:, h : h + 1], (BLOCK, LANES))
        mask_b[span(k), :] = jnp.broadcast_to(tall[:, 2 * heads : 2 * heads + 1], (BLOCK, LANES))

    def turn(v):
        return pltpu.roll(v, 64, 1)

    def slabs(ref, p):
        lo = ref[:, pl.ds(pl.multiple_of(p * LANES, LANES), LANES)].astype(F32)
        hi = ref[:, pl.ds(pl.multiple_of(half + p * LANES, LANES), LANES)].astype(F32)
        return lo, hi

    def join(lo, hi):
        return jnp.where(low, lo, turn(hi)), jnp.where(low, turn(lo), hi)

    def by_head(ref, g, k):
        return jnp.where(low, ref[g, span(k), :], ref[groups + g, span(k), :])

    def total(g, k):
        at = pl.ds((k + 1) * BLOCK - 1, 1)
        return jnp.where(low, wi_b[g, at, :], wi_b[groups + g, at, :])

    def hop_f(p):
        part = pl.ds(2 * p, 2)
        return pltpu.make_async_remote_copy(
            src_ref=state_out.at[part], dst_ref=state_in.at[part],
            send_sem=fs_sem.at[p], recv_sem=fr_sem.at[p],
            device_id={"seq": pos + 1}, device_id_type=pl.DeviceIdType.MESH,
        )

    def hop_b(p):
        part = pl.ds(2 * p, 2)
        return pltpu.make_async_remote_copy(
            src_ref=grad_out.at[part], dst_ref=grad_in.at[part],
            send_sem=bs_sem.at[p], recv_sem=br_sem.at[p],
            device_id={"seq": pos - 1}, device_id_type=pl.DeviceIdType.MESH,
        )

    def give(g, away):
        to = lax.rem(rank + away, ranks)
        return pltpu.make_async_remote_copy(
            src_ref=parts.at[g, :, pl.ds(pl.multiple_of(to * share, share), share), :],
            dst_ref=arrived.at[away - 1, g],
            send_sem=ps_sem.at[away - 1, g], recv_sem=pr_sem.at[away - 1, g],
            device_id={"head": to}, device_id_type=pl.DeviceIdType.MESH,
        )

    def piece(g, kind, owner):
        return parts.at[g, kind, pl.ds(pl.multiple_of(owner * share, share), share), :]

    def flip(bit):
        low_bit = lax.rem(rank, 2)
        if bit == 1:
            return rank + 1 - 2 * low_bit
        if bit == 2:
            return lax.rem(rank + 2, 4)
        return lax.rem(rank + 2, 4) + 1 - 2 * low_bit

    def first_hop(g, kind, which):
        to = flip(kind + 1)
        return pltpu.make_async_remote_copy(
            src_ref=piece(g, kind, to if which == 0 else flip(3)),
            dst_ref=arrived.at[which, g, kind],
            send_sem=ps_sem.at[2 * kind + which, g], recv_sem=pr_sem.at[2 * kind + which, g],
            device_id={"head": to}, device_id_type=pl.DeviceIdType.MESH,
        )

    def second_hop(g, kind):
        to = flip(2 - kind)
        return pltpu.make_async_remote_copy(
            src_ref=piece(g, kind, to), dst_ref=summed.at[g, kind],
            send_sem=ss_sem.at[kind, g], recv_sem=sr_sem.at[kind, g],
            device_id={"head": to}, device_id_type=pl.DeviceIdType.MESH,
        )

    square = ranks == 4

    def send_group(g):
        if square:
            for which in (1, 0):
                for kind in range(2):
                    first_hop(g, kind, which).start()
        else:
            for away in range(1, ranks):
                give(g, away).start()

    def forward_group(g):
        if square:
            for kind in range(2):
                first_hop(g, kind, 1).wait_recv()
                at = pl.ds(pl.multiple_of(flip(2 - kind) * share, share), share)
                parts[g, kind, at, :] += arrived[1, g, kind]
                second_hop(g, kind).start()

    def collect_group(g):
        own = pl.ds(pl.multiple_of(rank * share, share), share)
        for kind, out in enumerate((db_out, dc_out)):
            val = parts[g, kind, own, :]
            if square:
                first_hop(g, kind, 0).wait_recv()
                second_hop(g, kind).wait_recv()
                val = val + arrived[0, g, kind] + summed[g, kind]
            else:
                if kind == 0:
                    for away in range(1, ranks):
                        give(g, away).wait_recv()
                for away in range(1, ranks):
                    val = val + arrived[away - 1, g, kind]
            out[:, g, :] = val

    def settle_group(g):
        if square:
            for kind in range(2):
                for which in range(2):
                    first_hop(g, kind, which).wait_send()
                second_hop(g, kind).wait_send()
        else:
            for away in range(1, ranks):
                give(g, away).wait_send()

    def whole(g):
        return jnp.exp(prefix * (total(g, 0) + total(g, 1)))

    def pass_f(p):
        for j in range(2):
            g = 2 * p + j
            state_out[g] = whole(g) * state_in[g] + prefix * state[g]
        hop_f(p).start()

    def pass_b(p):
        for j in range(2):
            g = 2 * p + j
            grad_out[g] = whole(g) * grad_in[g] + grad_own[g]
        hop_b(p).start()

    @pl.when(pos == 0)
    def _():
        state_in[...] = jnp.zeros_like(state_in)

    @pl.when(pos == peers - 1)
    def _():
        grad_in[...] = jnp.zeros_like(grad_in)

    @pl.when(jnp.logical_or(pos == 0, pos == peers - 1))
    def _():
        pl.semaphore_wait(barrier, ranks)

    @pl.when(jnp.logical_and(pos > 0, pos < peers - 1))
    def _():
        pl.semaphore_wait(barrier, ranks + 1)

    def local_states(p, carry):
        xs = join(*slabs(x_ref, p))
        dys = join(*slabs(dy_ref, p))
        for j in range(2):
            g = 2 * p + j
            adds, backs = [], []
            for k in range(blocks):
                wi = by_head(wi_b, g, k)
                dt = by_head(dt_b, g, k)
                scaled = (xs[j][span(k)] * (dt * jnp.exp(total(g, k) - wi))).astype(BF16)
                adds.append(mm(b_ref[g, span(k), :], scaled, 0, 0))
                lifted = (dys[j][span(k)] * mask_b[span(k), :] * jnp.exp(wi)).astype(BF16)
                backs.append(mm(c_ref[g, span(k), :], lifted, 0, 0))
            first_state[g] = adds[0]
            state[g] = jnp.exp(total(g, 1)) * adds[0] + adds[1]
            later_grad[g] = backs[1]
            grad_own[g] = backs[0] + jnp.exp(total(g, 0)) * backs[1]

        @pl.when(pos == 0)
        def _():
            pass_f(p)

        @pl.when(pos == peers - 1)
        def _():
            pass_b(p)

        return carry

    lax.fori_loop(0, pairs, local_states, 0)

    def inside(p):
        xs = join(*slabs(x_ref, p))
        dys = join(*slabs(dy_ref, p))
        for j in range(2):
            g = 2 * p + j
            for k in range(blocks):
                b_blk = b_ref[g, span(k), :]
                c_blk = c_ref[g, span(k), :]
                scores = mm(c_blk, b_blk, 1, 1)
                x16 = xs[j][span(k)].astype(BF16)
                dyf = dys[j][span(k)] * mask_b[span(k), :]
                dy16 = dyf.astype(BF16)
                ys, dxs = [], []
                d_scores = None
                for m in range(2):
                    h = m * groups + g
                    col = wi_b[h, span(k), :]
                    col = jnp.concatenate([col, col], axis=1)
                    row = wi_t[pl.ds(h, 1), span(k)]
                    decay = jnp.where(tri, jnp.exp(jnp.minimum(col - row, 0.0)), 0.0)
                    decay = decay * dt_t[pl.ds(h, 1), span(k)]
                    weights = (scores * decay).astype(BF16)
                    mine = low if m == 0 else jnp.logical_not(low)
                    dy_m = jnp.where(mine, dyf, 0.0).astype(BF16)
                    d_weights = mm(dy_m, x16, 1, 1) * decay
                    d_scores = d_weights if d_scores is None else d_scores + d_weights
                    ys.append(mm(weights, x16, 1, 0))
                    dxs.append(mm(weights, dy16, 0, 0))
                y_acc[g, span(k), :] = jnp.where(low, ys[0], ys[1])
                dx_acc[g, span(k), :] = jnp.where(low, dxs[0], dxs[1])
                ds16 = d_scores.astype(BF16)
                parts[g, 1, span(k), :] = mm(ds16, b_blk, 1, 0)
                parts[g, 0, span(k), :] = mm(ds16, c_blk, 0, 0)

    q_acc[...] = jnp.zeros_like(q_acc)
    last = lax.broadcasted_iota(jnp.int32, (BLOCK, 1), 0) == BLOCK - 1
    pick_row = lax.broadcasted_iota(jnp.int32, (4 * LANES, LANES), 0)
    pick_col = lax.broadcasted_iota(jnp.int32, (4 * LANES, LANES), 1)
    pick_head = (
        jnp.where(pick_row % LANES >= 64, groups, 0) + jnp.where(pick_row >= 2 * LANES, heads, 0)
    )

    def across(p):
        @pl.when(pos == peers - 1)
        def _():
            hop_f(p).wait_recv()

        @pl.when(pos == 0)
        def _():
            hop_b(p).wait_recv()

        xs = join(*slabs(x_ref, p))
        dys = join(*slabs(dy_ref, p))
        y_parts, dx_parts = [], []
        for j in range(2):
            g = 2 * p + j
            pick = (pick_col == pick_head + g).astype(BF16)
            gain = jnp.where(low, gain_b[pl.ds(g, 1), :], gain_b[pl.ds(groups + g, 1), :])
            start = state_in[g]
            carry_grad = prefix * grad_in[g]
            entered = (start, jnp.exp(total(g, 0)) * start + first_state[g])
            leaving = (later_grad[g] + jnp.exp(total(g, 1)) * carry_grad, carry_grad)
            y_rows, dx_rows = [], []
            for k in range(blocks):
                wi = by_head(wi_b, g, k)
                dt = by_head(dt_b, g, k)
                end = total(g, k)
                up = jnp.exp(wi)
                down = dt * jnp.exp(end - wi)
                e16 = entered[k].astype(BF16)
                g16 = leaving[k].astype(BF16)
                x = xs[j][span(k)]
                mask = mask_b[span(k), :]
                dy = dys[j][span(k)] * mask
                b_blk = b_ref[g, span(k), :]
                c_blk = c_ref[g, span(k), :]
                y = y_acc[g, span(k), :] + up * mm(c_blk, e16, 1, 0)
                dx_s = down * mm(b_blk, g16, 1, 0)
                dx = dx_acc[g, span(k), :] + dx_s
                parts[g, 1, span(k), :] += mm((dy * up).astype(BF16), e16, 1, 1)
                parts[g, 0, span(k), :] += mm((x * down).astype(BF16), g16, 1, 1)
                q2 = x * dx
                extra = jnp.sum(x * dx_s, axis=0, keepdims=True) + jnp.exp(end) * jnp.sum(
                    leaving[k] * entered[k], axis=0, keepdims=True
                )
                q1 = dy * y - q2 + jnp.where(last, extra, 0.0)
                q1h = q1.astype(BF16)
                q2h = q2.astype(BF16)
                q1l = (q1 - q1h.astype(F32)).astype(BF16)
                q2l = (q2 - q2h.astype(F32)).astype(BF16)
                q_acc[span(k), :] += mm(jnp.concatenate([q1h, q1l, q2h, q2l], axis=1), pick, 1, 0)
                y_rows.append((y + gain * x) * mask)
                dx_rows.append(dx + gain * dy)
            send_group(g)
            y_parts.append(jnp.concatenate(y_rows, axis=0))
            dx_parts.append(jnp.concatenate(dx_rows, axis=0))
        for ref, pair in ((y_ref, y_parts), (dx_ref, dx_parts)):
            lo, hi = join(*pair)
            ref[:, pl.ds(pl.multiple_of(p * LANES, LANES), LANES)] = lo.astype(BF16)
            ref[:, pl.ds(pl.multiple_of(half + p * LANES, LANES), LANES)] = hi.astype(BF16)

    lag = max(1, peers - 3)
    middle = jnp.logical_and(pos > 0, pos < peers - 1)

    def stage(s, carry):
        pf = s - (pos - 1)
        pb = s - (peers - 2 - pos)

        @pl.when(jnp.logical_and(middle, jnp.logical_and(pf >= 0, pf < pairs)))
        def _():
            hop_f(pf).wait_recv()
            pass_f(pf)

        @pl.when(jnp.logical_and(middle, jnp.logical_and(pb >= 0, pb < pairs)))
        def _():
            hop_b(pb).wait_recv()
            pass_b(pb)

        @pl.when(s < pairs)
        def _():
            inside(s)

        @pl.when(jnp.logical_and(s >= lag, s < pairs + lag))
        def _():
            across(s - lag)

        @pl.when(jnp.logical_and(s > lag, s < pairs + lag))
        def _():
            for j in range(2):
                forward_group(2 * (s - lag - 1) + j)

        return carry

    lax.fori_loop(0, pairs + lag, stage, 0)
    for g in range(groups - 2, groups):
        forward_group(g)

    for k in range(blocks):
        q = q_acc[span(k), :].T
        step = dt_t[:, span(k)]
        d_log = lax.dot_general(
            q[:heads], tri.astype(F32), (((1,), (0,)), ((), ())),
            preferred_element_type=F32, precision=EXACT,
        )
        slope = jax.nn.sigmoid(step_ref[:, span(k)]) * kept(k)
        safe = jnp.where(step > 0.0, step, 1.0)
        gs_ref[:, span(k)] = slope * (q[heads : 2 * heads] / safe - rate * d_log)

    for g in range(groups):
        collect_group(g)
    for g in range(groups):
        settle_group(g)

    def finish(p, carry):
        @pl.when(pos < peers - 1)
        def _():
            hop_f(p).wait_send()

        @pl.when(pos > 0)
        def _():
            hop_b(p).wait_send()

        return carry

    lax.fori_loop(0, pairs, finish, 0)


def paired_kernel(
    peers, heads, groups,
    x_hbm, dy_hbm, b_hbm, c_hbm, step_hbm, gain_hbm, decay_hbm, lengths_hbm,
    y_hbm, dx_hbm, gs_ref, grads_hbm,
    x_in, dy_in, b_in, c_in, b_ref, c_ref, wide, wi_c, dt_c, wd_t, wd_f, xj, dyj,
    state, first_state, grad_own, later_grad, state_in, grad_in,
    y_acc, dx_acc, q_acc, mask_b, gain_b, decay_b, parts, arrived, summed,
    in_sem, bc_sem, out_sem, step_ref, gain_ref, decay_ref, lengths_ref, few_sem, grads, grads_sem, xs_sem, xr_sem, ws_sem, wr_sem, fs_sem, fr_sem, bs_sem, br_sem, ps_sem, pr_sem, ss_sem, sr_sem,
):
    ranks = 4
    pos = lax.axis_index("seq")
    rank = lax.axis_index("head")
    bit_x = lax.rem(rank, 2)
    bit_y = rank // 2
    prefix = jnp.where(pos < PREFIX_DEVS, 1.0, 0.0).astype(F32)
    rows = x_in.shape[0]
    blocks = rows // BLOCK
    pairs = groups // 2
    share = rows // ranks
    zero_unit = groups + pairs
    low = lax.broadcasted_iota(jnp.int32, (1, LANES), 1) < 64
    mesh_id = pl.DeviceIdType.MESH

    def bit(par):
        return (1 - par) * bit_x + par * bit_y

    def beside(par):
        return rank + (1 - par) * (1 - 2 * bit_x) + 2 * par * (1 - 2 * bit_y)

    def mine(p):
        return 2 * p + bit(p % 2)

    def given(p):
        return 2 * p + 1 - bit(p % 2)

    def slab(i):
        return pl.ds(pl.multiple_of(i * LANES, LANES), LANES)

    def fetch(i, which):
        src, dst = ((x_hbm, x_in), (dy_hbm, dy_in))[which]
        at = slice(2 * i * LANES, (2 * i + 2) * LANES)
        return pltpu.make_async_copy(src.at[:, at], dst.at[:, at], in_sem.at[which, i])

    def leave(i, which):
        src, dst = ((x_in, y_hbm), (dy_in, dx_hbm))[which]
        return pltpu.make_async_copy(src.at[:, slab(i)], dst.at[:, slab(i)], out_sem.at[which, i])

    def leave_grads(kind):
        return pltpu.make_async_copy(grads.at[kind], grads_hbm.at[kind], grads_sem.at[kind])

    few = [
        pltpu.make_async_copy(src, dst, few_sem.at[i])
        for i, (src, dst) in enumerate(
            ((lengths_hbm, lengths_ref), (gain_hbm, gain_ref), (decay_hbm, decay_ref), (step_hbm, step_ref))
        )
    ]

    chunk = b_in.shape[1]
    chunks = rows // chunk

    def fetch_proj(i, which):
        src, dst = ((b_hbm, b_in), (c_hbm, c_in))[which]
        at = pl.ds(pl.multiple_of(i * chunk, chunk), chunk)
        return pltpu.make_async_copy(src.at[at], dst.at[i % 2], bc_sem.at[which, i])

    def fetch_pairs(t, which):
        return [fetch(i, which) for i in (t, pairs // 2 + t)]

    for copy in fetch_pairs(0, 0):
        copy.start()
    barrier = pltpu.get_barrier_semaphore()
    for par in range(2):
        pl.semaphore_signal(barrier, inc=1, device_id={"head": beside(par)}, device_id_type=mesh_id)

    @pl.when(pos > 0)
    def _():
        pl.semaphore_signal(barrier, inc=1, device_id={"seq": pos - 1}, device_id_type=mesh_id)

    @pl.when(pos < peers - 1)
    def _():
        pl.semaphore_signal(barrier, inc=1, device_id={"seq": pos + 1}, device_id_type=mesh_id)

    def span(k):
        return slice(k * BLOCK, (k + 1) * BLOCK)

    tri = lax.broadcasted_iota(jnp.int32, (BLOCK, BLOCK), 0) >= lax.broadcasted_iota(
        jnp.int32, (BLOCK, BLOCK), 1
    )
    ids = lax.broadcasted_iota(jnp.int32, (1, BLOCK), 1)
    tall_ids = lax.broadcasted_iota(jnp.int32, (BLOCK, LANES), 0)

    def turn(v):
        return pltpu.roll(v, 64, 1)

    def join(lo, hi):
        return jnp.where(low, lo, turn(hi)), jnp.where(low, turn(lo), hi)

    def copy_of(src, dst, send, recv, where):
        return pltpu.make_async_remote_copy(
            src_ref=src, dst_ref=dst, send_sem=send, recv_sem=recv, device_id=where, device_id_type=mesh_id
        )

    def raw(p, which):
        ref = (xj, dyj)[which]
        return copy_of(
            ref.at[given(p)], ref.at[groups + p], xs_sem.at[which, p], xr_sem.at[which, p], {"head": beside(p % 2)}
        )

    def tell(par):
        return copy_of(wd_t, wd_f.at[par], ws_sem.at[par], wr_sem.at[par], {"head": beside(par)})

    def hop_f(u):
        return copy_of(state.at[u], state_in.at[u], fs_sem.at[u], fr_sem.at[u], {"seq": pos + 1})

    def hop_b(u):
        return copy_of(grad_own.at[u], grad_in.at[u], bs_sem.at[u], br_sem.at[u], {"seq": pos - 1})

    def piece(p, kind, owner):
        return parts.at[p, kind, pl.ds(pl.multiple_of(owner * share, share), share), :]

    def first_hop(p, kind, which):
        par = p % 2
        to = beside(1 - par)
        opposite = 3 - rank
        return copy_of(
            piece(p, kind, to if which == 0 else opposite), arrived.at[which, p, kind],
            ps_sem.at[which, p, kind], pr_sem.at[which, p, kind], {"head": to},
        )

    def second_hop(p, kind):
        to = beside(p % 2)
        return copy_of(
            piece(p, kind, to), summed.at[p, kind], ss_sem.at[p, kind], sr_sem.at[p, kind], {"head": to}
        )

    def spread(p, which):
        src, dst = ((x_in, xj), (dy_in, dyj))[which]
        lo, hi = src[:, slab(p)].astype(F32), src[:, slab(pairs + p)].astype(F32)
        if which == 1:
            lo, hi = lo * mask_b[...], hi * mask_b[...]
        dst[2 * p], dst[2 * p + 1] = join(lo, hi)

    few[0].start()
    for copy in fetch_pairs(0, 1) + few[1:] + fetch_pairs(1, 0) + fetch_pairs(1, 1):
        copy.start()
    for i in range(2):
        for which in range(2):
            fetch_proj(i, which).start()
    for copy in fetch_pairs(0, 0):
        copy.wait()
    for p in range(2):
        spread(p, 0)

    @pl.when(jnp.logical_or(pos == 0, pos == peers - 1))
    def _():
        pl.semaphore_wait(barrier, 3)

    @pl.when(jnp.logical_and(pos > 0, pos < peers - 1))
    def _():
        pl.semaphore_wait(barrier, 4)

    for p in range(2):
        raw(p, 0).start()
    few[0].wait()
    limit = jnp.where(pos < PREFIX_DEVS, rows, lengths_ref[jnp.maximum(pos - PREFIX_DEVS, 0)])
    for k in range(blocks):
        mask_b[span(k), :] = jnp.where(tall_ids + k * BLOCK < limit, 1.0, 0.0).astype(F32)
    for copy in fetch_pairs(0, 1):
        copy.wait()
    for p in range(2):
        spread(p, 1)
        raw(p, 1).start()
    for copy in few[1:]:
        copy.wait()

    def kept(k):
        return jnp.where(ids + k * BLOCK < limit, 1.0, 0.0).astype(F32)

    for h in range(heads):
        gain_b[h : h + 1, :] = jnp.full((1, LANES), gain_ref[h], F32)
        decay_b[h : h + 1, :] = jnp.full((1, LANES), decay_ref[h], F32)
    rate = jnp.concatenate([decay_b[...]] * (BLOCK // LANES), axis=1)
    for k in range(blocks):
        step_in = step_ref[:, span(k)]
        step = (jnp.maximum(step_in, 0.0) + jnp.log1p(jnp.exp(-jnp.abs(step_in)))) * kept(k)
        sums = lax.dot_general(
            -(step * rate), tri.astype(F32), (((1,), (1,)), ((), ())),
            preferred_element_type=F32, precision=EXACT,
        )
        wd_t[0, :, span(k)] = sums
        wd_t[1, :, span(k)] = step
    for par in range(2):
        tell(par).start()
    for copy in fetch_pairs(1, 0) + fetch_pairs(1, 1):
        copy.wait()
    for p in range(2, pairs):
        for which in range(2):
            spread(p, which)
            raw(p, which).start()
    state_in[zero_unit] = jnp.zeros_like(state_in[zero_unit])
    grad_in[zero_unit] = jnp.zeros_like(grad_in[zero_unit])

    def loop(start, stop, body):
        def step(i, carry):
            body(i)
            return carry

        lax.fori_loop(start, stop, step, 0)

    def columns(src, u, g):
        for kind, ref in ((0, wi_c), (1, dt_c)):
            for k in range(blocks):
                cols = [
                    jnp.broadcast_to(src(kind, pl.ds(m * groups + g, 1), span(k)), (64, BLOCK)) for m in range(2)
                ]
                ref[u, span(k), :] = jnp.concatenate(cols, axis=0).T

    def group_first(i):
        at = pl.ds(pl.multiple_of(i * chunk, chunk), chunk)
        for which, (src, dst) in enumerate(((b_in, b_ref), (c_in, c_ref))):
            fetch_proj(i, which).wait()
            flat = src[i % 2].astype(F32).reshape(chunk * groups, src.shape[3])
            for n in range(src.shape[3] // LANES):
                cut = slice(n * LANES, (n + 1) * LANES)
                wide[n] = flat[:, cut]
                for g in range(groups):
                    dst[g, at, cut] = wide[n, pl.ds(g, chunk, stride=groups), :].astype(BF16)

        @pl.when(i + 2 < chunks)
        def _():
            for which in range(2):
                fetch_proj(i + 2, which).start()

    loop(0, chunks, group_first)
    loop(0, groups, lambda g: columns(lambda kind, at, cut: wd_t[kind, at, cut], g, g))

    class Part:
        def __init__(self, unit, group):
            self.unit, self.group = unit, group

        def x(self, k):
            return xj[self.unit, span(k), :]

        def dy(self, k):
            return dyj[self.unit, span(k), :]

        def within(self, k):
            return wi_c[self.unit, span(k), :]

        def step(self, k):
            return dt_c[self.unit, span(k), :]

        def total(self, k):
            return wi_c[self.unit, pl.ds((k + 1) * BLOCK - 1, 1), :]

    def own_part(g):
        return Part(g, g)

    def handed_part(p):
        return Part(groups + p, mine(p))

    def whole(part):
        return jnp.exp(prefix * (part.total(0) + part.total(1)))

    def start_of(u):
        return state_in[jnp.where(pos > 0, u, zero_unit)]

    def carry_of(u):
        return grad_in[jnp.where(pos < PREFIX_DEVS, u, zero_unit)]

    def entered_by(part):
        start = start_of(part.unit)
        return start, jnp.exp(part.total(0)) * start + first_state[part.unit]

    def leaving_by(part):
        carry = carry_of(part.unit)
        return later_grad[part.unit] + jnp.exp(part.total(1)) * carry, carry

    def pass_f(part):
        u = part.unit
        state[u] = whole(part) * start_of(u) + prefix * state[u]
        hop_f(u).start()

    def pass_b(part):
        u = part.unit
        held = grad_in[jnp.where(pos < peers - 1, u, zero_unit)]
        grad_own[u] = whole(part) * held + grad_own[u]
        hop_b(u).start()

    def emit(part):
        @pl.when(pos == 0)
        def _():
            pass_f(part)

        @pl.when(pos == peers - 1)
        def _():
            pass_b(part)

    def relay_f(unit):
        hop_f(unit).wait_recv()

        @pl.when(pos < peers - 1)
        def _():
            pass_f(Part(unit, 0))

    def relay_b(unit):
        hop_b(unit).wait_recv()

        @pl.when(pos > 0)
        def _():
            pass_b(Part(unit, 0))

    order = [mine(0), mine(1), mine(2), groups, groups + 1, mine(3), given(0), groups + 2, groups + 3]
    order += [given(1), given(2), given(3)]

    def unit_at(i):
        unit = order[0]
        for k in range(1, len(order)):
            unit = jnp.where(i == k, order[k], unit)
        return unit

    served = [(0, 0, 0)]

    def serve(*upto):
        before = served[-1]
        served.append(upto)

        def count(marks, hops):
            marked = [jnp.where(hops == d + 1, marks[d], 0) for d in range(3)]
            return marked[0] + marked[1] + marked[2]

        for hops, how in ((pos, relay_f), (peers - 1 - pos, relay_b)):
            loop(count(before, hops), count(upto, hops), lambda i: how(unit_at(i)))

    def local_states(part):
        u, g = part.unit, part.group
        adds, backs = [], []
        for k in range(blocks):
            wi = part.within(k)
            scaled = (part.x(k) * (part.step(k) * jnp.exp(part.total(k) - wi))).astype(BF16)
            adds.append(mm(b_ref[g, span(k), :], scaled, 0, 0))
            lifted = (part.dy(k) * jnp.exp(wi)).astype(BF16)
            backs.append(mm(c_ref[g, span(k), :], lifted, 0, 0))
        first_state[u] = adds[0]
        state[u] = jnp.exp(part.total(1)) * adds[0] + adds[1]
        later_grad[u] = backs[1]
        grad_own[u] = backs[0] + jnp.exp(part.total(0)) * backs[1]

    def decay_by(row, dt_row):
        col = jnp.broadcast_to(row, (LANES, BLOCK)).T
        col = jnp.concatenate([col, col], axis=1)
        return jnp.where(tri, jnp.exp(jnp.minimum(col - row, 0.0)), 0.0) * dt_row

    def only(m, v):
        return jnp.where(low if m == 0 else jnp.logical_not(low), v, 0.0).astype(BF16)

    def inside(p, g, with_scores):
        for k in range(blocks):
            scores = mm(c_ref[g, span(k), :], b_ref[g, span(k), :], 1, 1)
            x16 = xj[g, span(k), :].astype(BF16)
            dyf = dyj[g, span(k), :]
            dy16 = dyf.astype(BF16)
            ys, dxs, d_scores = [], [], None
            for m in range(2):
                h = m * groups + g
                decay = decay_by(wd_t[0, pl.ds(h, 1), span(k)], wd_t[1, pl.ds(h, 1), span(k)])
                weights = (scores * decay).astype(BF16)
                if with_scores:
                    d_weights = mm(only(m, dyf), x16, 1, 1) * decay
                    d_scores = d_weights if d_scores is None else d_scores + d_weights
                ys.append(mm(weights, x16, 1, 0))
                dxs.append(mm(weights, dy16, 0, 0))
            y_acc[g, span(k), :] = jnp.where(low, ys[0], ys[1])
            dx_acc[g, span(k), :] = jnp.where(low, dxs[0], dxs[1])
            if with_scores:
                parts[p, 0, span(k), :] = d_scores

    def handed_scores(p):
        g = mine(p)
        for k in range(blocks):
            x16 = xj[groups + p, span(k), :].astype(BF16)
            dyf = dyj[groups + p, span(k), :]
            d_scores = parts[p, 0, span(k), :]
            for m in range(2):
                at = pl.ds(m * groups + g, 1)
                decay = decay_by(wd_f[p % 2, 0, at, span(k)], wd_f[p % 2, 1, at, span(k)])
                d_scores = d_scores + mm(only(m, dyf), x16, 1, 1) * decay
            ds16 = d_scores.astype(BF16)
            parts[p, 1, span(k), :] = mm(ds16, b_ref[g, span(k), :], 1, 0)
            parts[p, 0, span(k), :] = mm(ds16, c_ref[g, span(k), :], 0, 0)

    def grow_c(p):
        both = (own_part(mine(p)), handed_part(p))
        entered = [entered_by(part) for part in both]
        for k in range(blocks):
            e16 = jnp.concatenate([e[k].astype(BF16) for e in entered], axis=1)
            lifted = jnp.concatenate(
                [(part.dy(k) * jnp.exp(part.within(k))).astype(BF16) for part in both], axis=1
            )
            parts[p, 1, span(k), :] += mm(lifted, e16, 1, 1)

    def grow_b(p):
        both = (own_part(mine(p)), handed_part(p))
        leaving = [leaving_by(part) for part in both]
        for k in range(blocks):
            g16 = jnp.concatenate([v[k].astype(BF16) for v in leaving], axis=1)
            scaled = jnp.concatenate(
                [
                    (part.x(k) * (part.step(k) * jnp.exp(part.total(k) - part.within(k)))).astype(BF16)
                    for part in both
                ],
                axis=1,
            )
            parts[p, 0, span(k), :] += mm(scaled, g16, 1, 1)

    early_kind = jnp.where(pos < PREFIX_DEVS, 1, 0)
    late_kind = 1 - early_kind

    def send(p, kind):
        for which in (1, 0):
            first_hop(p, kind, which).start()

    def early(p):
        @pl.when(pos < PREFIX_DEVS)
        def _():
            grow_c(p)

        @pl.when(pos >= PREFIX_DEVS)
        def _():
            grow_b(p)

        send(p, early_kind)

    def late(p):
        @pl.when(pos < PREFIX_DEVS)
        def _():
            grow_b(p)

        @pl.when(pos >= PREFIX_DEVS)
        def _():
            grow_c(p)

        send(p, late_kind)

    def forward(p, kind):
        first_hop(p, kind, 1).wait_recv()
        at = pl.ds(pl.multiple_of(beside(p % 2) * share, share), share)
        parts[p, kind, at, :] += arrived[1, p, kind]
        second_hop(p, kind).start()

    def receive(p):
        for which in range(2):
            raw(p, which).wait_recv()
        columns(lambda kind, at, cut: wd_f[p % 2, kind, at, cut], groups + p, mine(p))
        part = handed_part(p)
        local_states(part)
        emit(part)
        handed_scores(p)

    last = lax.broadcasted_iota(jnp.int32, (BLOCK, 1), 0) == BLOCK - 1
    pick_row = lax.broadcasted_iota(jnp.int32, (4 * LANES, LANES), 0)
    pick_col = lax.broadcasted_iota(jnp.int32, (4 * LANES, LANES), 1)
    pick_head = (
        jnp.where(pick_row % LANES >= 64, groups, 0) + jnp.where(pick_row >= 2 * LANES, heads, 0)
    )

    def across(p):
        y_parts, dx_parts = [], []
        for j in range(2):
            g = 2 * p + j
            part = own_part(g)
            pick = (pick_col == pick_head + g).astype(BF16)
            gain = jnp.where(low, gain_b[pl.ds(g, 1), :], gain_b[pl.ds(groups + g, 1), :])
            entered = entered_by(part)
            leaving = leaving_by(part)
            y_rows, dx_rows = [], []
            for k in range(blocks):
                wi = part.within(k)
                end = part.total(k)
                up = jnp.exp(wi)
                down = part.step(k) * jnp.exp(end - wi)
                x = part.x(k)
                dy = part.dy(k)
                y = y_acc[g, span(k), :] + up * mm(c_ref[g, span(k), :], entered[k].astype(BF16), 1, 0)
                dx_s = down * mm(b_ref[g, span(k), :], leaving[k].astype(BF16), 1, 0)
                dx = dx_acc[g, span(k), :] + dx_s
                q2 = x * dx
                extra = jnp.sum(x * dx_s, axis=0, keepdims=True) + jnp.exp(end) * jnp.sum(
                    leaving[k] * entered[k], axis=0, keepdims=True
                )
                q1 = dy * y - q2 + jnp.where(last, extra, 0.0)
                q1h = q1.astype(BF16)
                q2h = q2.astype(BF16)
                q1l = (q1 - q1h.astype(F32)).astype(BF16)
                q2l = (q2 - q2h.astype(F32)).astype(BF16)
                q_acc[span(k), :] += mm(jnp.concatenate([q1h, q1l, q2h, q2l], axis=1), pick, 1, 0)
                y_rows.append((y + gain * x) * mask_b[span(k), :])
                dx_rows.append(dx + gain * dy)
            y_parts.append(jnp.concatenate(y_rows, axis=0))
            dx_parts.append(jnp.concatenate(dx_rows, axis=0))
        for which, (ref, pair) in enumerate(((x_in, y_parts), (dy_in, dx_parts))):
            lo, hi = join(*pair)
            ref[:, slab(p)] = lo.astype(BF16)
            ref[:, slab(pairs + p)] = hi.astype(BF16)
            for i in (p, pairs + p):
                leave(i, which).start()

    def finish_steps():
        for k in range(blocks):
            q = q_acc[span(k), :].T
            step = wd_t[1, :, span(k)]
            d_log = lax.dot_general(
                q[:heads], tri.astype(F32), (((1,), (0,)), ((), ())),
                preferred_element_type=F32, precision=EXACT,
            )
            slope = jax.nn.sigmoid(step_ref[:, span(k)]) * kept(k)
            safe = jnp.where(step > 0.0, step, 1.0)
            gs_ref[:, span(k)] = slope * (q[heads : 2 * heads] / safe - rate * d_log)

    def begin(p):
        local_states(own_part(mine(p)))

        @pl.when(p < pairs - 1)
        def _():
            emit(own_part(mine(p)))

    def kept_blocks(p):
        inside(p, mine(p), True)

    def given_blocks(p):
        local_states(own_part(given(p)))
        inside(p, given(p), False)

    own = pl.ds(pl.multiple_of(rank * share, share), share)

    def collect(p, kind):
        first_hop(p, kind, 0).wait_recv()
        second_hop(p, kind).wait_recv()
        kept_sum = parts[p, kind, own, :] + arrived[0, p, kind]
        other = summed[p, kind]
        first = bit(p % 2) == 0
        grads[kind, :, 2 * p, :] = jnp.where(first, kept_sum, other)
        grads[kind, :, 2 * p + 1, :] = jnp.where(first, other, kept_sum)

    q_acc[...] = jnp.zeros_like(q_acc)
    loop(0, pairs, begin)
    loop(0, pairs, kept_blocks)
    for par in range(2):
        tell(par).wait_recv()
    serve(1, 0, 0)
    receive(0)
    serve(2, 0, 0)
    receive(1)
    emit(own_part(mine(3)))
    serve(3, 1, 0)
    given_blocks(0)
    emit(own_part(given(0)))
    serve(4, 2, 0)
    early(0)
    given_blocks(1)
    serve(5, 3, 1)
    early(1)
    given_blocks(2)
    serve(6, 4, 2)
    receive(2)
    serve(6, 5, 3)
    receive(3)
    for p in (1, 2):
        emit(own_part(given(p)))
    serve(8, 6, 4)
    early(2)
    forward(0, early_kind)
    serve(9, 6, 4)
    early(3)
    forward(1, early_kind)
    serve(9, 7, 5)
    late(0)
    late(1)
    given_blocks(3)
    emit(own_part(given(3)))
    serve(10, 8, 6)
    forward(2, early_kind)
    forward(3, early_kind)
    serve(11, 9, 8)
    late(2)
    serve(12, 10, 9)
    late(3)
    forward(0, late_kind)
    forward(1, late_kind)
    across(0)
    serve(12, 11, 10)
    across(1)
    serve(12, 12, 11)
    across(2)
    serve(12, 12, 12)
    forward(2, late_kind)
    forward(3, late_kind)
    across(3)
    finish_steps()
    for kind in (early_kind, late_kind):
        for p in range(pairs):
            collect(p, kind)
        leave_grads(kind).start()

    for kind in range(2):
        leave_grads(kind).wait()
    for par in range(2):
        tell(par).wait_send()
    for which in range(2):
        for i in range(2 * pairs):
            leave(i, which).wait()
    def settle(p):
        for kind in range(2):
            raw(p, kind).wait_send()
            for which in range(2):
                first_hop(p, kind, which).wait_send()
            second_hop(p, kind).wait_send()

    loop(0, pairs, settle)

    def finish(u):
        @pl.when(pos < peers - 1)
        def _():
            hop_f(u).wait_send()

        @pl.when(pos > 0)
        def _():
            hop_b(u).wait_send()

    loop(0, groups + pairs, finish)


def writing_kernel(pieces, y_hbm, dx_hbm, gs_hbm, grads, *refs):
    sources = (y_hbm, dx_hbm, gs_hbm, grads.at[0], grads.at[1])
    count = len(sources)
    targets, held, (in_sem, out_sem) = refs[:count], refs[count : 2 * count], refs[2 * count :]
    arrive, onward = [], []
    for i in range(count):
        cuts = pieces if i != 2 else 1
        for n in range(cuts):
            part = held[i].shape[0] // cuts
            at = pl.ds(n * part, part)
            arrive.append(pltpu.make_async_copy(sources[i].at[at], held[i].at[at], in_sem.at[i, n]))
            onward.append(pltpu.make_async_copy(held[i].at[at], targets[i].at[at], out_sem.at[i, n]))
    for copy in arrive:
        copy.start()
    for copy, after in zip(arrive, onward):
        copy.wait()
        after.start()
    for copy in onward:
        copy.wait()


def write_out(pieces, y, dx, gs, grads):
    anywhere = pl.BlockSpec(memory_space=pl.ANY)
    shapes = [(v.shape, v.dtype) for v in (y, dx, gs)] + [(grads.shape[1:], grads.dtype)] * 2
    sems = pltpu.SemaphoreType.DMA((len(shapes), pieces))
    return pl.pallas_call(
        functools.partial(writing_kernel, pieces),
        out_shape=tuple(jax.ShapeDtypeStruct(*shape) for shape in shapes),
        in_specs=[anywhere] * 4,
        out_specs=(anywhere,) * len(shapes),
        scratch_shapes=[pltpu.VMEM(*shape) for shape in shapes] + [sems, sems],
        compiler_params=pltpu.CompilerParams(vmem_limit_bytes=56 * 1024 * 1024),
    )(y, dx, gs, grads)


def on_device(inputs, step_raw, decay_rate, skip_gain, b_proj, c_proj, lengths, cotangent):
    rows, width = inputs.shape
    heads = decay_rate.shape[0]
    groups, states = b_proj.shape[1:]
    peers = lax.axis_size("seq")
    ranks = lax.axis_size("head")
    hops = 2 if ranks == 4 else ranks - 1
    vmem = pl.BlockSpec(memory_space=pltpu.VMEM)
    smem = pl.BlockSpec(memory_space=pltpu.SMEM)
    carry = pltpu.VMEM((groups, states, LANES), F32)
    dma = pltpu.SemaphoreType.DMA((groups // 2,))

    if ranks == 4 and peers == 4 and groups == 2 * PAIRS:
        pairs = groups // 2
        units = pltpu.VMEM((groups + pairs, states, LANES), F32)
        arriving = pltpu.VMEM((groups + pairs + 1, states, LANES), F32)
        per_group = pltpu.VMEM((groups, rows, LANES), F32)
        per_unit = pltpu.VMEM((groups + pairs, rows, LANES), F32)
        wide_rows = pltpu.VMEM((rows, width), BF16)
        proj = pltpu.VMEM((2, rows // 4, groups, states), BF16)
        lead = pltpu.VMEM((groups, rows, states), BF16)
        hop = pltpu.SemaphoreType.DMA((groups + pairs,))
        kernel = functools.partial(paired_kernel, peers, heads, groups)
        operands = (b_proj, c_proj)
        big = pl.BlockSpec(memory_space=pl.ANY)
        in_specs = [big] * 8
        out_specs = (big, big, vmem, big)
        grads = (jax.ShapeDtypeStruct((2, rows // ranks, groups, states), F32),)
        scratch = [
            wide_rows, wide_rows, proj, proj, lead, lead,
            pltpu.VMEM((states // LANES, rows // 4 * groups, LANES), F32),
            per_unit, per_unit,
            pltpu.VMEM((2, heads, rows), F32),
            pltpu.VMEM((2, 2, heads, rows), F32),
            per_unit, per_unit,
            units, units, units, units, arriving, arriving,
            per_group, per_group,
            pltpu.VMEM((rows, LANES), F32),
            pltpu.VMEM((rows, LANES), F32),
            pltpu.VMEM((heads, LANES), F32),
            pltpu.VMEM((heads, LANES), F32),
            pltpu.VMEM((pairs, 2, rows, states), F32),
            pltpu.VMEM((2, pairs, 2, rows // ranks, states), F32),
            pltpu.VMEM((pairs, 2, rows // ranks, states), F32),
            pltpu.SemaphoreType.DMA((2, groups)),
            pltpu.SemaphoreType.DMA((2, 4)),
            pltpu.SemaphoreType.DMA((2, groups)),
            pltpu.VMEM((heads, rows), F32),
            pltpu.SMEM((heads,), F32),
            pltpu.SMEM((heads,), F32),
            pltpu.SMEM(lengths.shape, lengths.dtype),
            pltpu.SemaphoreType.DMA((4,)),
            pltpu.VMEM((2, rows // ranks, groups, states), F32),
            pltpu.SemaphoreType.DMA((2,)),
            pltpu.SemaphoreType.DMA((2, pairs)),
            pltpu.SemaphoreType.DMA((2, pairs)),
            pltpu.SemaphoreType.DMA((2,)),
            pltpu.SemaphoreType.DMA((2,)),
            hop, hop, hop, hop,
            pltpu.SemaphoreType.DMA((2, pairs, 2)),
            pltpu.SemaphoreType.DMA((2, pairs, 2)),
            pltpu.SemaphoreType.DMA((pairs, 2)),
            pltpu.SemaphoreType.DMA((pairs, 2)),
        ]
    else:
        kernel = functools.partial(layer_kernel, peers, ranks, heads, groups)
        operands = (jnp.swapaxes(b_proj, 0, 1), jnp.swapaxes(c_proj, 0, 1))
        in_specs = [vmem] * 5 + [smem] * 3
        out_specs = (vmem,) * 5
        grads = (jax.ShapeDtypeStruct((rows // ranks, groups, states), F32),) * 2
        scratch = [
            pltpu.VMEM((heads, rows, LANES), F32),
            pltpu.VMEM((heads, rows, LANES), F32),
            pltpu.VMEM((heads, rows), F32),
            pltpu.VMEM((heads, rows), F32),
            carry, carry, carry, carry, carry, carry, carry, carry,
            pltpu.VMEM((groups, rows, LANES), F32),
            pltpu.VMEM((groups, rows, LANES), F32),
            pltpu.VMEM((rows, LANES), F32),
            pltpu.VMEM((rows, LANES), F32),
            pltpu.VMEM((heads, LANES), F32),
            pltpu.VMEM((heads, LANES), F32),
            pltpu.VMEM((groups, 2, rows, states), F32),
            pltpu.VMEM((hops, groups, 2, rows // ranks, states), F32),
            pltpu.VMEM((groups, 2, rows // ranks, states), F32),
            dma, dma, dma, dma,
            pltpu.SemaphoreType.DMA((max(ranks - 1, 4), groups)),
            pltpu.SemaphoreType.DMA((max(ranks - 1, 4), groups)),
            pltpu.SemaphoreType.DMA((2, groups)),
            pltpu.SemaphoreType.DMA((2, groups)),
        ]

    results = pl.pallas_call(
        kernel,
        out_shape=(
            jax.ShapeDtypeStruct((rows, width), BF16),
            jax.ShapeDtypeStruct((rows, width), BF16),
            jax.ShapeDtypeStruct((heads, rows), F32),
            *grads,
        ),
        in_specs=in_specs,
        out_specs=out_specs,
        scratch_shapes=scratch,
        compiler_params=pltpu.CompilerParams(
            collective_id=0, has_side_effects=True, vmem_limit_bytes=56 * 1024 * 1024
        ),
    )(
        inputs, cotangent, *operands, step_raw.T, skip_gain, decay_rate, lengths
    )
    if ranks == 4 and peers == 4 and groups == 2 * PAIRS:
        results = write_out(1, *results)
    y, dx, gs, db, dc = results
    return (y, dx, gs.T, db, dc)


def solution(mesh):
    rows = P(("dp", "seq"), "head")
    proj = P(("dp", "seq"), None, None)
    grads = P(("dp", "seq", "head"), None, None)
    return jax.shard_map(
        on_device,
        mesh=mesh,
        in_specs=(rows, rows, P("head"), P("head"), proj, proj, P("dp"), rows),
        out_specs=(rows, rows, rows, grads, grads),
        check_vma=False,
    )
```

```python
import functools

import jax
import jax.numpy as jnp
from jax import lax
from jax.experimental import pallas as pl
from jax.experimental.pallas import tpu as pltpu
from jax.sharding import PartitionSpec as P

BLOCK = 256
PREFIX_DEVS = 2
LANES = 128
PAIRS = 4
F32 = jnp.float32
BF16 = jnp.bfloat16
EXACT = lax.Precision.HIGHEST


def mm(a, b, ca, cb):
    return lax.dot_general(a, b, (((ca,), (cb,)), ((), ())), preferred_element_type=F32)


def layer_kernel(
    peers, ranks, heads, groups,
    x_ref, dy_ref, b_ref, c_ref, step_ref, gain_ref, decay_ref, lengths_ref,
    y_ref, dx_ref, gs_ref, db_out, dc_out,
    wi_b, dt_b, wi_t, dt_t, state, first_state, grad_own, later_grad,
    state_in, state_out, grad_in, grad_out, y_acc, dx_acc, q_acc, mask_b, gain_b, decay_b,
    parts, arrived, summed, fs_sem, fr_sem, bs_sem, br_sem, ps_sem, pr_sem, ss_sem, sr_sem,
):
    pos = lax.axis_index("seq")
    rank = lax.axis_index("head")
    prefix = jnp.where(pos < PREFIX_DEVS, 1.0, 0.0).astype(F32)
    rows = x_ref.shape[0]
    blocks = rows // BLOCK
    pairs = groups // 2
    half = groups * 64
    low = lax.broadcasted_iota(jnp.int32, (1, LANES), 1) < 64

    share = rows // ranks
    barrier = pltpu.get_barrier_semaphore()
    for away in range(1, ranks):
        pl.semaphore_signal(
            barrier, inc=1, device_id={"head": lax.rem(rank + away, ranks)},
            device_id_type=pl.DeviceIdType.MESH,
        )

    @pl.when(pos > 0)
    def _():
        pl.semaphore_signal(barrier, inc=1, device_id={"seq": pos - 1}, device_id_type=pl.DeviceIdType.MESH)

    @pl.when(pos < peers - 1)
    def _():
        pl.semaphore_signal(barrier, inc=1, device_id={"seq": pos + 1}, device_id_type=pl.DeviceIdType.MESH)

    tri = lax.broadcasted_iota(jnp.int32, (BLOCK, BLOCK), 0) >= lax.broadcasted_iota(
        jnp.int32, (BLOCK, BLOCK), 1
    )

    def span(k):
        return slice(k * BLOCK, (k + 1) * BLOCK)

    limit = jnp.where(pos < PREFIX_DEVS, rows, lengths_ref[jnp.maximum(pos - PREFIX_DEVS, 0)])
    ids = lax.broadcasted_iota(jnp.int32, (1, BLOCK), 1)
    for h in range(heads):
        gain_b[h : h + 1, :] = jnp.full((1, LANES), gain_ref[h], F32)
        decay_b[h : h + 1, :] = jnp.full((1, LANES), decay_ref[h], F32)
    rate = jnp.concatenate([decay_b[...]] * (BLOCK // LANES), axis=1)

    def kept(k):
        return jnp.where(ids + k * BLOCK < limit, 1.0, 0.0).astype(F32)

    for k in range(blocks):
        raw = step_ref[:, span(k)]
        keep = kept(k)
        step = (jnp.maximum(raw, 0.0) + jnp.log1p(jnp.exp(-jnp.abs(raw)))) * keep
        sums = lax.dot_general(
            -(step * rate), tri.astype(F32), (((1,), (1,)), ((), ())),
            preferred_element_type=F32, precision=EXACT,
        )
        wi_t[:, span(k)] = sums
        dt_t[:, span(k)] = step
        tall = jnp.concatenate(
            [step, sums, jnp.broadcast_to(keep, (LANES - 2 * heads, BLOCK))], axis=0
        ).T
        for h in range(heads):
            wi_b[h, span(k), :] = jnp.broadcast_to(tall[:, heads + h : heads + h + 1], (BLOCK, LANES))
            dt_b[h, span(k), :] = jnp.broadcast_to(tall[:, h : h + 1], (BLOCK, LANES))
        mask_b[span(k), :] = jnp.broadcast_to(tall[:, 2 * heads : 2 * heads + 1], (BLOCK, LANES))

    def turn(v):
        return pltpu.roll(v, 64, 1)

    def slabs(ref, p):
        lo = ref[:, pl.ds(pl.multiple_of(p * LANES, LANES), LANES)].astype(F32)
        hi = ref[:, pl.ds(pl.multiple_of(half + p * LANES, LANES), LANES)].astype(F32)
        return lo, hi

    def join(lo, hi):
        return jnp.where(low, lo, turn(hi)), jnp.where(low, turn(lo), hi)

    def by_head(ref, g, k):
        return jnp.where(low, ref[g, span(k), :], ref[groups + g, span(k), :])

    def total(g, k):
        at = pl.ds((k + 1) * BLOCK - 1, 1)
        return jnp.where(low, wi_b[g, at, :], wi_b[groups + g, at, :])

    def hop_f(p):
        part = pl.ds(2 * p, 2)
        return pltpu.make_async_remote_copy(
            src_ref=state_out.at[part], dst_ref=state_in.at[part],
            send_sem=fs_sem.at[p], recv_sem=fr_sem.at[p],
            device_id={"seq": pos + 1}, device_id_type=pl.DeviceIdType.MESH,
        )

    def hop_b(p):
        part = pl.ds(2 * p, 2)
        return pltpu.make_async_remote_copy(
            src_ref=grad_out.at[part], dst_ref=grad_in.at[part],
            send_sem=bs_sem.at[p], recv_sem=br_sem.at[p],
            device_id={"seq": pos - 1}, device_id_type=pl.DeviceIdType.MESH,
        )

    def give(g, away):
        to = lax.rem(rank + away, ranks)
        return pltpu.make_async_remote_copy(
            src_ref=parts.at[g, :, pl.ds(pl.multiple_of(to * share, share), share), :],
            dst_ref=arrived.at[away - 1, g],
            send_sem=ps_sem.at[away - 1, g], recv_sem=pr_sem.at[away - 1, g],
            device_id={"head": to}, device_id_type=pl.DeviceIdType.MESH,
        )

    def piece(g, kind, owner):
        return parts.at[g, kind, pl.ds(pl.multiple_of(owner * share, share), share), :]

    def flip(bit):
        low_bit = lax.rem(rank, 2)
        if bit == 1:
            return rank + 1 - 2 * low_bit
        if bit == 2:
            return lax.rem(rank + 2, 4)
        return lax.rem(rank + 2, 4) + 1 - 2 * low_bit

    def first_hop(g, kind, which):
        to = flip(kind + 1)
        return pltpu.make_async_remote_copy(
            src_ref=piece(g, kind, to if which == 0 else flip(3)),
            dst_ref=arrived.at[which, g, kind],
            send_sem=ps_sem.at[2 * kind + which, g], recv_sem=pr_sem.at[2 * kind + which, g],
            device_id={"head": to}, device_id_type=pl.DeviceIdType.MESH,
        )

    def second_hop(g, kind):
        to = flip(2 - kind)
        return pltpu.make_async_remote_copy(
            src_ref=piece(g, kind, to), dst_ref=summed.at[g, kind],
            send_sem=ss_sem.at[kind, g], recv_sem=sr_sem.at[kind, g],
            device_id={"head": to}, device_id_type=pl.DeviceIdType.MESH,
        )

    square = ranks == 4

    def send_group(g):
        if square:
            for which in (1, 0):
                for kind in range(2):
                    first_hop(g, kind, which).start()
        else:
            for away in range(1, ranks):
                give(g, away).start()

    def forward_group(g):
        if square:
            for kind in range(2):
                first_hop(g, kind, 1).wait_recv()
                at = pl.ds(pl.multiple_of(flip(2 - kind) * share, share), share)
                parts[g, kind, at, :] += arrived[1, g, kind]
                second_hop(g, kind).start()

    def collect_group(g):
        own = pl.ds(pl.multiple_of(rank * share, share), share)
        for kind, out in enumerate((db_out, dc_out)):
            val = parts[g, kind, own, :]
            if square:
                first_hop(g, kind, 0).wait_recv()
                second_hop(g, kind).wait_recv()
                val = val + arrived[0, g, kind] + summed[g, kind]
            else:
                if kind == 0:
                    for away in range(1, ranks):
                        give(g, away).wait_recv()
                for away in range(1, ranks):
                    val = val + arrived[away - 1, g, kind]
            out[:, g, :] = val

    def settle_group(g):
        if square:
            for kind in range(2):
                for which in range(2):
                    first_hop(g, kind, which).wait_send()
                second_hop(g, kind).wait_send()
        else:
            for away in range(1, ranks):
                give(g, away).wait_send()

    def whole(g):
        return jnp.exp(prefix * (total(g, 0) + total(g, 1)))

    def pass_f(p):
        for j in range(2):
            g = 2 * p + j
            state_out[g] = whole(g) * state_in[g] + prefix * state[g]
        hop_f(p).start()

    def pass_b(p):
        for j in range(2):
            g = 2 * p + j
            grad_out[g] = whole(g) * grad_in[g] + grad_own[g]
        hop_b(p).start()

    @pl.when(pos == 0)
    def _():
        state_in[...] = jnp.zeros_like(state_in)

    @pl.when(pos == peers - 1)
    def _():
        grad_in[...] = jnp.zeros_like(grad_in)

    @pl.when(jnp.logical_or(pos == 0, pos == peers - 1))
    def _():
        pl.semaphore_wait(barrier, ranks)

    @pl.when(jnp.logical_and(pos > 0, pos < peers - 1))
    def _():
        pl.semaphore_wait(barrier, ranks + 1)

    def local_states(p, carry):
        xs = join(*slabs(x_ref, p))
        dys = join(*slabs(dy_ref, p))
        for j in range(2):
            g = 2 * p + j
            adds, backs = [], []
            for k in range(blocks):
                wi = by_head(wi_b, g, k)
                dt = by_head(dt_b, g, k)
                scaled = (xs[j][span(k)] * (dt * jnp.exp(total(g, k) - wi))).astype(BF16)
                adds.append(mm(b_ref[g, span(k), :], scaled, 0, 0))
                lifted = (dys[j][span(k)] * mask_b[span(k), :] * jnp.exp(wi)).astype(BF16)
                backs.append(mm(c_ref[g, span(k), :], lifted, 0, 0))
            first_state[g] = adds[0]
            state[g] = jnp.exp(total(g, 1)) * adds[0] + adds[1]
            later_grad[g] = backs[1]
            grad_own[g] = backs[0] + jnp.exp(total(g, 0)) * backs[1]

        @pl.when(pos == 0)
        def _():
            pass_f(p)

        @pl.when(pos == peers - 1)
        def _():
            pass_b(p)

        return carry

    lax.fori_loop(0, pairs, local_states, 0)

    def inside(p):
        xs = join(*slabs(x_ref, p))
        dys = join(*slabs(dy_ref, p))
        for j in range(2):
            g = 2 * p + j
            for k in range(blocks):
                b_blk = b_ref[g, span(k), :]
                c_blk = c_ref[g, span(k), :]
                scores = mm(c_blk, b_blk, 1, 1)
                x16 = xs[j][span(k)].astype(BF16)
                dyf = dys[j][span(k)] * mask_b[span(k), :]
                dy16 = dyf.astype(BF16)
                ys, dxs = [], []
                d_scores = None
                for m in range(2):
                    h = m * groups + g
                    col = wi_b[h, span(k), :]
                    col = jnp.concatenate([col, col], axis=1)
                    row = wi_t[pl.ds(h, 1), span(k)]
                    decay = jnp.where(tri, jnp.exp(jnp.minimum(col - row, 0.0)), 0.0)
                    decay = decay * dt_t[pl.ds(h, 1), span(k)]
                    weights = (scores * decay).astype(BF16)
                    mine = low if m == 0 else jnp.logical_not(low)
                    dy_m = jnp.where(mine, dyf, 0.0).astype(BF16)
                    d_weights = mm(dy_m, x16, 1, 1) * decay
                    d_scores = d_weights if d_scores is None else d_scores + d_weights
                    ys.append(mm(weights, x16, 1, 0))
                    dxs.append(mm(weights, dy16, 0, 0))
                y_acc[g, span(k), :] = jnp.where(low, ys[0], ys[1])
                dx_acc[g, span(k), :] = jnp.where(low, dxs[0], dxs[1])
                ds16 = d_scores.astype(BF16)
                parts[g, 1, span(k), :] = mm(ds16, b_blk, 1, 0)
                parts[g, 0, span(k), :] = mm(ds16, c_blk, 0, 0)

    q_acc[...] = jnp.zeros_like(q_acc)
    last = lax.broadcasted_iota(jnp.int32, (BLOCK, 1), 0) == BLOCK - 1
    pick_row = lax.broadcasted_iota(jnp.int32, (4 * LANES, LANES), 0)
    pick_col = lax.broadcasted_iota(jnp.int32, (4 * LANES, LANES), 1)
    pick_head = (
        jnp.where(pick_row % LANES >= 64, groups, 0) + jnp.where(pick_row >= 2 * LANES, heads, 0)
    )

    def across(p):
        @pl.when(pos == peers - 1)
        def _():
            hop_f(p).wait_recv()

        @pl.when(pos == 0)
        def _():
            hop_b(p).wait_recv()

        xs = join(*slabs(x_ref, p))
        dys = join(*slabs(dy_ref, p))
        y_parts, dx_parts = [], []
        for j in range(2):
            g = 2 * p + j
            pick = (pick_col == pick_head + g).astype(BF16)
            gain = jnp.where(low, gain_b[pl.ds(g, 1), :], gain_b[pl.ds(groups + g, 1), :])
            start = state_in[g]
            carry_grad = prefix * grad_in[g]
            entered = (start, jnp.exp(total(g, 0)) * start + first_state[g])
            leaving = (later_grad[g] + jnp.exp(total(g, 1)) * carry_grad, carry_grad)
            y_rows, dx_rows = [], []
            for k in range(blocks):
                wi = by_head(wi_b, g, k)
                dt = by_head(dt_b, g, k)
                end = total(g, k)
                up = jnp.exp(wi)
                down = dt * jnp.exp(end - wi)
                e16 = entered[k].astype(BF16)
                g16 = leaving[k].astype(BF16)
                x = xs[j][span(k)]
                mask = mask_b[span(k), :]
                dy = dys[j][span(k)] * mask
                b_blk = b_ref[g, span(k), :]
                c_blk = c_ref[g, span(k), :]
                y = y_acc[g, span(k), :] + up * mm(c_blk, e16, 1, 0)
                dx_s = down * mm(b_blk, g16, 1, 0)
                dx = dx_acc[g, span(k), :] + dx_s
                parts[g, 1, span(k), :] += mm((dy * up).astype(BF16), e16, 1, 1)
                parts[g, 0, span(k), :] += mm((x * down).astype(BF16), g16, 1, 1)
                q2 = x * dx
                extra = jnp.sum(x * dx_s, axis=0, keepdims=True) + jnp.exp(end) * jnp.sum(
                    leaving[k] * entered[k], axis=0, keepdims=True
                )
                q1 = dy * y - q2 + jnp.where(last, extra, 0.0)
                q1h = q1.astype(BF16)
                q2h = q2.astype(BF16)
                q1l = (q1 - q1h.astype(F32)).astype(BF16)
                q2l = (q2 - q2h.astype(F32)).astype(BF16)
                q_acc[span(k), :] += mm(jnp.concatenate([q1h, q1l, q2h, q2l], axis=1), pick, 1, 0)
                y_rows.append((y + gain * x) * mask)
                dx_rows.append(dx + gain * dy)
            send_group(g)
            y_parts.append(jnp.concatenate(y_rows, axis=0))
            dx_parts.append(jnp.concatenate(dx_rows, axis=0))
        for ref, pair in ((y_ref, y_parts), (dx_ref, dx_parts)):
            lo, hi = join(*pair)
            ref[:, pl.ds(pl.multiple_of(p * LANES, LANES), LANES)] = lo.astype(BF16)
            ref[:, pl.ds(pl.multiple_of(half + p * LANES, LANES), LANES)] = hi.astype(BF16)

    lag = max(1, peers - 3)
    middle = jnp.logical_and(pos > 0, pos < peers - 1)

    def stage(s, carry):
        pf = s - (pos - 1)
        pb = s - (peers - 2 - pos)

        @pl.when(jnp.logical_and(middle, jnp.logical_and(pf >= 0, pf < pairs)))
        def _():
            hop_f(pf).wait_recv()
            pass_f(pf)

        @pl.when(jnp.logical_and(middle, jnp.logical_and(pb >= 0, pb < pairs)))
        def _():
            hop_b(pb).wait_recv()
            pass_b(pb)

        @pl.when(s < pairs)
        def _():
            inside(s)

        @pl.when(jnp.logical_and(s >= lag, s < pairs + lag))
        def _():
            across(s - lag)

        @pl.when(jnp.logical_and(s > lag, s < pairs + lag))
        def _():
            for j in range(2):
                forward_group(2 * (s - lag - 1) + j)

        return carry

    lax.fori_loop(0, pairs + lag, stage, 0)
    for g in range(groups - 2, groups):
        forward_group(g)

    for k in range(blocks):
        q = q_acc[span(k), :].T
        step = dt_t[:, span(k)]
        d_log = lax.dot_general(
            q[:heads], tri.astype(F32), (((1,), (0,)), ((), ())),
            preferred_element_type=F32, precision=EXACT,
        )
        slope = jax.nn.sigmoid(step_ref[:, span(k)]) * kept(k)
        safe = jnp.where(step > 0.0, step, 1.0)
        gs_ref[:, span(k)] = slope * (q[heads : 2 * heads] / safe - rate * d_log)

    for g in range(groups):
        collect_group(g)
    for g in range(groups):
        settle_group(g)

    def finish(p, carry):
        @pl.when(pos < peers - 1)
        def _():
            hop_f(p).wait_send()

        @pl.when(pos > 0)
        def _():
            hop_b(p).wait_send()

        return carry

    lax.fori_loop(0, pairs, finish, 0)


def paired_kernel(
    peers, heads, groups,
    x_hbm, dy_hbm, b_hbm, c_hbm, step_hbm, gain_hbm, decay_hbm, lengths_hbm,
    y_hbm, dx_hbm, gs_ref, grads_hbm,
    x_in, dy_in, b_in, c_in, b_ref, c_ref, wide, wi_c, dt_c, wd_t, told, wd_f, xj, dyj,
    state, first_state, grad_own, later_grad, state_in, grad_in,
    y_acc, dx_acc, q_acc, mask_b, gain_b, decay_b, parts, arrived, summed,
    in_sem, bc_sem, out_sem, step_ref, gain_ref, decay_ref, lengths_ref, few_sem, grads, grads_sem, xs_sem, xr_sem, ws_sem, wr_sem, fs_sem, fr_sem, bs_sem, br_sem, ps_sem, pr_sem, ss_sem, sr_sem,
):
    ranks = 4
    pos = lax.axis_index("seq")
    rank = lax.axis_index("head")
    bit_x = lax.rem(rank, 2)
    bit_y = rank // 2
    prefix = jnp.where(pos < PREFIX_DEVS, 1.0, 0.0).astype(F32)
    rows = x_in.shape[0]
    blocks = rows // BLOCK
    pairs = groups // 2
    share = rows // ranks
    zero_unit = groups + pairs
    low = lax.broadcasted_iota(jnp.int32, (1, LANES), 1) < 64
    mesh_id = pl.DeviceIdType.MESH

    def bit(par):
        return (1 - par) * bit_x + par * bit_y

    def beside(par):
        return rank + (1 - par) * (1 - 2 * bit_x) + 2 * par * (1 - 2 * bit_y)

    def mine(p):
        return 2 * p + bit(p % 2)

    def given(p):
        return 2 * p + 1 - bit(p % 2)

    def slab(i):
        return pl.ds(pl.multiple_of(i * LANES, LANES), LANES)

    def fetch(i, which):
        src, dst = ((x_hbm, x_in), (dy_hbm, dy_in))[which]
        at = slice(2 * i * LANES, (2 * i + 2) * LANES)
        return pltpu.make_async_copy(src.at[:, at], dst.at[:, at], in_sem.at[which, i])

    def leave(i, which):
        src, dst = ((x_in, y_hbm), (dy_in, dx_hbm))[which]
        return pltpu.make_async_copy(src.at[:, slab(i)], dst.at[:, slab(i)], out_sem.at[which, i])

    def leave_grads(kind):
        return pltpu.make_async_copy(grads.at[kind], grads_hbm.at[kind], grads_sem.at[kind])

    few = [
        pltpu.make_async_copy(src, dst, few_sem.at[i])
        for i, (src, dst) in enumerate(
            ((lengths_hbm, lengths_ref), (gain_hbm, gain_ref), (decay_hbm, decay_ref), (step_hbm, step_ref))
        )
    ]

    chunk = b_in.shape[1]
    chunks = rows // chunk

    def fetch_proj(i, which):
        src, dst = ((b_hbm, b_in), (c_hbm, c_in))[which]
        at = pl.ds(pl.multiple_of(i * chunk, chunk), chunk)
        return pltpu.make_async_copy(src.at[at], dst.at[i % 2], bc_sem.at[which, i])

    def fetch_pairs(t, which):
        return [fetch(i, which) for i in (t, pairs // 2 + t)]

    for copy in fetch_pairs(0, 0):
        copy.start()
    barrier = pltpu.get_barrier_semaphore()
    for par in range(2):
        pl.semaphore_signal(barrier, inc=1, device_id={"head": beside(par)}, device_id_type=mesh_id)

    @pl.when(pos > 0)
    def _():
        pl.semaphore_signal(barrier, inc=1, device_id={"seq": pos - 1}, device_id_type=mesh_id)

    @pl.when(pos < peers - 1)
    def _():
        pl.semaphore_signal(barrier, inc=1, device_id={"seq": pos + 1}, device_id_type=mesh_id)

    def span(k):
        return slice(k * BLOCK, (k + 1) * BLOCK)

    tri = lax.broadcasted_iota(jnp.int32, (BLOCK, BLOCK), 0) >= lax.broadcasted_iota(
        jnp.int32, (BLOCK, BLOCK), 1
    )
    ids = lax.broadcasted_iota(jnp.int32, (1, BLOCK), 1)
    tall_ids = lax.broadcasted_iota(jnp.int32, (BLOCK, LANES), 0)

    def turn(v):
        return pltpu.roll(v, 64, 1)

    def join(lo, hi):
        return jnp.where(low, lo, turn(hi)), jnp.where(low, turn(lo), hi)

    def copy_of(src, dst, send, recv, where):
        return pltpu.make_async_remote_copy(
            src_ref=src, dst_ref=dst, send_sem=send, recv_sem=recv, device_id=where, device_id_type=mesh_id
        )

    def raw(p, which):
        ref = (xj, dyj)[which]
        return copy_of(
            ref.at[given(p)], ref.at[groups + p], xs_sem.at[which, p], xr_sem.at[which, p], {"head": beside(p % 2)}
        )

    def tell(par):
        return copy_of(told.at[par], wd_f.at[par], ws_sem.at[par], wr_sem.at[par], {"head": beside(par)})

    def told_row(kind, p, m):
        at = pairs * kind + 2 * (p // 2) + m
        return slice(at, at + 1)

    def hop_f(u):
        return copy_of(state.at[u], state_in.at[u], fs_sem.at[u], fr_sem.at[u], {"seq": pos + 1})

    def hop_b(u):
        return copy_of(grad_own.at[u], grad_in.at[u], bs_sem.at[u], br_sem.at[u], {"seq": pos - 1})

    def piece(p, kind, owner):
        return parts.at[p, kind, pl.ds(pl.multiple_of(owner * share, share), share), :]

    def first_hop(p, kind, which):
        par = p % 2
        to = beside(1 - par)
        opposite = 3 - rank
        return copy_of(
            piece(p, kind, to if which == 0 else opposite), arrived.at[which, p, kind],
            ps_sem.at[which, p, kind], pr_sem.at[which, p, kind], {"head": to},
        )

    def second_hop(p, kind):
        to = beside(p % 2)
        return copy_of(
            piece(p, kind, to), summed.at[p, kind], ss_sem.at[p, kind], sr_sem.at[p, kind], {"head": to}
        )

    def spread(p, which):
        src, dst = ((x_in, xj), (dy_in, dyj))[which]
        lo, hi = src[:, slab(p)].astype(F32), src[:, slab(pairs + p)].astype(F32)
        if which == 1:
            lo, hi = lo * mask_b[...], hi * mask_b[...]
        dst[2 * p], dst[2 * p + 1] = join(lo, hi)

    few[0].start()
    for copy in fetch_pairs(0, 1) + few[1:] + fetch_pairs(1, 0) + fetch_pairs(1, 1):
        copy.start()
    for i in range(2):
        for which in range(2):
            fetch_proj(i, which).start()
    for copy in fetch_pairs(0, 0):
        copy.wait()
    spread(0, 0)

    @pl.when(jnp.logical_or(pos == 0, pos == peers - 1))
    def _():
        pl.semaphore_wait(barrier, 3)

    @pl.when(jnp.logical_and(pos > 0, pos < peers - 1))
    def _():
        pl.semaphore_wait(barrier, 4)

    raw(0, 0).start()
    spread(1, 0)
    raw(1, 0).start()
    few[0].wait()
    limit = jnp.where(pos < PREFIX_DEVS, rows, lengths_ref[jnp.maximum(pos - PREFIX_DEVS, 0)])
    for k in range(blocks):
        mask_b[span(k), :] = jnp.where(tall_ids + k * BLOCK < limit, 1.0, 0.0).astype(F32)
    for copy in fetch_pairs(0, 1):
        copy.wait()
    for p in range(2):
        spread(p, 1)
        raw(p, 1).start()
    for copy in few[1:]:
        copy.wait()

    def kept(k):
        return jnp.where(ids + k * BLOCK < limit, 1.0, 0.0).astype(F32)

    for h in range(heads):
        gain_b[h : h + 1, :] = jnp.full((1, LANES), gain_ref[h], F32)
        decay_b[h : h + 1, :] = jnp.full((1, LANES), decay_ref[h], F32)
    rate = jnp.concatenate([decay_b[...]] * (BLOCK // LANES), axis=1)
    for k in range(blocks):
        step_in = step_ref[:, span(k)]
        step = (jnp.maximum(step_in, 0.0) + jnp.log1p(jnp.exp(-jnp.abs(step_in)))) * kept(k)
        sums = lax.dot_general(
            -(step * rate), tri.astype(F32), (((1,), (1,)), ((), ())),
            preferred_element_type=F32, precision=EXACT,
        )
        wd_t[0, :, span(k)] = sums
        wd_t[1, :, span(k)] = step
    for par in range(2):
        for kind in range(2):
            for p in range(par, pairs, 2):
                for m in range(2):
                    told[par, told_row(kind, p, m), :] = wd_t[kind, pl.ds(m * groups + given(p), 1), :]
        tell(par).start()
    for copy in fetch_pairs(1, 0) + fetch_pairs(1, 1):
        copy.wait()
    for p in range(2, pairs):
        for which in range(2):
            spread(p, which)
            raw(p, which).start()
    state_in[zero_unit] = jnp.zeros_like(state_in[zero_unit])
    grad_in[zero_unit] = jnp.zeros_like(grad_in[zero_unit])

    def loop(start, stop, body):
        def step(i, carry):
            body(i)
            return carry

        lax.fori_loop(start, stop, step, 0)

    def columns(row_of, u):
        for kind, ref in ((0, wi_c), (1, dt_c)):
            for k in range(blocks):
                cols = [jnp.broadcast_to(row_of(kind, m, span(k)), (64, BLOCK)) for m in range(2)]
                ref[u, span(k), :] = jnp.concatenate(cols, axis=0).T

    def group_first(i):
        at = pl.ds(pl.multiple_of(i * chunk, chunk), chunk)
        for which, (src, dst) in enumerate(((b_in, b_ref), (c_in, c_ref))):
            fetch_proj(i, which).wait()
            flat = src[i % 2].astype(F32).reshape(chunk * groups, src.shape[3])
            for n in range(src.shape[3] // LANES):
                cut = slice(n * LANES, (n + 1) * LANES)
                wide[n] = flat[:, cut]
                for g in range(groups):
                    dst[g, at, cut] = wide[n, pl.ds(g, chunk, stride=groups), :].astype(BF16)

        @pl.when(i + 2 < chunks)
        def _():
            for which in range(2):
                fetch_proj(i + 2, which).start()

    loop(0, chunks, group_first)
    loop(0, groups, lambda g: columns(lambda kind, m, cut: wd_t[kind, pl.ds(m * groups + g, 1), cut], g))

    class Part:
        def __init__(self, unit, group):
            self.unit, self.group = unit, group

        def x(self, k):
            return xj[self.unit, span(k), :]

        def dy(self, k):
            return dyj[self.unit, span(k), :]

        def within(self, k):
            return wi_c[self.unit, span(k), :]

        def step(self, k):
            return dt_c[self.unit, span(k), :]

        def total(self, k):
            return wi_c[self.unit, pl.ds((k + 1) * BLOCK - 1, 1), :]

    def own_part(g):
        return Part(g, g)

    def handed_part(p):
        return Part(groups + p, mine(p))

    def whole(part):
        return jnp.exp(prefix * (part.total(0) + part.total(1)))

    def start_of(u):
        return state_in[jnp.where(pos > 0, u, zero_unit)]

    def carry_of(u):
        return grad_in[jnp.where(pos < PREFIX_DEVS, u, zero_unit)]

    def entered_by(part):
        start = start_of(part.unit)
        return start, jnp.exp(part.total(0)) * start + first_state[part.unit]

    def leaving_by(part):
        carry = carry_of(part.unit)
        return later_grad[part.unit] + jnp.exp(part.total(1)) * carry, carry

    def pass_f(part):
        u = part.unit
        state[u] = whole(part) * start_of(u) + prefix * state[u]
        hop_f(u).start()

    def pass_b(part):
        u = part.unit
        held = grad_in[jnp.where(pos < peers - 1, u, zero_unit)]
        grad_own[u] = whole(part) * held + grad_own[u]
        hop_b(u).start()

    def emit(part):
        @pl.when(pos == 0)
        def _():
            pass_f(part)

        @pl.when(pos == peers - 1)
        def _():
            pass_b(part)

    def relay_f(unit):
        hop_f(unit).wait_recv()

        @pl.when(pos < peers - 1)
        def _():
            pass_f(Part(unit, 0))

    def relay_b(unit):
        hop_b(unit).wait_recv()

        @pl.when(pos > 0)
        def _():
            pass_b(Part(unit, 0))

    order = [mine(0), mine(1), mine(2), groups, groups + 1, mine(3), given(0), groups + 2, groups + 3]
    order += [given(1), given(2), given(3)]

    def unit_at(i):
        unit = order[0]
        for k in range(1, len(order)):
            unit = jnp.where(i == k, order[k], unit)
        return unit

    served = [(0, 0, 0)]

    def serve(*upto):
        before = served[-1]
        served.append(upto)

        def count(marks, hops):
            marked = [jnp.where(hops == d + 1, marks[d], 0) for d in range(3)]
            return marked[0] + marked[1] + marked[2]

        for hops, how in ((pos, relay_f), (peers - 1 - pos, relay_b)):
            loop(count(before, hops), count(upto, hops), lambda i: how(unit_at(i)))

    def local_states(part):
        u, g = part.unit, part.group
        adds, backs = [], []
        for k in range(blocks):
            wi = part.within(k)
            scaled = (part.x(k) * (part.step(k) * jnp.exp(part.total(k) - wi))).astype(BF16)
            adds.append(mm(b_ref[g, span(k), :], scaled, 0, 0))
            lifted = (part.dy(k) * jnp.exp(wi)).astype(BF16)
            backs.append(mm(c_ref[g, span(k), :], lifted, 0, 0))
        first_state[u] = adds[0]
        state[u] = jnp.exp(part.total(1)) * adds[0] + adds[1]
        later_grad[u] = backs[1]
        grad_own[u] = backs[0] + jnp.exp(part.total(0)) * backs[1]

    def decay_by(row, dt_row):
        col = jnp.broadcast_to(row, (LANES, BLOCK)).T
        col = jnp.concatenate([col, col], axis=1)
        return jnp.where(tri, jnp.exp(jnp.minimum(col - row, 0.0)), 0.0) * dt_row

    def only(m, v):
        return jnp.where(low if m == 0 else jnp.logical_not(low), v, 0.0).astype(BF16)

    def inside(p, g, with_scores):
        for k in range(blocks):
            scores = mm(c_ref[g, span(k), :], b_ref[g, span(k), :], 1, 1)
            x16 = xj[g, span(k), :].astype(BF16)
            dyf = dyj[g, span(k), :]
            dy16 = dyf.astype(BF16)
            ys, dxs, d_scores = [], [], None
            for m in range(2):
                h = m * groups + g
                decay = decay_by(wd_t[0, pl.ds(h, 1), span(k)], wd_t[1, pl.ds(h, 1), span(k)])
                weights = (scores * decay).astype(BF16)
                if with_scores:
                    d_weights = mm(only(m, dyf), x16, 1, 1) * decay
                    d_scores = d_weights if d_scores is None else d_scores + d_weights
                ys.append(mm(weights, x16, 1, 0))
                dxs.append(mm(weights, dy16, 0, 0))
            y_acc[g, span(k), :] = jnp.where(low, ys[0], ys[1])
            dx_acc[g, span(k), :] = jnp.where(low, dxs[0], dxs[1])
            if with_scores:
                parts[p, 0, span(k), :] = d_scores

    def handed_scores(p):
        g = mine(p)
        for k in range(blocks):
            x16 = xj[groups + p, span(k), :].astype(BF16)
            dyf = dyj[groups + p, span(k), :]
            d_scores = parts[p, 0, span(k), :]
            for m in range(2):
                row, dt_row = (wd_f[p % 2, told_row(kind, p, m), span(k)] for kind in range(2))
                decay = decay_by(row, dt_row)
                d_scores = d_scores + mm(only(m, dyf), x16, 1, 1) * decay
            ds16 = d_scores.astype(BF16)
            parts[p, 1, span(k), :] = mm(ds16, b_ref[g, span(k), :], 1, 0)
            parts[p, 0, span(k), :] = mm(ds16, c_ref[g, span(k), :], 0, 0)

    def grow_c(p):
        both = (own_part(mine(p)), handed_part(p))
        entered = [entered_by(part) for part in both]
        for k in range(blocks):
            e16 = jnp.concatenate([e[k].astype(BF16) for e in entered], axis=1)
            lifted = jnp.concatenate(
                [(part.dy(k) * jnp.exp(part.within(k))).astype(BF16) for part in both], axis=1
            )
            parts[p, 1, span(k), :] += mm(lifted, e16, 1, 1)

    def grow_b(p):
        both = (own_part(mine(p)), handed_part(p))
        leaving = [leaving_by(part) for part in both]
        for k in range(blocks):
            g16 = jnp.concatenate([v[k].astype(BF16) for v in leaving], axis=1)
            scaled = jnp.concatenate(
                [
                    (part.x(k) * (part.step(k) * jnp.exp(part.total(k) - part.within(k)))).astype(BF16)
                    for part in both
                ],
                axis=1,
            )
            parts[p, 0, span(k), :] += mm(scaled, g16, 1, 1)

    early_kind = jnp.where(pos < PREFIX_DEVS, 1, 0)
    late_kind = 1 - early_kind

    def send(p, kind):
        for which in (1, 0):
            first_hop(p, kind, which).start()

    def early(p):
        @pl.when(pos < PREFIX_DEVS)
        def _():
            grow_c(p)

        @pl.when(pos >= PREFIX_DEVS)
        def _():
            grow_b(p)

        send(p, early_kind)

    def late(p):
        @pl.when(pos < PREFIX_DEVS)
        def _():
            grow_b(p)

        @pl.when(pos >= PREFIX_DEVS)
        def _():
            grow_c(p)

        send(p, late_kind)

    def forward(p, kind):
        first_hop(p, kind, 1).wait_recv()
        at = pl.ds(pl.multiple_of(beside(p % 2) * share, share), share)
        parts[p, kind, at, :] += arrived[1, p, kind]
        second_hop(p, kind).start()

    def receive(p):
        for which in range(2):
            raw(p, which).wait_recv()
        columns(lambda kind, m, cut: wd_f[p % 2, told_row(kind, p, m), cut], groups + p)
        part = handed_part(p)
        local_states(part)
        emit(part)
        handed_scores(p)

    last = lax.broadcasted_iota(jnp.int32, (BLOCK, 1), 0) == BLOCK - 1
    pick_row = lax.broadcasted_iota(jnp.int32, (4 * LANES, LANES), 0)
    pick_col = lax.broadcasted_iota(jnp.int32, (4 * LANES, LANES), 1)
    pick_head = (
        jnp.where(pick_row % LANES >= 64, groups, 0) + jnp.where(pick_row >= 2 * LANES, heads, 0)
    )

    def across(p):
        y_parts, dx_parts = [], []
        for j in range(2):
            g = 2 * p + j
            part = own_part(g)
            pick = (pick_col == pick_head + g).astype(BF16)
            gain = jnp.where(low, gain_b[pl.ds(g, 1), :], gain_b[pl.ds(groups + g, 1), :])
            entered = entered_by(part)
            leaving = leaving_by(part)
            y_rows, dx_rows = [], []
            for k in range(blocks):
                wi = part.within(k)
                end = part.total(k)
                up = jnp.exp(wi)
                down = part.step(k) * jnp.exp(end - wi)
                x = part.x(k)
                dy = part.dy(k)
                y = y_acc[g, span(k), :] + up * mm(c_ref[g, span(k), :], entered[k].astype(BF16), 1, 0)
                dx_s = down * mm(b_ref[g, span(k), :], leaving[k].astype(BF16), 1, 0)
                dx = dx_acc[g, span(k), :] + dx_s
                q2 = x * dx
                extra = jnp.sum(x * dx_s, axis=0, keepdims=True) + jnp.exp(end) * jnp.sum(
                    leaving[k] * entered[k], axis=0, keepdims=True
                )
                q1 = dy * y - q2 + jnp.where(last, extra, 0.0)
                q1h = q1.astype(BF16)
                q2h = q2.astype(BF16)
                q1l = (q1 - q1h.astype(F32)).astype(BF16)
                q2l = (q2 - q2h.astype(F32)).astype(BF16)
                q_acc[span(k), :] += mm(jnp.concatenate([q1h, q1l, q2h, q2l], axis=1), pick, 1, 0)
                y_rows.append((y + gain * x) * mask_b[span(k), :])
                dx_rows.append(dx + gain * dy)
            y_parts.append(jnp.concatenate(y_rows, axis=0))
            dx_parts.append(jnp.concatenate(dx_rows, axis=0))
        for which, (ref, pair) in enumerate(((x_in, y_parts), (dy_in, dx_parts))):
            lo, hi = join(*pair)
            ref[:, slab(p)] = lo.astype(BF16)
            ref[:, slab(pairs + p)] = hi.astype(BF16)
            for i in (p, pairs + p):
                leave(i, which).start()

    def finish_steps():
        for k in range(blocks):
            q = q_acc[span(k), :].T
            step = wd_t[1, :, span(k)]
            d_log = lax.dot_general(
                q[:heads], tri.astype(F32), (((1,), (0,)), ((), ())),
                preferred_element_type=F32, precision=EXACT,
            )
            slope = jax.nn.sigmoid(step_ref[:, span(k)]) * kept(k)
            safe = jnp.where(step > 0.0, step, 1.0)
            gs_ref[:, span(k)] = slope * (q[heads : 2 * heads] / safe - rate * d_log)

    def begin(p):
        local_states(own_part(mine(p)))

        @pl.when(p < pairs - 1)
        def _():
            emit(own_part(mine(p)))

    def kept_blocks(p):
        inside(p, mine(p), True)

    def given_blocks(p):
        local_states(own_part(given(p)))
        inside(p, given(p), False)

    own = pl.ds(pl.multiple_of(rank * share, share), share)

    def collect(p, kind):
        first_hop(p, kind, 0).wait_recv()
        second_hop(p, kind).wait_recv()
        kept_sum = parts[p, kind, own, :] + arrived[0, p, kind]
        other = summed[p, kind]
        first = bit(p % 2) == 0
        grads[kind, :, 2 * p, :] = jnp.where(first, kept_sum, other)
        grads[kind, :, 2 * p + 1, :] = jnp.where(first, other, kept_sum)

    q_acc[...] = jnp.zeros_like(q_acc)
    loop(0, pairs, begin)
    loop(0, pairs, kept_blocks)
    for par in range(2):
        tell(par).wait_recv()
    serve(1, 0, 0)
    receive(0)
    serve(2, 0, 0)
    receive(1)
    emit(own_part(mine(3)))
    serve(3, 1, 0)
    given_blocks(0)
    emit(own_part(given(0)))
    serve(4, 2, 0)
    early(0)
    given_blocks(1)
    serve(5, 3, 1)
    early(1)
    given_blocks(2)
    serve(6, 4, 2)
    receive(2)
    serve(6, 5, 3)
    receive(3)
    for p in (1, 2):
        emit(own_part(given(p)))
    serve(8, 6, 4)
    early(2)
    forward(0, early_kind)
    serve(9, 6, 4)
    early(3)
    forward(1, early_kind)
    serve(9, 7, 5)
    late(0)
    late(1)
    given_blocks(3)
    emit(own_part(given(3)))
    serve(10, 8, 6)
    forward(2, early_kind)
    forward(3, early_kind)
    serve(11, 9, 8)
    late(2)
    serve(12, 10, 9)
    late(3)
    forward(0, late_kind)
    forward(1, late_kind)
    across(0)
    serve(12, 11, 10)
    across(1)
    serve(12, 12, 11)
    across(2)
    serve(12, 12, 12)
    forward(2, late_kind)
    forward(3, late_kind)
    across(3)
    finish_steps()
    for kind in (early_kind, late_kind):
        for p in range(pairs):
            collect(p, kind)
        leave_grads(kind).start()

    for kind in range(2):
        leave_grads(kind).wait()
    for par in range(2):
        tell(par).wait_send()
    for which in range(2):
        for i in range(2 * pairs):
            leave(i, which).wait()
    def settle(p):
        for kind in range(2):
            raw(p, kind).wait_send()
            for which in range(2):
                first_hop(p, kind, which).wait_send()
            second_hop(p, kind).wait_send()

    loop(0, pairs, settle)

    def finish(u):
        @pl.when(pos < peers - 1)
        def _():
            hop_f(u).wait_send()

        @pl.when(pos > 0)
        def _():
            hop_b(u).wait_send()

    loop(0, groups + pairs, finish)


def writing_kernel(pieces, y_hbm, dx_hbm, gs_hbm, grads, *refs):
    sources = (y_hbm, dx_hbm, gs_hbm, grads.at[0], grads.at[1])
    count = len(sources)
    targets, held, (in_sem, out_sem) = refs[:count], refs[count : 2 * count], refs[2 * count :]
    arrive, onward = [], []
    for i in range(count):
        cuts = pieces if i != 2 else 1
        for n in range(cuts):
            part = held[i].shape[0] // cuts
            at = pl.ds(n * part, part)
            arrive.append(pltpu.make_async_copy(sources[i].at[at], held[i].at[at], in_sem.at[i, n]))
            onward.append(pltpu.make_async_copy(held[i].at[at], targets[i].at[at], out_sem.at[i, n]))
    for copy in arrive:
        copy.start()
    for copy, after in zip(arrive, onward):
        copy.wait()
        after.start()
    for copy in onward:
        copy.wait()


def write_out(pieces, y, dx, gs, grads):
    anywhere = pl.BlockSpec(memory_space=pl.ANY)
    shapes = [(v.shape, v.dtype) for v in (y, dx, gs)] + [(grads.shape[1:], grads.dtype)] * 2
    sems = pltpu.SemaphoreType.DMA((len(shapes), pieces))
    return pl.pallas_call(
        functools.partial(writing_kernel, pieces),
        out_shape=tuple(jax.ShapeDtypeStruct(*shape) for shape in shapes),
        in_specs=[anywhere] * 4,
        out_specs=(anywhere,) * len(shapes),
        scratch_shapes=[pltpu.VMEM(*shape) for shape in shapes] + [sems, sems],
        compiler_params=pltpu.CompilerParams(vmem_limit_bytes=56 * 1024 * 1024),
    )(y, dx, gs, grads)


def on_device(inputs, step_raw, decay_rate, skip_gain, b_proj, c_proj, lengths, cotangent):
    rows, width = inputs.shape
    heads = decay_rate.shape[0]
    groups, states = b_proj.shape[1:]
    peers = lax.axis_size("seq")
    ranks = lax.axis_size("head")
    hops = 2 if ranks == 4 else ranks - 1
    vmem = pl.BlockSpec(memory_space=pltpu.VMEM)
    smem = pl.BlockSpec(memory_space=pltpu.SMEM)
    carry = pltpu.VMEM((groups, states, LANES), F32)
    dma = pltpu.SemaphoreType.DMA((groups // 2,))

    if ranks == 4 and peers == 4 and groups == 2 * PAIRS:
        pairs = groups // 2
        units = pltpu.VMEM((groups + pairs, states, LANES), F32)
        arriving = pltpu.VMEM((groups + pairs + 1, states, LANES), F32)
        per_group = pltpu.VMEM((groups, rows, LANES), F32)
        per_unit = pltpu.VMEM((groups + pairs, rows, LANES), F32)
        wide_rows = pltpu.VMEM((rows, width), BF16)
        proj = pltpu.VMEM((2, rows // 4, groups, states), BF16)
        lead = pltpu.VMEM((groups, rows, states), BF16)
        hop = pltpu.SemaphoreType.DMA((groups + pairs,))
        kernel = functools.partial(paired_kernel, peers, heads, groups)
        operands = (b_proj, c_proj)
        big = pl.BlockSpec(memory_space=pl.ANY)
        in_specs = [big] * 8
        out_specs = (big, big, vmem, big)
        grads = (jax.ShapeDtypeStruct((2, rows // ranks, groups, states), F32),)
        scratch = [
            wide_rows, wide_rows, proj, proj, lead, lead,
            pltpu.VMEM((states // LANES, rows // 4 * groups, LANES), F32),
            per_unit, per_unit,
            pltpu.VMEM((2, heads, rows), F32),
            pltpu.VMEM((2, groups, rows), F32),
            pltpu.VMEM((2, groups, rows), F32),
            per_unit, per_unit,
            units, units, units, units, arriving, arriving,
            per_group, per_group,
            pltpu.VMEM((rows, LANES), F32),
            pltpu.VMEM((rows, LANES), F32),
            pltpu.VMEM((heads, LANES), F32),
            pltpu.VMEM((heads, LANES), F32),
            pltpu.VMEM((pairs, 2, rows, states), F32),
            pltpu.VMEM((2, pairs, 2, rows // ranks, states), F32),
            pltpu.VMEM((pairs, 2, rows // ranks, states), F32),
            pltpu.SemaphoreType.DMA((2, groups)),
            pltpu.SemaphoreType.DMA((2, 4)),
            pltpu.SemaphoreType.DMA((2, groups)),
            pltpu.VMEM((heads, rows), F32),
            pltpu.SMEM((heads,), F32),
            pltpu.SMEM((heads,), F32),
            pltpu.SMEM(lengths.shape, lengths.dtype),
            pltpu.SemaphoreType.DMA((4,)),
            pltpu.VMEM((2, rows // ranks, groups, states), F32),
            pltpu.SemaphoreType.DMA((2,)),
            pltpu.SemaphoreType.DMA((2, pairs)),
            pltpu.SemaphoreType.DMA((2, pairs)),
            pltpu.SemaphoreType.DMA((2,)),
            pltpu.SemaphoreType.DMA((2,)),
            hop, hop, hop, hop,
            pltpu.SemaphoreType.DMA((2, pairs, 2)),
            pltpu.SemaphoreType.DMA((2, pairs, 2)),
            pltpu.SemaphoreType.DMA((pairs, 2)),
            pltpu.SemaphoreType.DMA((pairs, 2)),
        ]
    else:
        kernel = functools.partial(layer_kernel, peers, ranks, heads, groups)
        operands = (jnp.swapaxes(b_proj, 0, 1), jnp.swapaxes(c_proj, 0, 1))
        in_specs = [vmem] * 5 + [smem] * 3
        out_specs = (vmem,) * 5
        grads = (jax.ShapeDtypeStruct((rows // ranks, groups, states), F32),) * 2
        scratch = [
            pltpu.VMEM((heads, rows, LANES), F32),
            pltpu.VMEM((heads, rows, LANES), F32),
            pltpu.VMEM((heads, rows), F32),
            pltpu.VMEM((heads, rows), F32),
            carry, carry, carry, carry, carry, carry, carry, carry,
            pltpu.VMEM((groups, rows, LANES), F32),
            pltpu.VMEM((groups, rows, LANES), F32),
            pltpu.VMEM((rows, LANES), F32),
            pltpu.VMEM((rows, LANES), F32),
            pltpu.VMEM((heads, LANES), F32),
            pltpu.VMEM((heads, LANES), F32),
            pltpu.VMEM((groups, 2, rows, states), F32),
            pltpu.VMEM((hops, groups, 2, rows // ranks, states), F32),
            pltpu.VMEM((groups, 2, rows // ranks, states), F32),
            dma, dma, dma, dma,
            pltpu.SemaphoreType.DMA((max(ranks - 1, 4), groups)),
            pltpu.SemaphoreType.DMA((max(ranks - 1, 4), groups)),
            pltpu.SemaphoreType.DMA((2, groups)),
            pltpu.SemaphoreType.DMA((2, groups)),
        ]

    results = pl.pallas_call(
        kernel,
        out_shape=(
            jax.ShapeDtypeStruct((rows, width), BF16),
            jax.ShapeDtypeStruct((rows, width), BF16),
            jax.ShapeDtypeStruct((heads, rows), F32),
            *grads,
        ),
        in_specs=in_specs,
        out_specs=out_specs,
        scratch_shapes=scratch,
        compiler_params=pltpu.CompilerParams(
            collective_id=0, has_side_effects=True, vmem_limit_bytes=56 * 1024 * 1024
        ),
    )(
        inputs, cotangent, *operands, step_raw.T, skip_gain, decay_rate, lengths
    )
    if ranks == 4 and peers == 4 and groups == 2 * PAIRS:
        results = write_out(1, *results)
    y, dx, gs, db, dc = results
    return (y, dx, gs.T, db, dc)


def solution(mesh):
    rows = P(("dp", "seq"), "head")
    proj = P(("dp", "seq"), None, None)
    grads = P(("dp", "seq", "head"), None, None)
    return jax.shard_map(
        on_device,
        mesh=mesh,
        in_specs=(rows, rows, P("head"), P("head"), proj, proj, P("dp"), rows),
        out_specs=(rows, rows, rows, grads, grads),
        check_vma=False,
    )
```
